32 devices in a mesh: dp: 4 (over x, core), seq: 2 (over y), mp: 4 (over z).
Axes of the slice: x: 2, y: 2, z: 4, core: 2. Of those that a mesh axis runs over, the one named last changes fastest.
Arguments:
- inputs: float32 [4, 1024, 1024], P('dp', 'seq'), may hold values from -6 to 6
- receptance_key_value_weight: bfloat16 [3, 1024, 1024], P(None, ('dp', 'seq'), 'mp'), may hold values from -0.1875 to 0.1875
- output_weight: bfloat16 [1024, 1024], P('mp', ('dp', 'seq')), may hold values from -0.375 to 0.375
- lowrank_first_factors: bfloat16 [2, 1024, 64], P(None, ('dp', 'seq')), may hold values from -0.1875 to 0.1875
- lowrank_second_factors: bfloat16 [2, 64, 1024], P(None, ('dp', 'seq'), 'mp'), may hold values from -0.75 to 0.75
- gate_first_factor: bfloat16 [1024, 128], P(('dp', 'seq')), may hold values from -0.1875 to 0.1875
- gate_second_factor: bfloat16 [128, 1024], P(('dp', 'seq'), 'mp'), may hold values from -0.5 to 0.5
- channel_key_weight: bfloat16 [1024, 4096], P(('dp', 'seq'), 'mp'), may hold values from -0.1875 to 0.1875
- channel_value_weight: bfloat16 [4096, 1024], P('mp', ('dp', 'seq')), may hold values from -0.09375 to 0.09375
- head_table: bfloat16 [7, 16, 64], P(None, 'mp', ('dp', 'seq')), may hold values from -8.5 to 1.5, as said below
- feature_table: bfloat16 [11, 1024], P(None, ('dp', 'seq')), may hold values from -0.5 to 1.5, as said below
- cotangent: float32 [4, 1024, 1024], P('dp', 'seq'), may hold values from -6 to 6
Outputs:
- block_out: float32 [4, 1024, 1024], P('dp', ('seq', 'mp'))
- input_grad: float32 [4, 1024, 1024], P('dp', ('seq', 'mp'))
- receptance_key_value_gradient: float32 [3, 1024, 1024], P(None, ('dp', 'seq'), 'mp')
- output_weight_gradient: float32 [1024, 1024], P('mp', ('dp', 'seq'))
- lowrank_first_gradient: float32 [2, 1024, 64], P(None, ('dp', 'seq'))
- lowrank_second_gradient: float32 [2, 64, 1024], P(None, ('dp', 'seq'), 'mp')
- gate_first_gradient: float32 [1024, 128], P(('dp', 'seq'))
- gate_second_gradient: float32 [128, 1024], P(('dp', 'seq'), 'mp')
- ffn_key_grad: float32 [1024, 4096], P(('dp', 'seq'), 'mp')
- ffn_value_grad: float32 [4096, 1024], P('mp', ('dp', 'seq'))
- head_table_gradient: float32 [7, 16, 64], P(None, 'mp', ('dp', 'seq'))
- feature_table_gradient: float32 [11, 1024], P(None, ('dp', 'seq'))
The draws below stay inside these ranges and needn't reach their ends.
Inputs may be any that keep to these rules, and one draw needn't show every extreme that they name: `head_table`: Rows: decay base, rate base, key normalization scale, key rate scale, bonus, group norm gain, group norm bias; the decay base lies in -8.5 to -1. `feature_table`: rows 0 and 2 are gains of 0.5 to 1.5, rows 1 and 3 biases of -0.5 to 0.5, rows 4 to 10 token-shift weights of 0.05 to 0.95.
All inputs are finite; a program needn't handle non-finite values.
Results may differ from the reference program's by a relative error of at most 0.02.
Values may be sent and summed in bfloat16 or wider, within the bound.
No kernel may reach another device: no remote copies, remote signals or barrier semaphores. Data moves between devices by JAX's collectives and lax.ppermute only.
A program may use at most 128 MiB of HBM per device.

```python
import jax
import jax.numpy as jnp
from jax import lax

MODEL_WIDTH = 1024
HEADS = 16
ATTENTION_SPAN = 64
FF = 4096
DECAY_RATE_RANK = 64
GATE_RANK = 128
BLOCK = 64
LENGTH = 1024
SEQS = 4


def draw_head_table(key, part):
    stochastic_seed_parts = jax.random.split(jax.random.fold_in(key, 11), 9)
    axis_arrangement = (HEADS, ATTENTION_SPAN)
    slow_share = 0.5
    slow_mask = jax.random.bernoulli(stochastic_seed_parts[0], slow_share, axis_arrangement)
    slow_base = jax.random.uniform(stochastic_seed_parts[1], axis_arrangement, jnp.float32, -8.5, -6.0)
    fast_base = jax.random.uniform(stochastic_seed_parts[2], axis_arrangement, jnp.float32, -3.0, -1.0)
    forgetting_shift_entries = jnp.where(slow_mask, slow_base, fast_base)
    learning_speed_shift = jax.random.uniform(stochastic_seed_parts[3], axis_arrangement, jnp.float32, -1.5, 1.5)
    lookup_unit_multiplier = jax.random.uniform(stochastic_seed_parts[4], axis_arrangement, jnp.float32, 0.5, 1.5)
    lookup_speed_multiplier = jax.random.uniform(stochastic_seed_parts[5], axis_arrangement, jnp.float32, 0.5, 1.5)
    extra_coefficients = jax.random.uniform(stochastic_seed_parts[6], axis_arrangement, jnp.float32, -1.0, 1.0)
    multiplier_entries = jax.random.uniform(stochastic_seed_parts[7], axis_arrangement, jnp.float32, 0.5, 1.5)
    shift_entries = jax.random.uniform(stochastic_seed_parts[8], axis_arrangement, jnp.float32, -0.5, 0.5)
    return jnp.stack([forgetting_shift_entries, learning_speed_shift, lookup_unit_multiplier, lookup_speed_multiplier, extra_coefficients, multiplier_entries, shift_entries]).astype(jnp.bfloat16)


def draw_feature_table(key, part):
    stochastic_seed_parts = jax.random.split(jax.random.fold_in(key, 23), 3)
    gains = jax.random.uniform(stochastic_seed_parts[0], (2, MODEL_WIDTH), jnp.float32, 0.5, 1.5)
    biases = jax.random.uniform(stochastic_seed_parts[1], (2, MODEL_WIDTH), jnp.float32, -0.5, 0.5)
    weights_mix = jax.random.uniform(stochastic_seed_parts[2], (7, MODEL_WIDTH), jnp.float32, 0.05, 0.95)
    rows_out = jnp.stack([gains[0], biases[0], gains[1], biases[1]])
    return jnp.concatenate([rows_out, weights_mix], axis=0).astype(jnp.bfloat16)


def block_levels(key, dims, pieces, low, high):
    loudness = 1.0
    for dim, blocks in pieces:
        draws = jax.random.uniform(jax.random.fold_in(jax.random.fold_in(key, 6), dim), (blocks,), jnp.float32, low / len(pieces), high / len(pieces))
        loudness = loudness * jnp.repeat(jnp.exp(draws), dims[dim] // blocks).reshape((-1,) + (1,) * (len(dims) - 1 - dim))
    return loudness


def scatter_about(rng, extent, scale, reach, shards=(), held_as=jnp.bfloat16):
    level = block_levels(rng, extent, shards, -0.22, 0.18) if shards else 1.0
    drawn = jax.random.normal(rng, extent, jnp.float32) * scale * level
    return jnp.minimum(jnp.maximum(drawn, -reach), reach).astype(held_as)


def setup_inputs(seed: int = 0) -> dict:
    key_of = jax.random.split(jax.random.key(seed), 13)
    return {
        "inputs": scatter_about(key_of[0], (SEQS, LENGTH, MODEL_WIDTH), 1.0, 6.0, ((0, 4), (1, 2)), jnp.float32),
        "receptance_key_value_weight": scatter_about(key_of[1], (3, MODEL_WIDTH, MODEL_WIDTH), MODEL_WIDTH ** -0.5, 0.1875, ((1, 8), (2, 4))),
        "output_weight": scatter_about(key_of[2], (MODEL_WIDTH, MODEL_WIDTH), (MODEL_WIDTH // 4) ** -0.5, 0.375, ((0, 4), (1, 8))),
        "lowrank_first_factors": scatter_about(key_of[3], (2, MODEL_WIDTH, DECAY_RATE_RANK), MODEL_WIDTH ** -0.5, 0.1875, ((1, 8),)),
        "lowrank_second_factors": scatter_about(key_of[4], (2, DECAY_RATE_RANK, MODEL_WIDTH), DECAY_RATE_RANK ** -0.5, 0.75, ((1, 8), (2, 4))),
        "gate_first_factor": scatter_about(key_of[5], (MODEL_WIDTH, GATE_RANK), MODEL_WIDTH ** -0.5, 0.1875, ((0, 8),)),
        "gate_second_factor": scatter_about(key_of[6], (GATE_RANK, MODEL_WIDTH), GATE_RANK ** -0.5, 0.5, ((0, 8), (1, 4))),
        "channel_key_weight": scatter_about(key_of[7], (MODEL_WIDTH, FF), MODEL_WIDTH ** -0.5, 0.1875, ((0, 8), (1, 4))),
        "channel_value_weight": scatter_about(key_of[8], (FF, MODEL_WIDTH), FF ** -0.5, 0.09375, ((0, 4), (1, 8))),
        "head_table": draw_head_table(jax.random.fold_in(key_of[12], 71), 0),
        "feature_table": draw_feature_table(jax.random.fold_in(key_of[12], 71), 0),
        "cotangent": scatter_about(key_of[11], (SEQS, LENGTH, MODEL_WIDTH), 1.0, 6.0, ((0, 4), (1, 2)), jnp.float32),
    }


precise = lax.Precision.HIGHEST

def matrix_product(former, latter):
    return jnp.dot(former.astype(jnp.float32), latter.astype(jnp.float32), preferred_element_type=jnp.float32)

def matrix_product_transposed_right(former, latter):
    return lax.dot_general(former.astype(jnp.float32), latter.astype(jnp.float32), (((1,), (1,)), ((), ())), preferred_element_type=jnp.float32)

def matrix_product_transposed_left(former, latter):
    return lax.dot_general(former.astype(jnp.float32), latter.astype(jnp.float32), (((0,), (0,)), ((), ())), preferred_element_type=jnp.float32)

def norm_rows(values, multiplier_entries, offset):
    center = values - lax.optimization_barrier(jnp.mean(values, axis=-1, keepdims=True))
    spread = lax.optimization_barrier(jnp.mean(center * center, axis=-1, keepdims=True))
    return center * lax.rsqrt(spread + 1e-05) * multiplier_entries + offset

def shift_later(values):
    return jnp.concatenate([jnp.zeros_like(values[:1]), values[:-1]], axis=0)

def shift_earlier(values):
    return jnp.concatenate([values[1:], jnp.zeros_like(values[:1])], axis=0)

def prepare(acceptor_lines, key_proj, payload_mapped, decay_input, rate_input, head_rows):
    overall_line_count = key_proj.shape[0]
    log_decay = -jnp.exp(-jax.nn.softplus(-(head_rows[0] + decay_input)) - 0.5)
    context_rate = jax.nn.sigmoid(head_rows[1] + rate_input)
    scaled = (key_proj * head_rows[2]).reshape(overall_line_count, -1, ATTENTION_SPAN)
    unit_key = (scaled * lax.rsqrt(lax.optimization_barrier(jnp.sum(scaled * scaled, axis=-1, keepdims=True)) + 1e-06)).reshape(overall_line_count, -1)
    corrected_lookup = key_proj * (1.0 + (context_rate - 1.0) * head_rows[3])
    removal = unit_key * context_rate
    return (acceptor_lines, log_decay, corrected_lookup, payload_mapped, unit_key, removal)

def finish(read_out, acceptor_lines, corrected_lookup, payload_mapped, valve_sigmoided, standardized_lines):
    overall_line_count = read_out.shape[0]
    grouped = read_out.reshape(overall_line_count, -1, ATTENTION_SPAN)
    center = grouped - lax.optimization_barrier(jnp.mean(grouped, axis=-1, keepdims=True))
    spread = lax.optimization_barrier(jnp.mean(center * center, axis=-1, keepdims=True))
    standardized_source = (center * lax.rsqrt(spread + 0.00064)).reshape(overall_line_count, -1) * standardized_lines[1] + standardized_lines[2]
    extra_term_sum = lax.optimization_barrier(jnp.sum((acceptor_lines * corrected_lookup * standardized_lines[0]).reshape(overall_line_count, -1, ATTENTION_SPAN), axis=-1, keepdims=True))
    extra_term_share = (extra_term_sum * payload_mapped.reshape(overall_line_count, -1, ATTENTION_SPAN)).reshape(overall_line_count, -1)
    return (standardized_source + extra_term_share) * valve_sigmoided

def to_blocks(values, heads_here):
    overall_line_count = values.shape[0]
    return values.reshape(overall_line_count // BLOCK, BLOCK, heads_here, ATTENTION_SPAN).transpose(0, 2, 1, 3)

def from_blocks(blocked):
    return blocked.transpose(0, 2, 1, 3).reshape(blocked.shape[0] * blocked.shape[2], -1)

def pair_product(former, latter):
    return jnp.einsum('htj,hsj->hts', former, latter, precision=precise)

def block_parts(acceptor_lines, log_decay, corrected_lookup, payload_mapped, unit_key, removal):
    length_here = acceptor_lines.shape[1]
    width_here = acceptor_lines.shape[2]
    inclusive = jnp.cumsum(log_decay, axis=1)
    exclusive = jnp.concatenate([jnp.zeros_like(inclusive[:, :1]), inclusive[:, :-1]], axis=1)
    growth = jnp.exp(-inclusive)
    key_scaled = corrected_lookup * growth
    removal_scaled = removal * growth
    query_unit = unit_key * jnp.exp(exclusive)
    query_read = acceptor_lines * jnp.exp(inclusive)
    positions = jnp.arange(length_here)
    strict = (positions[:, None] > positions[None, :]).astype(inclusive.dtype)
    inclusive_mask = (positions[:, None] >= positions[None, :]).astype(inclusive.dtype)
    key_mix = pair_product(query_unit, key_scaled) * strict
    removal_mix = pair_product(query_unit, removal_scaled) * strict
    read_key = pair_product(query_read, key_scaled) * inclusive_mask
    read_removal = pair_product(query_read, removal_scaled) * inclusive_mask
    system = removal_mix + jnp.eye(length_here, dtype=inclusive.dtype)
    start_map = lax.linalg.triangular_solve(system, query_unit, left_side=True, lower=True, unit_diagonal=True)
    pushed = jnp.einsum('hts,hsi->hti', key_mix, payload_mapped, precision=precise)
    local_push = lax.linalg.triangular_solve(system, pushed, left_side=True, lower=True, unit_diagonal=True)
    local_out = jnp.einsum('hts,hsi->hti', read_key, payload_mapped, precision=precise) - jnp.einsum('hts,hsi->hti', read_removal, local_push, precision=precise)
    state_read = query_read - jnp.einsum('hts,hsj->htj', read_removal, start_map, precision=precise)
    tail_decay = jnp.exp(inclusive[:, -1:, :] - inclusive)
    key_tail = corrected_lookup * tail_decay
    removal_tail = removal * tail_decay
    eye_here = jnp.eye(width_here, dtype=inclusive.dtype)
    carry_map = jnp.exp(inclusive[:, -1, :])[:, :, None] * eye_here - jnp.einsum('htj,htl->hjl', start_map, removal_tail, precision=precise)
    carry_add = jnp.einsum('hti,htj->hij', payload_mapped, key_tail, precision=precise) - jnp.einsum('hti,htj->hij', local_push, removal_tail, precision=precise)
    return (local_out, state_read, carry_map, carry_add)

def block_step(state_now, inputs_here):
    local_out, state_read, carry_map, carry_add = block_parts(*inputs_here)
    read_out = local_out + jnp.einsum('htj,hij->hti', state_read, state_now, precision=precise)
    next_state = jnp.einsum('hij,hjl->hil', state_now, carry_map, precision=precise) + carry_add
    return (read_out, next_state)

def sequence_core(*blocked):
    heads_here = blocked[0].shape[1]

    def advance(state_now, inputs_here):
        read_out, next_state = block_step(state_now, inputs_here)
        return (next_state, read_out)
    zero_state = jnp.zeros((heads_here, ATTENTION_SPAN, ATTENTION_SPAN), blocked[0].dtype)
    final_state, read_blocks = lax.scan(jax.checkpoint(advance), zero_state, blocked)
    return read_blocks

def single_sequence(residual_stream, cotangent_whole, receptance_key_value_weight, output_weight, lowrank_first_factors, lowrank_second_factors, gate_first_factor, gate_second_factor, channel_key_weight, channel_value_weight, head_table, feature_table):
    norms = feature_table.astype(jnp.float32)
    head_rows = head_table.astype(jnp.float32).reshape(head_table.shape[0], -1)
    first_norm, first_pull = jax.vjp(norm_rows, residual_stream, norms[0], norms[1])
    first_diff = shift_later(first_norm) - first_norm
    mixed_inputs = [(first_norm + first_diff * norms[4 + slot_index]).astype(jnp.bfloat16) for slot_index in range(6)]
    acceptor_lines = matrix_product(mixed_inputs[0], receptance_key_value_weight[0])
    key_proj = matrix_product(mixed_inputs[2], receptance_key_value_weight[1])
    payload_mapped = matrix_product(mixed_inputs[3], receptance_key_value_weight[2])
    decay_latent = jnp.tanh(matrix_product(mixed_inputs[1], lowrank_first_factors[0]))
    decay_lowrank = decay_latent.astype(jnp.bfloat16)
    decay_input = matrix_product(decay_lowrank, lowrank_second_factors[0])
    rate_lowrank = matrix_product(mixed_inputs[4], lowrank_first_factors[1]).astype(jnp.bfloat16)
    rate_input = matrix_product(rate_lowrank, lowrank_second_factors[1])
    gate_lat = jax.nn.sigmoid(matrix_product(mixed_inputs[5], gate_first_factor))
    gate_low = gate_lat.astype(jnp.bfloat16)
    valve_sigmoided = matrix_product(gate_low, gate_second_factor)
    prepared, prep_pull = jax.vjp(prepare, acceptor_lines, key_proj, payload_mapped, decay_input, rate_input, head_rows[:4])
    blocked = tuple((to_blocks(member, HEADS) for member in prepared))
    read_blocks, core_pull = jax.vjp(sequence_core, *blocked)
    read_out = from_blocks(read_blocks)
    gated, post_pull = jax.vjp(finish, read_out, prepared[0], prepared[2], prepared[3], valve_sigmoided, head_rows[4:])
    gated_low = gated.astype(jnp.bfloat16)
    middle = residual_stream + matrix_product(gated_low, output_weight)
    second_norm, second_pull = jax.vjp(norm_rows, middle, norms[2], norms[3])
    second_diff = shift_later(second_norm) - second_norm
    ffn_in = (second_norm + second_diff * norms[10]).astype(jnp.bfloat16)
    pre_act = matrix_product(ffn_in, channel_key_weight)
    hidden = jnp.square(jnp.maximum(pre_act, 0.0)).astype(jnp.bfloat16)
    block_out = middle + matrix_product(hidden, channel_value_weight)
    cot_low = cotangent_whole.astype(jnp.bfloat16)
    d_pre = (matrix_product_transposed_right(cot_low, channel_value_weight) * 2.0 * jnp.maximum(pre_act, 0.0)).astype(jnp.bfloat16)
    value_gradient = matrix_product_transposed_left(hidden, cot_low)
    key_gradient = matrix_product_transposed_left(ffn_in, d_pre)
    d_ffn_in = matrix_product_transposed_right(d_pre, channel_key_weight)
    d_second = d_ffn_in * (1.0 - norms[10]) + shift_earlier(d_ffn_in * norms[10])
    mu_ffn_grad = lax.optimization_barrier(jnp.sum(d_ffn_in * second_diff, axis=0))
    d_middle_ln, gain_two_grad, bias_two_grad = second_pull(d_second)
    d_middle = cotangent_whole + d_middle_ln
    d_mid_low = d_middle.astype(jnp.bfloat16)
    output_weight_gradient = matrix_product_transposed_left(gated_low, d_mid_low)
    d_gated = matrix_product_transposed_right(d_mid_low, output_weight)
    d_read, d_recept_post, d_newkey_post, d_value_post, d_gate, post_grad = post_pull(d_gated)
    core_grads = core_pull(to_blocks(d_read, HEADS))
    core_flat = [from_blocks(member) for member in core_grads]
    d_prepared = (core_flat[0] + d_recept_post, core_flat[1], core_flat[2] + d_newkey_post, core_flat[3] + d_value_post, core_flat[4], core_flat[5])
    d_recept, d_key, d_value, d_decay, d_rate, pre_grad = prep_pull(d_prepared)
    receptance_lowrank_gradient = d_recept.astype(jnp.bfloat16)
    key_lowrank_gradient = d_key.astype(jnp.bfloat16)
    value_lowrank_gradient = d_value.astype(jnp.bfloat16)
    decay_lowrank_gradient = d_decay.astype(jnp.bfloat16)
    rate_lowrank_gradient = d_rate.astype(jnp.bfloat16)
    d_gate_low = d_gate.astype(jnp.bfloat16)
    receptance_key_value_gradient = jnp.stack([matrix_product_transposed_left(mixed_inputs[0], receptance_lowrank_gradient), matrix_product_transposed_left(mixed_inputs[2], key_lowrank_gradient), matrix_product_transposed_left(mixed_inputs[3], value_lowrank_gradient)])
    lowrank_second_gradient = jnp.stack([matrix_product_transposed_left(decay_lowrank, decay_lowrank_gradient), matrix_product_transposed_left(rate_lowrank, rate_lowrank_gradient)])
    gate_second_gradient = matrix_product_transposed_left(gate_low, d_gate_low)
    decay_latent_gradient = matrix_product_transposed_right(decay_lowrank_gradient, lowrank_second_factors[0])
    rate_latent_gradient = matrix_product_transposed_right(rate_lowrank_gradient, lowrank_second_factors[1])
    d_gate_lat = matrix_product_transposed_right(d_gate_low, gate_second_factor)
    decay_preactivation = (decay_latent_gradient * (1.0 - decay_latent * decay_latent)).astype(jnp.bfloat16)
    rate_preactivation = rate_latent_gradient.astype(jnp.bfloat16)
    gate_preactivation = (d_gate_lat * gate_lat * (1.0 - gate_lat)).astype(jnp.bfloat16)
    lowrank_first_gradient = jnp.stack([matrix_product_transposed_left(mixed_inputs[1], decay_preactivation), matrix_product_transposed_left(mixed_inputs[4], rate_preactivation)])
    gate_first_gradient = matrix_product_transposed_left(mixed_inputs[5], gate_preactivation)
    mixed_inputs_gradient = [matrix_product_transposed_right(receptance_lowrank_gradient, receptance_key_value_weight[0]), matrix_product_transposed_right(decay_preactivation, lowrank_first_factors[0]), matrix_product_transposed_right(key_lowrank_gradient, receptance_key_value_weight[1]), matrix_product_transposed_right(value_lowrank_gradient, receptance_key_value_weight[2]), matrix_product_transposed_right(rate_preactivation, lowrank_first_factors[1]), matrix_product_transposed_right(gate_preactivation, gate_first_factor)]
    shifted_sum = sum((mixed_inputs_gradient[slot_index] * norms[4 + slot_index] for slot_index in range(6)))
    direct_sum = sum((mixed_inputs_gradient[slot_index] * (1.0 - norms[4 + slot_index]) for slot_index in range(6)))
    d_first = direct_sum + shift_earlier(shifted_sum)
    mu_grads = jnp.stack([lax.optimization_barrier(jnp.sum(mixed_inputs_gradient[slot_index] * first_diff, axis=0)) for slot_index in range(6)])
    d_input_ln, gain_one_grad, bias_one_grad = first_pull(d_first)
    input_grad = d_middle + d_input_ln
    feature_table_gradient = jnp.concatenate([jnp.stack([gain_one_grad, bias_one_grad, gain_two_grad, bias_two_grad]), mu_grads, mu_ffn_grad[None]], axis=0)
    head_table_gradient = jnp.concatenate([pre_grad, post_grad], axis=0).reshape(head_table.shape)
    gradient_tree = (receptance_key_value_gradient, output_weight_gradient, lowrank_first_gradient, lowrank_second_gradient, gate_first_gradient, gate_second_gradient, key_gradient, value_gradient, head_table_gradient, feature_table_gradient)
    return (block_out, input_grad, gradient_tree)

def reference(inputs, receptance_key_value_weight, output_weight, lowrank_first_factors, lowrank_second_factors, gate_first_factor, gate_second_factor, channel_key_weight, channel_value_weight, head_table, feature_table, cotangent):
    weight_tree = (receptance_key_value_weight, output_weight, lowrank_first_factors, lowrank_second_factors, gate_first_factor, gate_second_factor, channel_key_weight, channel_value_weight, head_table, feature_table)
    totals = tuple((jnp.zeros(member.shape, jnp.float32) for member in weight_tree))

    def per_sequence(carried, pair_here):
        block_out, input_grad, gradient_tree = single_sequence(pair_here[0], pair_here[1], *weight_tree)
        return (tuple((left_sum + right_sum for left_sum, right_sum in zip(carried, gradient_tree))), (block_out, input_grad))
    totals, outputs = lax.scan(per_sequence, totals, (inputs, cotangent))
    return (outputs[0], outputs[1], totals[0], totals[1], totals[2], totals[3], totals[4], totals[5], totals[6], totals[7], totals[8], totals[9])
```

```python
import functools

import jax
import jax.numpy as jnp
from jax import lax
from jax.experimental import pallas as pl
from jax.experimental.pallas import tpu as pltpu
from jax.sharding import PartitionSpec as P

SPAN = 64
f32 = jnp.float32
bf16 = jnp.bfloat16


def halves(x):
    high = x.astype(bf16)
    return high, (x - high.astype(f32)).astype(bf16)


def dot(a, b, ca, cb):
    return lax.dot_general(a, b, (((ca,), (cb,)), ((), ())), preferred_element_type=f32)


def spread(x, mask):
    tiled = jnp.concatenate([x] * (x.shape[1] // SPAN), axis=0)
    return jnp.where(mask, tiled, jnp.zeros_like(tiled))


def fold(x, mask):
    x = jnp.where(mask, x, jnp.zeros_like(x))
    return sum(x[i * SPAN : (i + 1) * SPAN] for i in range(x.shape[0] // SPAN))


def times(a, b, mask, cb):
    return dot(a.astype(bf16), spread(b.astype(bf16), mask), 1, cb)


def fine(a, b, mask, cb):
    ah, al = halves(a)
    bh, bl = halves(b)
    rows = a.shape[0]
    both = dot(jnp.concatenate([ah, al], axis=0), spread(bh, mask), 1, cb)
    return both[:rows] + both[rows:] + dot(ah, spread(bl, mask), 1, cb)


def cross(a, b):
    return dot(a.astype(bf16), b.astype(bf16), 0, 0)


def fine_cross(a, b):
    ah, al = halves(a)
    bh, bl = halves(b)
    return dot(
        jnp.concatenate([ah, al, ah], axis=0), jnp.concatenate([bh, bh, bl], axis=0), 0, 0
    )


def exact_left(ones, x):
    high = x.astype(bf16)
    rest = x - high.astype(f32)
    mid = rest.astype(bf16)
    low = (rest - mid.astype(f32)).astype(bf16)
    return dot(ones, high, 1, 0) + dot(ones, mid, 1, 0) + dot(ones, low, 1, 0)


def head_sum(x, ones):
    high, low = halves(x)
    rows = x.shape[0]
    both = dot(jnp.concatenate([high, low], axis=0), ones, 1, 0)
    return both[:rows] + both[rows:]


def constants(width):
    iota = lax.broadcasted_iota
    big_row = iota(jnp.int32, (width, width), 0)
    big_col = iota(jnp.int32, (width, width), 1)
    mask = (big_row // SPAN) == (big_col // SPAN)
    t = iota(jnp.int32, (SPAN, SPAN), 0)
    s = iota(jnp.int32, (SPAN, SPAN), 1)
    row = iota(jnp.int32, (SPAN, width), 0)
    col = iota(jnp.int32, (SPAN, width), 1) % SPAN
    one = lambda where: jnp.where(where, 1.0, 0.0).astype(f32)
    return dict(
        mask=mask,
        diagonal=one(big_row == big_col),
        ones=one(mask).astype(bf16),
        lower=one(t >= s).astype(bf16),
        upper=one(t <= s).astype(bf16),
        strict=row > col,
        incl=row >= col,
        eye=one(row == col),
        near=(row // 4 == col // 4) & (row > col),
        mid=(row // 16 == col // 16) & (row // 4 > col // 4),
        far=row // 16 > col // 16,
    )


def ready(q, kp, din, rin, rows, c):
    sig = jax.nn.sigmoid(rows[0:1] + din)
    log_decay = -0.6065306597126334 * sig
    rate = jax.nn.sigmoid(rows[1:2] + rin)
    scaled = kp * rows[2:3]
    inv = lax.rsqrt(head_sum(scaled * scaled, c["ones"]) + 1e-6)
    unit = scaled * inv
    removal = unit * rate
    total = exact_left(c["lower"], log_decay)
    up = jnp.exp(total)
    down = jnp.exp(-total)
    before = jnp.exp(total - log_decay)
    return dict(
        sig=sig,
        log_decay=log_decay,
        rate=rate,
        inv=inv,
        unit=unit,
        up=up,
        down=down,
        before=before,
        Q=q * up,
        U=unit * before,
        K=kp * (1.0 + (rate - 1.0) * rows[3:4]) * down,
        R=removal * down,
        last=up[SPAN - 1 : SPAN],
    )


def inverse(lower, c):
    mask = c["mask"]
    zero = jnp.zeros_like(lower)
    inner = jnp.where(c["near"], lower, zero)
    square = fine(inner, inner, mask, 0)
    out = c["eye"] - inner + square - fine(inner, square, mask, 0)
    for level in ("mid", "far"):
        step = fine(out, jnp.where(c[level], lower, zero), mask, 0)
        step_two = fine(step, step, mask, 0)
        first = out - fine(step, out, mask, 0)
        out = first + fine(step_two, first, mask, 0)
    return out


def pairs(e, c):
    mask = c["mask"]
    zero = jnp.zeros((SPAN, mask.shape[0]), f32)
    queries = jnp.concatenate([e["U"], e["Q"]], axis=0)
    by_key = fine(queries, e["K"], mask, 1)
    by_removal = fine(queries, e["R"], mask, 1)
    return (
        jnp.where(c["strict"], by_key[:SPAN], zero),
        jnp.where(c["incl"], by_key[SPAN:], zero),
        jnp.where(c["strict"], by_removal[:SPAN], zero),
        jnp.where(c["incl"], by_removal[SPAN:], zero),
    )


def blocks_per_step(count):
    return 2 if count % 2 == 0 else 1


def local_kernel(per, q, kp, v, din, rin, rows_ref, local_out, read, push_map, push, inv_out,
                 uk_out, qk_out, qr_out, carry, maps, adds, map_end, add_end, map_now, add_now):
    width = q.shape[1]
    c = constants(width)
    rows = rows_ref[...]

    @pl.when(pl.program_id(0) == 0)
    def _():
        map_now[...] = c["eye"]
        add_now[...] = jnp.zeros_like(add_now)

    chain = []
    for i in range(per):
        at = slice(i * SPAN, (i + 1) * SPAN)
        e = ready(q[at, :], kp[at, :], din[at, :], rin[at, :], rows, c)
        uk, qk, ur, qr = pairs(e, c)
        inv = inverse(ur, c)
        values = v[at, :]
        mixed = fine(jnp.concatenate([uk, qk], axis=0), values, c["mask"], 0)
        y = fine(inv, mixed[:SPAN], c["mask"], 0)
        w = fine(inv, e["U"], c["mask"], 0)
        local_out[at, :] = mixed[SPAN:] - fine(qr, y, c["mask"], 0)
        read[at, :] = e["Q"] - fine(qr, w, c["mask"], 0)
        push_map[at, :] = w
        push[at, :] = y
        inv_out[at, :] = inv.astype(bf16)
        uk_out[at, :] = uk.astype(bf16)
        qk_out[at, :] = qk.astype(bf16)
        qr_out[at, :] = qr.astype(bf16)
        carried = jnp.where(c["mask"], fine_cross(w, e["R"]), jnp.zeros_like(c["diagonal"]))
        carry_here = ((c["diagonal"] - carried) * e["last"]).astype(bf16)
        carry[i * width : (i + 1) * width, :] = carry_here
        added = fold(
            fine_cross(
                jnp.concatenate([values, y], axis=0), jnp.concatenate([e["K"], -e["R"]], axis=0)
            ),
            c["mask"],
        ) * e["last"]
        chain.append((at, carry_here, added))
    state_map, state_add = map_now[...], add_now[...]
    for at, carry_here, added in chain:
        both = dot(
            jnp.concatenate([state_map, state_add], axis=0).astype(bf16), carry_here, 1, 0
        )
        state_map, state_add = both[:SPAN], both[SPAN:] + added
        maps[at, :] = state_map
        adds[at, :] = state_add
    map_now[...] = state_map
    add_now[...] = state_add
    map_end[...] = state_map
    add_end[...] = state_add


def normed(out, q, k, v, rows, c):
    ones = c["ones"]
    center = out - head_sum(out, ones) * (1.0 / SPAN)
    spread_here = head_sum(center * center, ones) * (1.0 / SPAN)
    scale = lax.rsqrt(spread_here + 0.00064)
    unit = center * scale
    extra = head_sum(q * k * rows[4:5], ones)
    return unit, scale, extra, unit * rows[5:6] + rows[6:7] + extra * v


def finish_kernel(per, q, kp, v, rin, gate, rows_ref, local_out, read, push_map, push, maps, adds,
                  state_in, gated, out_ref, push_out, starts, ends, state_now):
    c = constants(q.shape[1])
    rows = rows_ref[...]
    mask = c["mask"]

    @pl.when(pl.program_id(0) == 0)
    def _():
        state_now[...] = state_in[...]

    entering = state_in[...]
    state = state_now[...]
    for i in range(per):
        at = slice(i * SPAN, (i + 1) * SPAN)
        starts[at, :] = state
        both = fine(jnp.concatenate([read[at, :], push_map[at, :]], axis=0), state, mask, 1)
        out = local_out[at, :] + both[:SPAN]
        push_out[at, :] = push[at, :] + both[SPAN:]
        out_ref[at, :] = out
        rate = jax.nn.sigmoid(rows[1:2] + rin[at, :])
        k = kp[at, :] * (1.0 + (rate - 1.0) * rows[3:4])
        _, _, _, summed = normed(out, q[at, :], k, v[at, :], rows, c)
        gated[at, :] = (summed * gate[at, :]).astype(bf16)
        state = adds[at, :] + times(entering, maps[at, :], mask, 0)
        ends[at, :] = state
    state_now[...] = state


def reads_kernel(per, q, kp, v, rin, gate, rows_ref, out_ref, d_gated, read, carry, d_out, dq_post,
                 dk_post, dv_post, d_gate, maps, adds, map_end, add_end, row_grads, map_now,
                 add_now):
    width = q.shape[1]
    c = constants(width)
    rows = rows_ref[...]
    ones = c["ones"]

    @pl.when(pl.program_id(0) == 0)
    def _():
        map_now[...] = c["eye"]
        add_now[...] = jnp.zeros_like(add_now)
        row_grads[...] = jnp.zeros_like(row_grads)

    state_map, state_add = map_now[...], add_now[...]
    column = lambda x: jnp.sum(x, axis=0, keepdims=True)
    for i in reversed(range(per)):
        at = slice(i * SPAN, (i + 1) * SPAN)
        q_here, v_here, g_here = q[at, :], v[at, :], gate[at, :]
        rate = jax.nn.sigmoid(rows[1:2] + rin[at, :])
        k = kp[at, :] * (1.0 + (rate - 1.0) * rows[3:4])
        unit, scale, extra, summed = normed(out_ref[at, :], q_here, k, v_here, rows, c)
        grad = d_gated[at, :].astype(f32)
        d_gate[at, :] = (grad * summed).astype(bf16)
        d_sum = grad * g_here
        d_unit = d_sum * rows[5:6]
        d_here = scale * (
            d_unit
            - head_sum(d_unit, ones) * (1.0 / SPAN)
            - unit * head_sum(d_unit * unit, ones) * (1.0 / SPAN)
        )
        d_extra = head_sum(d_sum * v_here, ones)
        d_out[at, :] = d_here
        dq_post[at, :] = d_extra * k * rows[4:5]
        dk_post[at, :] = d_extra * q_here * rows[4:5]
        dv_post[at, :] = d_sum * extra
        row_grads[4:5, :] += column(d_extra * q_here * k)
        row_grads[5:6, :] += column(d_sum * unit)
        row_grads[6:7, :] += column(d_sum)
        maps[at, :] = state_map
        adds[at, :] = state_add
        carry_here = carry[i * width : (i + 1) * width, :]
        both = dot(
            jnp.concatenate([state_map, state_add], axis=0).astype(bf16), carry_here, 1, 1
        )
        state_map = both[:SPAN]
        state_add = both[SPAN:] + fold(cross(d_here, read[at, :]), c["mask"])
    map_now[...] = state_map
    add_now[...] = state_add
    map_end[...] = state_map
    add_end[...] = state_add


def grads_kernel(per, q, kp, v, din, rin, lat_ref, d_gate_ref, rows_ref, up_ref, push_ref, inv_ref, uk_ref, qk_ref, qr_ref,
                 starts, ends, d_out, dq_post, dk_post, dv_post, maps, adds, grad_in, dq_ref,
                 dkp_ref, dv_ref, pre_ref, row_grads, up_grads):
    c = constants(q.shape[1])
    up = up_ref[...]
    rows = rows_ref[...]
    mask, ones = c["mask"], c["ones"]
    cat = lambda *parts: jnp.concatenate(parts, axis=0)
    column = lambda x: jnp.sum(x, axis=0, keepdims=True)

    @pl.when(pl.program_id(0) == 0)
    def _():
        row_grads[...] = jnp.zeros_like(row_grads)
        up_grads[...] = jnp.zeros_like(up_grads)

    zero = jnp.zeros((SPAN, mask.shape[0]), f32)
    rank, gate_at = low_parts(up.shape[0])
    lane = lax.broadcasted_iota(jnp.int32, (SPAN, up.shape[0]), 1)
    low_row = lax.broadcasted_iota(jnp.int32, up_grads.shape, 0)
    for i in range(per):
        at = slice(i * SPAN, (i + 1) * SPAN)
        q_here, kp_here, v_here = q[at, :], kp[at, :], v[at, :]
        e = ready(q_here, kp_here, din[at, :], rin[at, :], rows, c)
        start, end, pushed, d_read = starts[at, :], ends[at, :], push_ref[at, :], d_out[at, :]
        grad_end = adds[at, :] + times(grad_in[...], maps[at, :], mask, 0)
        grown = grad_end * e["last"]
        by_state = times(cat(e["K"], e["R"]), grown, mask, 1)
        d_push = -fold(cross(qr_ref[at, :], d_read), mask) - by_state[SPAN:]
        d_rhs = fold(cross(inv_ref[at, :], d_push), mask)
        d_value = (
            by_state[:SPAN]
            + fold(cross(cat(qk_ref[at, :], uk_ref[at, :]), cat(d_read, d_rhs)), mask)
        )
        both = cat(d_rhs, d_read)
        by_value = times(both, v_here, mask, 1)
        by_push = times(both, pushed, mask, 1)
        d_key_pairs = cat(
            jnp.where(c["strict"], by_value[:SPAN], zero), jnp.where(c["incl"], by_value[SPAN:], zero)
        )
        d_removal_pairs = cat(
            jnp.where(c["strict"], -by_push[:SPAN], zero), jnp.where(c["incl"], -by_push[SPAN:], zero)
        )
        d_queries = (
            times(both, start, mask, 0)
            + times(d_key_pairs, e["K"], mask, 0)
            + times(d_removal_pairs, e["R"], mask, 0)
        )
        by_grown = times(cat(v_here, -pushed), grown, mask, 0)
        queries = cat(e["U"], e["Q"])
        d_k_grown = by_grown[:SPAN] + fold(cross(d_key_pairs, queries), mask)
        d_r_grown = by_grown[SPAN:] + fold(cross(d_removal_pairs, queries), mask)
        d_u_grown, d_q_grown = d_queries[:SPAN], d_queries[SPAN:]
        on_unit = d_u_grown * e["U"]
        steps = d_q_grown * e["Q"] - d_k_grown * e["K"] - d_r_grown * e["R"] + on_unit
        d_log = exact_left(c["upper"], steps) - on_unit + column(grad_end * end)
        rate = e["rate"]
        d_k = d_k_grown * e["down"] + dk_post[at, :]
        d_removal = d_r_grown * e["down"]
        d_unit = d_u_grown * e["before"] + d_removal * rate
        d_rate_value = d_removal * e["unit"] + d_k * kp_here * rows[3:4]
        d_scaled = e["inv"] * (d_unit - e["unit"] * head_sum(d_unit * e["unit"], ones))
        d_rate = d_rate_value * rate * (1.0 - rate)
        d_decay = d_log * e["log_decay"] * (1.0 - e["sig"])
        dq_ref[at, :] = (d_q_grown * e["up"] + dq_post[at, :]).astype(bf16)
        dkp_ref[at, :] = (d_k * (1.0 + (rate - 1.0) * rows[3:4]) + d_scaled * rows[2:3]).astype(bf16)
        dv_ref[at, :] = (d_value + dv_post[at, :]).astype(bf16)
        lat = lat_ref[at, :]
        low = lat.astype(bf16)
        d_outs = (d_decay.astype(bf16), d_rate.astype(bf16), d_gate_ref[at, :])
        pick = lambda where, parts: jnp.where(
            where < rank, parts[0], jnp.where(where < gate_at, parts[1], parts[2])
        )
        slope = pick(lane, (1.0 - lat * lat, jnp.ones_like(lat), lat * (1.0 - lat)))
        pre = pick(lane, [dot(x, up, 1, 1) for x in d_outs]) * slope
        pre_ref[at, :] = pre.astype(bf16)
        up_grads[...] += pick(low_row, [dot(low, x, 0, 0) for x in d_outs])
        row_grads[0:1, :] += column(d_decay)
        row_grads[1:2, :] += column(d_rate)
        row_grads[2:3, :] += column(d_scaled * kp_here)
        row_grads[3:4, :] += column(d_k * kp_here * (rate - 1.0))


def run_blocks(kernel, name, ins, outs, scratch, tokens, reverse=False):
    count = tokens // SPAN
    per = blocks_per_step(count)
    steps = count // per

    def spec(shape, cut):
        if not cut:
            return pl.BlockSpec(shape, lambda i: (0, 0))
        rows = shape[0] // steps
        if reverse:
            return pl.BlockSpec((rows, shape[1]), lambda i: (steps - 1 - i, 0))
        return pl.BlockSpec((rows, shape[1]), lambda i: (i, 0))

    return pl.pallas_call(
        functools.partial(kernel, per),
        grid=(steps,),
        in_specs=[spec(x.shape, cut) for x, cut in ins],
        out_specs=[spec(shape, cut) for shape, _, cut in outs],
        out_shape=[jax.ShapeDtypeStruct(shape, kind) for shape, kind, _ in outs],
        scratch_shapes=[pltpu.VMEM(shape, f32) for shape in scratch],
        compiler_params=pltpu.CompilerParams(dimension_semantics=("arbitrary",)),
        cost_estimate=pl.CostEstimate(flops=10**10, bytes_accessed=2 * 10**7, transcendentals=0),
        name=name,
    )(*[x for x, _ in ins])


def low_parts(width):
    return width // 4, width // 2


def mixed(unit, edge, norms, count):
    first = unit * norms[0:1] + norms[1:2]
    before = (edge[0:1] * norms[0:1] + norms[1:2]) * edge[1:2]
    row = lax.broadcasted_iota(jnp.int32, first.shape, 0)
    diff = jnp.where(row == 0, before, pltpu.roll(first, 1, 0)) - first
    return diff, [(first + diff * norms[4 + i : 5 + i]).astype(bf16) for i in range(count)]


def slab_weights(gathered, width):
    parts, rows, _ = gathered.shape
    part = rows // 4
    piece = lambda i, w: jnp.concatenate(
        [gathered[j, i * part : (i + 1) * part, :w] for j in range(parts)], axis=0
    )
    return [piece(i, width) for i in range(3)] + [piece(3, gathered.shape[2])]


def project_kernel(unit, edge, norms, gathered, up, q, kp, v, din, rin, gate, lat, low_total):
    width = q.shape[1]
    step = pl.program_id(0)
    norms_here = norms[...]
    _, mixes = mixed(unit[...], edge[...], norms_here, 6)
    w_q, w_k, w_v, w_low = slab_weights(gathered, width)
    low_width = w_low.shape[1]
    rank, gate_at = low_parts(low_width)
    lane = lax.broadcasted_iota(jnp.int32, low_total.shape, 1)
    low = jnp.where(
        lane < rank,
        dot(mixes[1], w_low, 1, 0),
        jnp.where(lane < gate_at, dot(mixes[4], w_low, 1, 0), dot(mixes[5], w_low, 1, 0)),
    )

    @pl.when(step == 0)
    def _():
        q[...] = dot(mixes[0], w_q, 1, 0)
        kp[...] = dot(mixes[2], w_k, 1, 0)
        v[...] = dot(mixes[3], w_v, 1, 0)
        low_total[...] = low

    @pl.when(step > 0)
    def _():
        q[...] += dot(mixes[0], w_q, 1, 0)
        kp[...] += dot(mixes[2], w_k, 1, 0)
        v[...] += dot(mixes[3], w_v, 1, 0)
        low_total[...] += low

    @pl.when(step == pl.num_programs(0) - 1)
    def _():
        total = low_total[...]
        lats = jnp.where(
            lane < rank, jnp.tanh(total), jnp.where(lane < gate_at, total, jax.nn.sigmoid(total))
        )
        lat[...] = lats
        zero = jnp.zeros_like(lats)
        chosen = lambda where: jnp.where(where, lats, zero).astype(bf16)
        din[...] = dot(chosen(lane < rank), up[...], 1, 0)
        rin[...] = dot(chosen((lane >= rank) & (lane < gate_at)), up[...], 1, 0)
        gate[...] = dot(chosen(lane >= gate_at), up[...], 1, 0)


def unproject_kernel(unit, edge, scales, norms, gathered, dq, dkp, dv, pre, packed, feature, edge_fix,
                     d_in, all_first, all_unit, all_gain):
    width = dq.shape[1]
    step = pl.program_id(0)
    n = norms[...]
    edge_here = edge[...]
    unit_here = unit[...]
    diff, mixes = mixed(unit_here, edge_here, n, 6)
    weights = slab_weights(gathered, width)
    w_low = weights[3]
    slab, low_width = w_low.shape
    rank, gate_at = low_parts(low_width)
    pre_here = pre[...]
    lane = lax.broadcasted_iota(jnp.int32, pre_here.shape, 1)
    none = jnp.zeros_like(pre_here)
    pres = [
        jnp.where(lane < rank, pre_here, none),
        jnp.where((lane >= rank) & (lane < gate_at), pre_here, none),
        jnp.where(lane >= gate_at, pre_here, none),
    ]
    sources = [(0, dq[...], 0), (2, dkp[...], 1), (3, dv[...], 2), (1, pres[0], 3), (4, pres[1], 3),
               (5, pres[2], 3)]
    low_lane = lax.broadcasted_iota(jnp.int32, (slab, low_width), 1)
    column = lambda x: jnp.sum(x, axis=0, keepdims=True)
    parts = gathered.shape[0]
    part = slab // parts
    direct = shifted = None
    low_grad = None
    for mix, grad, which in sources:
        weight_grad = dot(mixes[mix], grad, 0, 0)
        if which < 3:
            for j in range(parts):
                packed[j, which * part : (which + 1) * part, :width] = weight_grad[
                    j * part : (j + 1) * part
                ].astype(bf16)
                if width < low_width:
                    packed[j, which * part : (which + 1) * part, width:] = jnp.zeros(
                        (part, low_width - width), bf16
                    )
        else:
            low_grad = weight_grad if low_grad is None else low_grad + weight_grad
        d_mix = dot(grad, weights[which], 1, 1)
        feature[4 + mix : 5 + mix, :] = column(d_mix * diff)
        to_shift = d_mix * n[4 + mix : 5 + mix]
        shifted = to_shift if shifted is None else shifted + to_shift
        direct = d_mix - to_shift if direct is None else direct + (d_mix - to_shift)
    for j in range(parts):
        packed[j, 3 * part : 4 * part, :] = low_grad[j * part : (j + 1) * part].astype(bf16)
    tokens = unit_here.shape[0]
    row = lax.broadcasted_iota(jnp.int32, shifted.shape, 0)
    d_first = direct + jnp.where(row == tokens - 1, 0.0, pltpu.roll(shifted, tokens - 1, 0))
    before = shifted[0:1] * edge_here[1:2]
    feature[0:1, :] = column(d_first * unit_here) + before * edge_here[0:1]
    feature[1:2, :] = column(d_first) + before
    feature[2:4, :] = jnp.zeros_like(feature[2:4, :])
    feature[10:, :] = jnp.zeros_like(feature[10:, :])
    at = pl.ds(pl.multiple_of(step * slab, slab), slab)
    all_first[:tokens, at] = d_first * n[0:1]
    all_first[tokens:, at] = jnp.broadcast_to(before * n[0:1], (8, slab))
    all_unit[:tokens, at] = unit_here
    all_unit[tokens:, at] = jnp.broadcast_to(edge_here[0:1], (8, slab))

    @pl.when(step == pl.num_programs(0) - 1)
    def _():
        d_unit = all_first[...]
        units = all_unit[...]
        features = d_unit.shape[1]
        mean = jnp.sum(d_unit, axis=1, keepdims=True) * (1.0 / features)
        along = jnp.sum(d_unit * units, axis=1, keepdims=True) * (1.0 / features)
        result = scales[...] * (d_unit - mean - units * along)
        d_in[...] = result[:tokens]
        edge_fix[...] = result[tokens:]


def run_slabs(kernel, name, ins, outs, scratch, slabs):
    def spec(shape, cut):
        shape = tuple(shape)
        if cut is None:
            return pl.BlockSpec(shape, lambda i: (0,) * len(shape))
        dim, size = cut
        block = list(shape)
        block[dim] = shape[dim] // slabs
        if size is not None:
            block[size[0]] = size[1]
        return pl.BlockSpec(tuple(block), lambda i: tuple(i if k == dim else 0 for k in range(len(shape))))

    return pl.pallas_call(
        kernel,
        grid=(slabs,),
        in_specs=[spec(x.shape, cut) for x, cut in ins],
        out_specs=[spec(shape, cut) for shape, _, cut in outs],
        out_shape=[jax.ShapeDtypeStruct(shape, kind) for shape, kind, _ in outs],
        scratch_shapes=[pltpu.VMEM(shape, f32) for shape in scratch],
        compiler_params=pltpu.CompilerParams(dimension_semantics=("arbitrary",)),
        cost_estimate=pl.CostEstimate(flops=10**10, bytes_accessed=2 * 10**7, transcendentals=0),
        name=name,
    )(*[x for x, _ in ins])


def to_next(x, axis, by):
    devices = lax.axis_size(axis)
    pairs_here = [(i, i + by) for i in range(devices) if 0 <= i + by < devices]
    return lax.ppermute(x, axis, pairs_here)


def around(x, by):
    devices = lax.axis_size("mp")
    return lax.ppermute(x, "mp", [(i, (i + by) % devices) for i in range(devices)])


def gather_shares(x):
    devices = lax.axis_size("mp")
    came = [x] + [around(x, by) for by in range(1, devices)]
    turned = jnp.stack([came[-k % devices] for k in range(devices)] * 2)
    at = (devices - lax.axis_index("mp")) % devices
    return lax.dynamic_slice_in_dim(turned, at, devices, 0)


def scatter_shares(x):
    devices = lax.axis_size("mp")
    here = lax.axis_index("mp")
    term = lambda at: lax.dynamic_index_in_dim(x, at % devices, 0, keepdims=False)
    total = term(here).astype(f32)
    for by in range(1, devices):
        total = total + around(term(here + by), by).astype(f32)
    return total


def mm(a, b):
    return jnp.dot(a, b, preferred_element_type=f32)


def mm_right(a, b):
    return dot(a, b, 1, 1)


def mm_left(a, b):
    return dot(a, b, 0, 0)


def statistics(values):
    center = values - jnp.mean(values, axis=-1, keepdims=True)
    scale = lax.rsqrt(jnp.mean(center * center, axis=-1, keepdims=True) + 1e-05)
    return center * scale, scale


def norm_back(grad, unit, scale, gain):
    d_unit = grad * gain
    mean = jnp.mean(d_unit, axis=-1, keepdims=True)
    along = jnp.mean(d_unit * unit, axis=-1, keepdims=True)
    return scale * (d_unit - mean - unit * along), jnp.sum(grad * unit, axis=0), jnp.sum(grad, axis=0)


def earlier(values, edge):
    return jnp.concatenate([values[1:], edge], axis=0)


def later(values, edge):
    return jnp.concatenate([edge, values[:-1]], axis=0)


def carry_states(state_map, state_add, by):
    entering = to_next(state_add.astype(bf16), "seq", by).astype(f32)
    heads = state_map.shape[1] // SPAN
    apart = lambda x: x.reshape(SPAN, heads, SPAN).transpose(1, 0, 2)
    for _ in range(lax.axis_size("seq") - 2):
        moved = jnp.einsum("hij,hjl->hil", apart(entering), apart(state_map), precision="highest")
        passed = moved.transpose(1, 0, 2).reshape(state_add.shape) + state_add
        entering = to_next(passed.astype(bf16), "seq", by).astype(f32)
    return entering


def wide(x, width):
    return jnp.pad(x, ((0, 0), (0, width - x.shape[1])))


def body(inputs, rkv_weight, output_weight, first_factors, second_factors, gate_first, gate_second,
         key_weight, value_weight, head_table, feature_table, cotangent):
    group = ("dp", "seq")
    count = lax.axis_size("dp") * lax.axis_size("seq")
    mp = lax.axis_size("mp")
    mp_here = lax.axis_index("mp")
    stream = inputs[0]
    cot = cotangent[0]
    tokens, features = stream.shape
    share = tokens // mp
    share_at = mp_here * share
    part = features // count
    width = rkv_weight.shape[2]
    heads = width // SPAN
    rank, gate_rank = first_factors.shape[2], gate_first.shape[1]
    low_width = 2 * rank + gate_rank
    lanes = max(width, low_width, part)
    up_rows, gate_rows = second_factors.shape[1], gate_second.shape[0]
    head_part = head_table.shape[2]
    edge_row = to_next(stream[-1:], "seq", 1)
    pieces = [
        wide(rkv_weight.reshape(3 * part, width), lanes),
        wide(jnp.concatenate([first_factors[0], first_factors[1], gate_first], axis=1), lanes),
        wide(second_factors.reshape(2 * up_rows, width), lanes),
        wide(gate_second, lanes),
        wide(feature_table, lanes),
        wide(head_table.reshape(7, heads * head_part), lanes),
    ]
    edges = [0]
    for piece in pieces:
        edges.append(edges[-1] + piece.shape[0])
    packed = jnp.concatenate(pieces, axis=0)
    rows_full = -(-packed.shape[0] // 16) * 16
    packed = jnp.pad(packed, ((0, rows_full - packed.shape[0]), (0, 0)))
    gathered = lax.all_gather(packed, group, axis=0, tiled=False)
    cut = lambda i, w: gathered[:, edges[i] : edges[i + 1], :w]
    up = cut(2, width).reshape(count, 2, up_rows, width).transpose(1, 0, 2, 3)
    up = jnp.concatenate(
        [up.reshape(2 * rank, width), cut(3, width).reshape(gate_rank, width)], axis=0
    )
    norms = cut(4, part).transpose(1, 0, 2).reshape(11, features).astype(f32)
    norms = jnp.pad(norms, ((0, 5), (0, 0)))
    head_rows = (
        cut(5, heads * head_part)
        .reshape(count, 7, heads, head_part)
        .transpose(1, 2, 0, 3)
        .reshape(7, width)
        .astype(f32)
    )
    head_rows = jnp.pad(head_rows, ((0, 1), (0, 0)))

    out_column = gather_shares(output_weight).reshape(features, part)
    rest = lax.all_gather(
        jnp.concatenate([value_weight, out_column], axis=0), group, axis=0, tiled=False
    )
    hidden_here = value_weight.shape[0]
    key_full = lax.all_gather(key_weight, group, axis=0, tiled=True)

    unit_one, scale_one = statistics(stream)
    edge_unit, edge_scale = statistics(edge_row)
    has_edge = (lax.axis_index("seq") > 0).astype(f32)
    edge = jnp.concatenate(
        [edge_unit, jnp.broadcast_to(has_edge, (1, features)), jnp.zeros((6, features), f32)]
    )
    slab = max(256, part)
    slabs = features // slab
    in_slabs = (1, None)
    of_gathered = (0, (1, 4 * part))
    whole = (tokens, width)
    q, kp, v, din, rin, gate, lat = run_slabs(
        project_kernel,
        "project",
        [(unit_one, in_slabs), (edge, in_slabs), (norms, in_slabs), (gathered, of_gathered), (up, None)],
        [(whole, f32, None)] * 6 + [((tokens, low_width), f32, None)],
        [(tokens, low_width)],
        slabs,
    )

    state = (SPAN, width)
    (local_out, read, push_map, push, inv, uk, qk, qr, carry, maps, adds, map_end, add_end) = run_blocks(
        local_kernel,
        "local",
        [(q, True), (kp, True), (v, True), (din, True), (rin, True), (head_rows, False)],
        [(whole, f32, True)] * 4
        + [(whole, bf16, True)] * 4
        + [((tokens // SPAN * width, width), bf16, True)]
        + [(whole, f32, True)] * 2
        + [(state, f32, False)] * 2,
        [state, state],
        tokens,
    )
    entering = carry_states(map_end, add_end, 1)
    gated, read_out, pushed, starts, ends = run_blocks(
        finish_kernel,
        "finish",
        [(x, True) for x in (q, kp, v, rin, gate)]
        + [(head_rows, False)]
        + [(x, True) for x in (local_out, read, push_map, push, maps, adds)]
        + [(entering, False)],
        [(whole, bf16, True)] + [(whole, f32, True)] * 4,
        [state],
        tokens,
    )

    gated, rest, key_full = lax.optimization_barrier((gated, rest, key_full))
    value_full = rest[:, :hidden_here].transpose(1, 0, 2).reshape(hidden_here, features)
    out_full = rest[:, hidden_here:].transpose(1, 0, 2).reshape(features, features)
    gated_all = lax.all_gather(gated, "mp", axis=0, tiled=False)
    gated_full = gated_all.transpose(1, 0, 2).reshape(tokens, features)
    middle = stream + mm(gated_full, out_full)
    unit_two, scale_two = statistics(middle)
    second_norm = unit_two * norms[2] + norms[3]
    second_diff = later(second_norm, to_next(second_norm[-1:], "seq", 1)) - second_norm
    ffn_in = (second_norm + second_diff * norms[10]).astype(bf16)
    pre_act = mm(ffn_in, key_full)
    rectified = jnp.maximum(pre_act, 0.0)
    hidden = jnp.square(rectified).astype(bf16)
    cot_low = cot.astype(bf16)
    d_pre = (mm_right(cot_low, value_full) * 2.0 * rectified).astype(bf16)
    d_ffn = mm_right(d_pre, key_full)
    d_second = d_ffn * (1.0 - norms[10]) + earlier(
        d_ffn * norms[10], to_next(d_ffn[:1] * norms[10], "seq", -1)
    )
    mu_ffn = jnp.sum(d_ffn * second_diff, axis=0)
    d_mid, gain_two, bias_two = norm_back(d_second, unit_two, scale_two, norms[2])
    d_mid_low = (d_mid + cot * (1.0 / mp)).astype(bf16)
    d_gated_parts = mm_right(d_mid_low, out_full).astype(bf16)
    d_gated_parts = d_gated_parts.reshape(tokens, mp, width).transpose(1, 0, 2)
    d_gated = lax.psum_scatter(d_gated_parts, "mp", scatter_dimension=0, tiled=False)

    ffn_out = mm(hidden, value_full).astype(bf16)
    block_out = lax.dynamic_slice_in_dim(middle, share_at, share, 0) + scatter_shares(
        ffn_out.reshape(mp, share, features)
    )
    by_part = lambda x: x.astype(bf16).reshape(x.shape[0], count, part).transpose(1, 0, 2)
    key_grad = mm_left(ffn_in, d_pre).astype(bf16)
    lots = key_grad.shape[1] // part
    key_grad = key_grad.reshape(count, part, lots, part).transpose(0, 2, 1, 3)
    large = jnp.concatenate(
        [
            by_part(mm_left(hidden, cot_low)),
            key_grad.reshape(count, lots * part, part),
            by_part(mm_left(gated_full, d_mid_low)),
        ],
        axis=1,
    )
    d_gated, large = lax.optimization_barrier((d_gated, large))
    large = lax.psum_scatter(large, group, scatter_dimension=0, tiled=False)
    value_grad = large[:hidden_here].astype(f32)
    key_grad = large[hidden_here : hidden_here + lots * part].reshape(lots, part, part)
    key_grad = key_grad.transpose(1, 0, 2).reshape(part, lots * part).astype(f32)
    out_grad = scatter_shares(large[hidden_here + lots * part :].reshape(mp, width, part))

    (d_read, dq_post, dk_post, dv_post, d_gate, back_maps, back_adds, back_map_end, back_add_end,
     row_grads_post) = run_blocks(
        reads_kernel,
        "reads",
        [(x, True) for x in (q, kp, v, rin, gate)]
        + [(head_rows, False)]
        + [(x, True) for x in (read_out, d_gated, read, carry)],
        [(whole, f32, True)] * 4
        + [(whole, bf16, True)]
        + [(whole, f32, True)] * 2
        + [(state, f32, False)] * 2
        + [((8, width), f32, False)],
        [state, state],
        tokens,
        reverse=True,
    )
    grad_in = carry_states(back_map_end, back_add_end, -1)
    dq, dkp, dv, pre, row_grads, up_grads = run_blocks(
        grads_kernel,
        "grads",
        [(x, True) for x in (q, kp, v, din, rin, lat, d_gate)]
        + [(head_rows, False), (up, False)]
        + [
            (x, True)
            for x in (pushed, inv, uk, qk, qr, starts, ends, d_read, dq_post, dk_post, dv_post,
                      back_maps, back_adds)
        ]
        + [(grad_in, False)],
        [(whole, bf16, True)] * 3
        + [((tokens, low_width), bf16, True), ((8, width), f32, False)]
        + [((low_width, width), f32, False)],
        [],
        tokens,
    )
    row_grads = jnp.concatenate([row_grads[:4], row_grads_post[4:7]], axis=0)

    scales = jnp.concatenate([scale_one, jnp.broadcast_to(edge_scale, (8, 1))], axis=0)
    packed, feature_grad, edge_fix, d_in = run_slabs(
        unproject_kernel,
        "unproject",
        [(unit_one, in_slabs), (edge, in_slabs), (scales, None), (norms, in_slabs)]
        + [(gathered, of_gathered), (dq, None), (dkp, None), (dv, None), (pre, None)],
        [
            ((count, 4 * part, lanes), bf16, (0, None)),
            ((16, features), f32, in_slabs),
            ((8, features), f32, None),
            ((tokens, features), f32, None),
        ],
        [(tokens + 8, features)] * 2 + [(8, 128)],
        slabs,
    )
    fix = to_next(edge_fix[:1], "seq", -1)
    last = lax.broadcasted_iota(jnp.int32, (tokens, 1), 0) == tokens - 1
    d_stream = d_in + d_mid + jnp.where(last, fix, 0.0)
    input_grad = lax.dynamic_slice_in_dim(cot, share_at, share, 0) + scatter_shares(
        d_stream.astype(bf16).reshape(mp, share, features)
    )

    feature_grad = jnp.concatenate(
        [feature_grad[:2], gain_two[None], bias_two[None], feature_grad[4:10], mu_ffn[None]]
    )
    split_rows = lambda x: x.reshape(count, x.shape[0] // count, x.shape[1])
    wider = lambda x: jnp.pad(x.astype(bf16), ((0, 0), (0, 0), (0, lanes - x.shape[2])))
    grads = [
        split_rows(up_grads[:rank]),
        split_rows(up_grads[rank : 2 * rank]),
        split_rows(up_grads[2 * rank :]),
        feature_grad.reshape(11, count, part).transpose(1, 0, 2),
        row_grads.reshape(7, heads, count, head_part)
        .transpose(2, 0, 1, 3)
        .reshape(count, 7, heads * head_part),
    ]
    grads = jnp.concatenate([wider(x) for x in grads], axis=1)
    grads = jnp.pad(grads, ((0, 0), (0, rows_full - 4 * part - grads.shape[1]), (0, 0)))
    grads = jnp.concatenate([packed, grads], axis=1)
    summed = lax.psum_scatter(grads, group, scatter_dimension=0, tiled=False)
    own = lambda i, w: summed[edges[i] : edges[i + 1], :w].astype(f32)
    everywhere = jnp.concatenate(
        [summed[edges[1] : edges[2]], summed[edges[4] : edges[5]]], axis=0
    )
    everywhere = jnp.sum(gather_shares(everywhere).astype(f32), axis=0)
    down_sum = everywhere[:part]
    return (
        block_out[None],
        input_grad[None],
        own(0, width).reshape(3, part, width),
        out_grad,
        jnp.stack([down_sum[:, :rank], down_sum[:, rank : 2 * rank]]),
        own(2, width).reshape(2, up_rows, width),
        down_sum[:, 2 * rank : low_width],
        own(3, width),
        key_grad,
        value_grad,
        own(5, heads * head_part).reshape(7, heads, head_part),
        everywhere[part:, :part],
    )


def solution(mesh):
    both = ("dp", "seq")
    return jax.shard_map(
        body,
        mesh=mesh,
        in_specs=(
            P("dp", "seq", None),
            P(None, both, "mp"),
            P("mp", both),
            P(None, both, None),
            P(None, both, "mp"),
            P(both, None),
            P(both, "mp"),
            P(both, "mp"),
            P("mp", both),
            P(None, "mp", both),
            P(None, both),
            P("dp", "seq", None),
        ),
        out_specs=(
            P("dp", ("seq", "mp"), None),
            P("dp", ("seq", "mp"), None),
            P(None, both, "mp"),
            P("mp", both),
            P(None, both, None),
            P(None, both, "mp"),
            P(both, None),
            P(both, "mp"),
            P(both, "mp"),
            P("mp", both),
            P(None, "mp", both),
            P(None, both),
        ),
        check_vma=False,
    )
```

```python
import functools

import jax
import jax.numpy as jnp
from jax import lax
from jax.experimental import pallas as pl
from jax.experimental.pallas import tpu as pltpu
from jax.sharding import PartitionSpec as P

SPAN = 64
f32 = jnp.float32
bf16 = jnp.bfloat16


def halves(x):
    high = x.astype(bf16)
    return high, (x - high.astype(f32)).astype(bf16)


def dot(a, b, ca, cb):
    return lax.dot_general(a, b, (((ca,), (cb,)), ((), ())), preferred_element_type=f32)


def spread(x, mask):
    tiled = jnp.concatenate([x] * (x.shape[1] // SPAN), axis=0)
    return jnp.where(mask, tiled, jnp.zeros_like(tiled))


def fold(x, mask):
    x = jnp.where(mask, x, jnp.zeros_like(x))
    return sum(x[i * SPAN : (i + 1) * SPAN] for i in range(x.shape[0] // SPAN))


def times(a, b, mask, cb):
    return dot(a.astype(bf16), spread(b.astype(bf16), mask), 1, cb)


def fine(a, b, mask, cb):
    ah, al = halves(a)
    bh, bl = halves(b)
    rows = a.shape[0]
    both = dot(jnp.concatenate([ah, al], axis=0), spread(bh, mask), 1, cb)
    return both[:rows] + both[rows:] + dot(ah, spread(bl, mask), 1, cb)


def cross(a, b):
    return dot(a.astype(bf16), b.astype(bf16), 0, 0)


def fine_cross(a, b):
    ah, al = halves(a)
    bh, bl = halves(b)
    return dot(
        jnp.concatenate([ah, al, ah], axis=0), jnp.concatenate([bh, bh, bl], axis=0), 0, 0
    )


def exact_left(ones, x):
    high = x.astype(bf16)
    rest = x - high.astype(f32)
    mid = rest.astype(bf16)
    low = (rest - mid.astype(f32)).astype(bf16)
    return dot(ones, high, 1, 0) + dot(ones, mid, 1, 0) + dot(ones, low, 1, 0)


def head_sum(x, ones):
    high, low = halves(x)
    rows = x.shape[0]
    both = dot(jnp.concatenate([high, low], axis=0), ones, 1, 0)
    return both[:rows] + both[rows:]


def constants(width):
    iota = lax.broadcasted_iota
    big_row = iota(jnp.int32, (width, width), 0)
    big_col = iota(jnp.int32, (width, width), 1)
    mask = (big_row // SPAN) == (big_col // SPAN)
    t = iota(jnp.int32, (SPAN, SPAN), 0)
    s = iota(jnp.int32, (SPAN, SPAN), 1)
    row = iota(jnp.int32, (SPAN, width), 0)
    col = iota(jnp.int32, (SPAN, width), 1) % SPAN
    one = lambda where: jnp.where(where, 1.0, 0.0).astype(f32)
    return dict(
        mask=mask,
        diagonal=one(big_row == big_col),
        ones=one(mask).astype(bf16),
        lower=one(t >= s).astype(bf16),
        upper=one(t <= s).astype(bf16),
        strict=row > col,
        incl=row >= col,
        eye=one(row == col),
        near=(row // 4 == col // 4) & (row > col),
        mid=(row // 16 == col // 16) & (row // 4 > col // 4),
        far=row // 16 > col // 16,
    )


def ready(q, kp, din, rin, rows, c):
    sig = jax.nn.sigmoid(rows[0:1] + din)
    log_decay = -0.6065306597126334 * sig
    rate = jax.nn.sigmoid(rows[1:2] + rin)
    scaled = kp * rows[2:3]
    inv = lax.rsqrt(head_sum(scaled * scaled, c["ones"]) + 1e-6)
    unit = scaled * inv
    removal = unit * rate
    total = exact_left(c["lower"], log_decay)
    up = jnp.exp(total)
    down = jnp.exp(-total)
    before = jnp.exp(total - log_decay)
    return dict(
        sig=sig,
        log_decay=log_decay,
        rate=rate,
        inv=inv,
        unit=unit,
        up=up,
        down=down,
        before=before,
        Q=q * up,
        U=unit * before,
        K=kp * (1.0 + (rate - 1.0) * rows[3:4]) * down,
        R=removal * down,
        last=up[SPAN - 1 : SPAN],
    )


def inverse(lower, c):
    mask = c["mask"]
    zero = jnp.zeros_like(lower)
    inner = jnp.where(c["near"], lower, zero)
    square = fine(inner, inner, mask, 0)
    out = c["eye"] - inner + square - fine(inner, square, mask, 0)
    for level in ("mid", "far"):
        step = fine(out, jnp.where(c[level], lower, zero), mask, 0)
        step_two = fine(step, step, mask, 0)
        first = out - fine(step, out, mask, 0)
        out = first + fine(step_two, first, mask, 0)
    return out


def pairs(e, c):
    mask = c["mask"]
    zero = jnp.zeros((SPAN, mask.shape[0]), f32)
    queries = jnp.concatenate([e["U"], e["Q"]], axis=0)
    by_key = fine(queries, e["K"], mask, 1)
    by_removal = fine(queries, e["R"], mask, 1)
    return (
        jnp.where(c["strict"], by_key[:SPAN], zero),
        jnp.where(c["incl"], by_key[SPAN:], zero),
        jnp.where(c["strict"], by_removal[:SPAN], zero),
        jnp.where(c["incl"], by_removal[SPAN:], zero),
    )


def blocks_per_step(count):
    return 2 if count % 2 == 0 else 1


def local_kernel(per, q, kp, v, din, rin, rows_ref, local_out, read, push_map, push, inv_out,
                 uk_out, qk_out, qr_out, carry, maps, adds, map_end, add_end, map_now, add_now):
    width = q.shape[1]
    c = constants(width)
    rows = rows_ref[...]

    @pl.when(pl.program_id(0) == 0)
    def _():
        map_now[...] = c["eye"]
        add_now[...] = jnp.zeros_like(add_now)

    chain = []
    for i in range(per):
        at = slice(i * SPAN, (i + 1) * SPAN)
        e = ready(q[at, :], kp[at, :], din[at, :], rin[at, :], rows, c)
        uk, qk, ur, qr = pairs(e, c)
        inv = inverse(ur, c)
        values = v[at, :]
        mixed = fine(jnp.concatenate([uk, qk], axis=0), values, c["mask"], 0)
        y = fine(inv, mixed[:SPAN], c["mask"], 0)
        w = fine(inv, e["U"], c["mask"], 0)
        local_out[at, :] = mixed[SPAN:] - fine(qr, y, c["mask"], 0)
        read[at, :] = e["Q"] - fine(qr, w, c["mask"], 0)
        push_map[at, :] = w
        push[at, :] = y
        inv_out[at, :] = inv.astype(bf16)
        uk_out[at, :] = uk.astype(bf16)
        qk_out[at, :] = qk.astype(bf16)
        qr_out[at, :] = qr.astype(bf16)
        carried = jnp.where(c["mask"], fine_cross(w, e["R"]), jnp.zeros_like(c["diagonal"]))
        carry_here = ((c["diagonal"] - carried) * e["last"]).astype(bf16)
        carry[i * width : (i + 1) * width, :] = carry_here
        added = fold(
            fine_cross(
                jnp.concatenate([values, y], axis=0), jnp.concatenate([e["K"], -e["R"]], axis=0)
            ),
            c["mask"],
        ) * e["last"]
        chain.append((at, carry_here, added))
    state_map, state_add = map_now[...], add_now[...]
    for at, carry_here, added in chain:
        both = dot(
            jnp.concatenate([state_map, state_add], axis=0).astype(bf16), carry_here, 1, 0
        )
        state_map, state_add = both[:SPAN], both[SPAN:] + added
        maps[at, :] = state_map
        adds[at, :] = state_add
    map_now[...] = state_map
    add_now[...] = state_add
    map_end[...] = state_map
    add_end[...] = state_add


def normed(out, q, k, v, rows, c):
    ones = c["ones"]
    center = out - head_sum(out, ones) * (1.0 / SPAN)
    spread_here = head_sum(center * center, ones) * (1.0 / SPAN)
    scale = lax.rsqrt(spread_here + 0.00064)
    unit = center * scale
    extra = head_sum(q * k * rows[4:5], ones)
    return unit, scale, extra, unit * rows[5:6] + rows[6:7] + extra * v


def finish_kernel(per, q, kp, v, rin, gate, rows_ref, local_out, read, push_map, push, maps, adds,
                  state_in, gated, out_ref, push_out, starts, ends, state_now):
    c = constants(q.shape[1])
    rows = rows_ref[...]
    mask = c["mask"]

    @pl.when(pl.program_id(0) == 0)
    def _():
        state_now[...] = state_in[...]

    entering = state_in[...]
    state = state_now[...]
    for i in range(per):
        at = slice(i * SPAN, (i + 1) * SPAN)
        starts[at, :] = state
        both = fine(jnp.concatenate([read[at, :], push_map[at, :]], axis=0), state, mask, 1)
        out = local_out[at, :] + both[:SPAN]
        push_out[at, :] = push[at, :] + both[SPAN:]
        out_ref[at, :] = out
        rate = jax.nn.sigmoid(rows[1:2] + rin[at, :])
        k = kp[at, :] * (1.0 + (rate - 1.0) * rows[3:4])
        _, _, _, summed = normed(out, q[at, :], k, v[at, :], rows, c)
        gated[at, :] = (summed * gate[at, :]).astype(bf16)
        state = adds[at, :] + times(entering, maps[at, :], mask, 0)
        ends[at, :] = state
    state_now[...] = state


def reads_kernel(devices, per, q, kp, v, rin, gate, rows_ref, out_ref, read, carry, *refs):
    d_gated, fixes, refs = refs[:devices], refs[devices : 2 * devices], refs[2 * devices :]
    d_out, dq_post, dk_post, dv_post, d_gate, maps, adds, map_end, add_end, row_grads = refs[:10]
    map_now, add_now = refs[10:]
    width = q.shape[1]
    first_step = (pl.program_id(0) == 0).astype(f32)
    fix = sum(x[...].astype(f32) for x in fixes)[EDGE - 1 : EDGE] * first_step
    last_row = lax.broadcasted_iota(jnp.int32, (SPAN, width), 0) == SPAN - 1
    c = constants(width)
    rows = rows_ref[...]
    ones = c["ones"]

    @pl.when(pl.program_id(0) == 0)
    def _():
        map_now[...] = c["eye"]
        add_now[...] = jnp.zeros_like(add_now)
        row_grads[...] = jnp.zeros_like(row_grads)

    state_map, state_add = map_now[...], add_now[...]
    column = lambda x: jnp.sum(x, axis=0, keepdims=True)
    for i in reversed(range(per)):
        at = slice(i * SPAN, (i + 1) * SPAN)
        q_here, v_here, g_here = q[at, :], v[at, :], gate[at, :]
        rate = jax.nn.sigmoid(rows[1:2] + rin[at, :])
        k = kp[at, :] * (1.0 + (rate - 1.0) * rows[3:4])
        unit, scale, extra, summed = normed(out_ref[at, :], q_here, k, v_here, rows, c)
        grad = sum(x[at, :].astype(f32) for x in d_gated)
        if i == per - 1:
            grad = grad + jnp.where(last_row, fix, 0.0)
        d_gate[at, :] = (grad * summed).astype(bf16)
        d_sum = grad * g_here
        d_unit = d_sum * rows[5:6]
        d_here = scale * (
            d_unit
            - head_sum(d_unit, ones) * (1.0 / SPAN)
            - unit * head_sum(d_unit * unit, ones) * (1.0 / SPAN)
        )
        d_extra = head_sum(d_sum * v_here, ones)
        d_out[at, :] = d_here
        dq_post[at, :] = d_extra * k * rows[4:5]
        dk_post[at, :] = d_extra * q_here * rows[4:5]
        dv_post[at, :] = d_sum * extra
        row_grads[4:5, :] += column(d_extra * q_here * k)
        row_grads[5:6, :] += column(d_sum * unit)
        row_grads[6:7, :] += column(d_sum)
        maps[at, :] = state_map
        adds[at, :] = state_add
        carry_here = carry[i * width : (i + 1) * width, :]
        both = dot(
            jnp.concatenate([state_map, state_add], axis=0).astype(bf16), carry_here, 1, 1
        )
        state_map = both[:SPAN]
        state_add = both[SPAN:] + fold(cross(d_here, read[at, :]), c["mask"])
    map_now[...] = state_map
    add_now[...] = state_add
    map_end[...] = state_map
    add_end[...] = state_add


def grads_kernel(per, q, kp, v, din, rin, lat_ref, d_gate_ref, rows_ref, up_ref, push_ref, inv_ref, uk_ref, qk_ref, qr_ref,
                 starts, ends, d_out, dq_post, dk_post, dv_post, maps, adds, grad_in, dq_ref,
                 dkp_ref, dv_ref, pre_ref, row_grads, up_grads):
    c = constants(q.shape[1])
    up = up_ref[...]
    rows = rows_ref[...]
    mask, ones = c["mask"], c["ones"]
    cat = lambda *parts: jnp.concatenate(parts, axis=0)
    column = lambda x: jnp.sum(x, axis=0, keepdims=True)

    @pl.when(pl.program_id(0) == 0)
    def _():
        row_grads[...] = jnp.zeros_like(row_grads)
        up_grads[...] = jnp.zeros_like(up_grads)

    zero = jnp.zeros((SPAN, mask.shape[0]), f32)
    rank, gate_at = low_parts(up.shape[0])
    lane = lax.broadcasted_iota(jnp.int32, (SPAN, up.shape[0]), 1)
    low_row = lax.broadcasted_iota(jnp.int32, up_grads.shape, 0)
    for i in range(per):
        at = slice(i * SPAN, (i + 1) * SPAN)
        q_here, kp_here, v_here = q[at, :], kp[at, :], v[at, :]
        e = ready(q_here, kp_here, din[at, :], rin[at, :], rows, c)
        start, end, pushed, d_read = starts[at, :], ends[at, :], push_ref[at, :], d_out[at, :]
        grad_end = adds[at, :] + times(grad_in[...], maps[at, :], mask, 0)
        grown = grad_end * e["last"]
        by_state = times(cat(e["K"], e["R"]), grown, mask, 1)
        d_push = -fold(cross(qr_ref[at, :], d_read), mask) - by_state[SPAN:]
        d_rhs = fold(cross(inv_ref[at, :], d_push), mask)
        d_value = (
            by_state[:SPAN]
            + fold(cross(cat(qk_ref[at, :], uk_ref[at, :]), cat(d_read, d_rhs)), mask)
        )
        both = cat(d_rhs, d_read)
        by_value = times(both, v_here, mask, 1)
        by_push = times(both, pushed, mask, 1)
        d_key_pairs = cat(
            jnp.where(c["strict"], by_value[:SPAN], zero), jnp.where(c["incl"], by_value[SPAN:], zero)
        )
        d_removal_pairs = cat(
            jnp.where(c["strict"], -by_push[:SPAN], zero), jnp.where(c["incl"], -by_push[SPAN:], zero)
        )
        d_queries = (
            times(both, start, mask, 0)
            + times(d_key_pairs, e["K"], mask, 0)
            + times(d_removal_pairs, e["R"], mask, 0)
        )
        by_grown = times(cat(v_here, -pushed), grown, mask, 0)
        queries = cat(e["U"], e["Q"])
        d_k_grown = by_grown[:SPAN] + fold(cross(d_key_pairs, queries), mask)
        d_r_grown = by_grown[SPAN:] + fold(cross(d_removal_pairs, queries), mask)
        d_u_grown, d_q_grown = d_queries[:SPAN], d_queries[SPAN:]
        on_unit = d_u_grown * e["U"]
        steps = d_q_grown * e["Q"] - d_k_grown * e["K"] - d_r_grown * e["R"] + on_unit
        d_log = exact_left(c["upper"], steps) - on_unit + column(grad_end * end)
        rate = e["rate"]
        d_k = d_k_grown * e["down"] + dk_post[at, :]
        d_removal = d_r_grown * e["down"]
        d_unit = d_u_grown * e["before"] + d_removal * rate
        d_rate_value = d_removal * e["unit"] + d_k * kp_here * rows[3:4]
        d_scaled = e["inv"] * (d_unit - e["unit"] * head_sum(d_unit * e["unit"], ones))
        d_rate = d_rate_value * rate * (1.0 - rate)
        d_decay = d_log * e["log_decay"] * (1.0 - e["sig"])
        dq_ref[at, :] = (d_q_grown * e["up"] + dq_post[at, :]).astype(bf16)
        dkp_ref[at, :] = (d_k * (1.0 + (rate - 1.0) * rows[3:4]) + d_scaled * rows[2:3]).astype(bf16)
        dv_ref[at, :] = (d_value + dv_post[at, :]).astype(bf16)
        lat = lat_ref[at, :]
        low = lat.astype(bf16)
        d_outs = (d_decay.astype(bf16), d_rate.astype(bf16), d_gate_ref[at, :])
        pick = lambda where, parts: jnp.where(
            where < rank, parts[0], jnp.where(where < gate_at, parts[1], parts[2])
        )
        slope = pick(lane, (1.0 - lat * lat, jnp.ones_like(lat), lat * (1.0 - lat)))
        pre = pick(lane, [dot(x, up, 1, 1) for x in d_outs]) * slope
        pre_ref[at, :] = pre.astype(bf16)
        up_grads[...] += pick(low_row, [dot(low, x, 0, 0) for x in d_outs])
        row_grads[0:1, :] += column(d_decay)
        row_grads[1:2, :] += column(d_rate)
        row_grads[2:3, :] += column(d_scaled * kp_here)
        row_grads[3:4, :] += column(d_k * kp_here * (rate - 1.0))


def run_blocks(kernel, name, ins, outs, scratch, tokens, reverse=False):
    count = tokens // SPAN
    per = blocks_per_step(count)
    steps = count // per

    def spec(shape, cut):
        if not cut:
            return pl.BlockSpec(shape, lambda i: (0, 0))
        rows = shape[0] // steps
        if reverse:
            return pl.BlockSpec((rows, shape[1]), lambda i: (steps - 1 - i, 0))
        return pl.BlockSpec((rows, shape[1]), lambda i: (i, 0))

    return pl.pallas_call(
        functools.partial(kernel, per),
        grid=(steps,),
        in_specs=[spec(x.shape, cut) for x, cut in ins],
        out_specs=[spec(shape, cut) for shape, _, cut in outs],
        out_shape=[jax.ShapeDtypeStruct(shape, kind) for shape, kind, _ in outs],
        scratch_shapes=[pltpu.VMEM(shape, f32) for shape in scratch],
        compiler_params=pltpu.CompilerParams(dimension_semantics=("arbitrary",)),
        cost_estimate=pl.CostEstimate(flops=10**10, bytes_accessed=2 * 10**7, transcendentals=0),
        name=name,
    )(*[x for x, _ in ins])


def low_parts(width):
    return width // 4, width // 2


def mixed(unit, edge, norms, count):
    first = unit * norms[0:1] + norms[1:2]
    before = (edge[0:1] * norms[0:1] + norms[1:2]) * edge[1:2]
    row = lax.broadcasted_iota(jnp.int32, first.shape, 0)
    diff = jnp.where(row == 0, before, pltpu.roll(first, 1, 0)) - first
    return diff, [(first + diff * norms[4 + i : 5 + i]).astype(bf16) for i in range(count)]


def slab_weights(gathered, width):
    parts, rows, _ = gathered.shape
    part = rows // 4
    piece = lambda i, w: jnp.concatenate(
        [gathered[j, i * part : (i + 1) * part, :w] for j in range(parts)], axis=0
    )
    return [piece(i, width) for i in range(3)] + [piece(3, gathered.shape[2])]


def project_kernel(unit, edge, norms, gathered, up, q, kp, v, din, rin, gate, lat, low_total):
    width = q.shape[1]
    step = pl.program_id(0)
    norms_here = norms[...]
    _, mixes = mixed(unit[...], edge[...], norms_here, 6)
    w_q, w_k, w_v, w_low = slab_weights(gathered, width)
    low_width = w_low.shape[1]
    rank, gate_at = low_parts(low_width)
    lane = lax.broadcasted_iota(jnp.int32, low_total.shape, 1)
    low = jnp.where(
        lane < rank,
        dot(mixes[1], w_low, 1, 0),
        jnp.where(lane < gate_at, dot(mixes[4], w_low, 1, 0), dot(mixes[5], w_low, 1, 0)),
    )

    @pl.when(step == 0)
    def _():
        q[...] = dot(mixes[0], w_q, 1, 0)
        kp[...] = dot(mixes[2], w_k, 1, 0)
        v[...] = dot(mixes[3], w_v, 1, 0)
        low_total[...] = low

    @pl.when(step > 0)
    def _():
        q[...] += dot(mixes[0], w_q, 1, 0)
        kp[...] += dot(mixes[2], w_k, 1, 0)
        v[...] += dot(mixes[3], w_v, 1, 0)
        low_total[...] += low

    @pl.when(step == pl.num_programs(0) - 1)
    def _():
        total = low_total[...]
        lats = jnp.where(
            lane < rank, jnp.tanh(total), jnp.where(lane < gate_at, total, jax.nn.sigmoid(total))
        )
        lat[...] = lats
        zero = jnp.zeros_like(lats)
        chosen = lambda where: jnp.where(where, lats, zero).astype(bf16)
        din[...] = dot(chosen(lane < rank), up[...], 1, 0)
        rin[...] = dot(chosen((lane >= rank) & (lane < gate_at)), up[...], 1, 0)
        gate[...] = dot(chosen(lane >= gate_at), up[...], 1, 0)


def unproject_kernel(here, unit, edge, scales, norms, gathered, dq, dkp, dv, pre, d_mid, packed,
                     feature, edge_fix, *rest):
    pieces, (all_first, all_unit) = rest[:-2], rest[-2:]
    width = dq.shape[1]
    step = pl.program_id(0)
    n = norms[...]
    edge_here = edge[...]
    unit_here = unit[...]
    diff, mixes = mixed(unit_here, edge_here, n, 6)
    weights = slab_weights(gathered, width)
    w_low = weights[3]
    slab, low_width = w_low.shape
    rank, gate_at = low_parts(low_width)
    pre_here = pre[...]
    lane = lax.broadcasted_iota(jnp.int32, pre_here.shape, 1)
    none = jnp.zeros_like(pre_here)
    pres = [
        jnp.where(lane < rank, pre_here, none),
        jnp.where((lane >= rank) & (lane < gate_at), pre_here, none),
        jnp.where(lane >= gate_at, pre_here, none),
    ]
    sources = [(0, dq[...], 0), (2, dkp[...], 1), (3, dv[...], 2), (1, pres[0], 3), (4, pres[1], 3),
               (5, pres[2], 3)]
    low_lane = lax.broadcasted_iota(jnp.int32, (slab, low_width), 1)
    column = lambda x: jnp.sum(x, axis=0, keepdims=True)
    parts = gathered.shape[0]
    part = slab // parts
    direct = shifted = None
    low_grad = None
    for mix, grad, which in sources:
        weight_grad = dot(mixes[mix], grad, 0, 0)
        if which < 3:
            for j in range(parts):
                packed[j, which * part : (which + 1) * part, :width] = weight_grad[
                    j * part : (j + 1) * part
                ].astype(bf16)
                if width < low_width:
                    packed[j, which * part : (which + 1) * part, width:] = jnp.zeros(
                        (part, low_width - width), bf16
                    )
        else:
            low_grad = weight_grad if low_grad is None else low_grad + weight_grad
        d_mix = dot(grad, weights[which], 1, 1)
        feature[4 + mix : 5 + mix, :] = column(d_mix * diff)
        to_shift = d_mix * n[4 + mix : 5 + mix]
        shifted = to_shift if shifted is None else shifted + to_shift
        direct = d_mix - to_shift if direct is None else direct + (d_mix - to_shift)
    for j in range(parts):
        packed[j, 3 * part : 4 * part, :] = low_grad[j * part : (j + 1) * part].astype(bf16)
    tokens = unit_here.shape[0]
    row = lax.broadcasted_iota(jnp.int32, shifted.shape, 0)
    d_first = direct + jnp.where(row == tokens - 1, 0.0, pltpu.roll(shifted, tokens - 1, 0))
    before = shifted[0:1] * edge_here[1:2]
    feature[0:1, :] = column(d_first * unit_here) + before * edge_here[0:1]
    feature[1:2, :] = column(d_first) + before
    feature[2:4, :] = jnp.zeros_like(feature[2:4, :])
    feature[10:, :] = jnp.zeros_like(feature[10:, :])
    at = pl.ds(pl.multiple_of(step * slab, slab), slab)
    all_first[:tokens, at] = d_first * n[0:1]
    all_first[tokens:, at] = jnp.broadcast_to(before * n[0:1], (8, slab))
    all_unit[:tokens, at] = unit_here
    all_unit[tokens:, at] = jnp.broadcast_to(edge_here[0:1], (8, slab))

    @pl.when(step == pl.num_programs(0) - 1)
    def _():
        d_unit = all_first[...]
        units = all_unit[...]
        features = d_unit.shape[1]
        mean = jnp.sum(d_unit, axis=1, keepdims=True) * (1.0 / features)
        along = jnp.sum(d_unit * units, axis=1, keepdims=True) * (1.0 / features)
        result = scales[...] * (d_unit - mean - units * along)
        edge_fix[...] = result[tokens:] + d_mid[tokens + EDGE - 8 :, :]
        all_first[:tokens, :] = result[:tokens] + d_mid[:tokens, :]
        send_pieces(pieces, all_first, here[0])


EDGE = 16


def share_of(here, by, devices, size):
    return pl.ds(pl.multiple_of(lax.rem(here + by + devices, devices) * size, size), size)


def send_pieces(pieces, whole, here):
    share = pieces[0].shape[0]
    for by, piece in enumerate(pieces):
        piece[...] = whole[share_of(here, by, len(pieces), share), :].astype(piece.dtype)


def channel_kernel(devices, *refs):
    here, stream, edge_stream, has_edge, cot, norms, out_full, key, value = refs[:9]
    gated, edges = refs[9 : 9 + devices], refs[9 + devices : 9 + 2 * devices]
    refs = refs[9 + 2 * devices :]
    ffn_in, hidden, d_pre, cot_low, d_mid_low, d_mid, feature, middle_share = refs[:8]
    ffn_pieces, refs = refs[8 : 8 + devices], refs[8 + devices :]
    grad_pieces, refs = refs[:devices], refs[devices:]
    fix_pieces, refs = refs[:devices], refs[devices:]
    middle, unit, scale, diff, d_ffn, ffn_out = refs
    step = pl.program_id(0)
    tokens, features = stream.shape
    width = gated[0].shape[1]
    n = norms[...]
    flag = has_edge[0:1, 0:1]
    row = lax.broadcasted_iota(jnp.int32, (tokens + EDGE, features), 0)

    @pl.when(step == 0)
    def _():
        middle[:tokens, :] = stream[...]
        middle[tokens:, :] = edge_stream[...]
        for by in range(devices):
            rows = out_full[share_of(here[0], -by, devices, width), :]
            middle[:tokens, :] += dot(gated[by][...], rows, 1, 0)
            middle[tokens:, :] += dot(edges[by][...], rows, 1, 0)
        middle_share[...] = middle[share_of(here[0], 0, devices, tokens // devices), :]
        values = middle[...]
        center = values - jnp.sum(values, axis=1, keepdims=True) * (1.0 / features)
        spread_here = jnp.sum(center * center, axis=1, keepdims=True) * (1.0 / features)
        scale_here = lax.rsqrt(spread_here + 1e-05)
        unit_here = center * scale_here
        unit[...] = unit_here
        scale[...] = scale_here
        norm = unit_here * n[2:3] + n[3:4]
        before = pltpu.roll(norm, 1, 0)
        diff_here = jnp.where(row == 0, before * flag, before) - norm
        diff[...] = diff_here
        ffn_in[...] = (norm + diff_here * n[10:11])[:tokens].astype(bf16)
        cot_low[...] = cot[...].astype(bf16)
        d_ffn[...] = jnp.zeros_like(d_ffn)
        ffn_out[...] = jnp.zeros_like(ffn_out)

    act = jnp.maximum(dot(ffn_in[...], key[...], 1, 0), 0.0)
    hidden_here = (act * act).astype(bf16)
    hidden[...] = hidden_here
    d_pre_here = (dot(cot_low[...], value[...], 1, 1) * 2.0 * act).astype(bf16)
    d_pre[...] = d_pre_here
    d_ffn[:tokens, :] += dot(d_pre_here, key[...], 1, 1)
    ffn_out[...] += dot(hidden_here, value[...], 1, 0)

    @pl.when(step == pl.num_programs(0) - 1)
    def _():
        send_pieces(ffn_pieces, ffn_out, here[0])
        grad = d_ffn[...]
        to_shift = grad * n[10:11]
        moved = pltpu.roll(to_shift, tokens + EDGE - 1, 0)
        d_second = grad - to_shift + jnp.where(row == tokens + EDGE - 1, moved * flag, moved)
        unit_here = unit[...]
        column = lambda x: jnp.sum(x, axis=0, keepdims=True)
        feature[...] = jnp.zeros_like(feature)
        feature[0:1, :] = column(d_second * unit_here)
        feature[1:2, :] = column(d_second)
        feature[2:3, :] = column(grad * diff[...])
        d_unit = d_second * n[2:3]
        mean = jnp.sum(d_unit, axis=1, keepdims=True) * (1.0 / features)
        along = jnp.sum(d_unit * unit_here, axis=1, keepdims=True) * (1.0 / features)
        d_mid_here = scale[...] * (d_unit - mean - unit_here * along)
        d_mid[...] = d_mid_here
        d_mid_low[tokens:, :] = d_mid_here[tokens:].astype(bf16)
        d_mid_low[:tokens, :] = (d_mid_here[:tokens] + cot[...] * (1.0 / devices)).astype(bf16)
        for by in range(devices):
            rows = out_full[share_of(here[0], by, devices, width), :]
            grad_pieces[by][...] = dot(d_mid_low[:tokens, :], rows, 1, 1).astype(bf16)
            fix_pieces[by][...] = dot(d_mid_low[tokens:, :], rows, 1, 1).astype(bf16)


def large_kernel(devices, *refs):
    here, hidden, cot_low, ffn_in, d_pre, d_mid_low = refs[:6]
    gated, edges, large = refs[6 : 6 + devices], refs[6 + devices : 6 + 2 * devices], refs[-1]
    tokens, hidden_here = hidden.shape
    part = large.shape[2]
    width = gated[0].shape[1]
    large[0, :hidden_here, :] = dot(hidden[...], cot_low[...], 0, 0).astype(bf16)
    key_grad = dot(ffn_in[...], d_pre[...], 0, 0).astype(bf16)
    for j in range(hidden_here // part):
        at = hidden_here + j * part
        large[0, at : at + part, :] = key_grad[:, j * part : (j + 1) * part]
    grad, grad_edge = d_mid_low[:tokens, :], d_mid_low[tokens:, :]
    for by in range(devices):
        rows = dot(gated[by][...], grad, 0, 0) + dot(edges[by][...], grad_edge, 0, 0)
        at = lax.rem(here[0] - by + devices, devices) * width + 2 * hidden_here
        large[0, pl.ds(pl.multiple_of(at, width), width), :] = rows.astype(bf16)


def run_slabs(kernel, name, ins, outs, scratch, slabs):
    def spec(shape, cut):
        shape = tuple(shape)
        if cut == "scalar":
            return pl.BlockSpec(memory_space=pltpu.SMEM)
        if cut is None:
            return pl.BlockSpec(shape, lambda i: (0,) * len(shape))
        dim, size = cut
        block = list(shape)
        block[dim] = shape[dim] // slabs
        if size is not None:
            block[size[0]] = size[1]
        return pl.BlockSpec(tuple(block), lambda i: tuple(i if k == dim else 0 for k in range(len(shape))))

    return pl.pallas_call(
        kernel,
        grid=(slabs,),
        in_specs=[spec(x.shape, cut) for x, cut in ins],
        out_specs=[spec(shape, cut) for shape, _, cut in outs],
        out_shape=[jax.ShapeDtypeStruct(shape, kind) for shape, kind, _ in outs],
        scratch_shapes=[pltpu.VMEM(shape, f32) for shape in scratch],
        compiler_params=pltpu.CompilerParams(dimension_semantics=("arbitrary",)),
        cost_estimate=pl.CostEstimate(flops=10**10, bytes_accessed=2 * 10**7, transcendentals=0),
        name=name,
    )(*[x for x, _ in ins])


def to_next(x, axis, by):
    devices = lax.axis_size(axis)
    pairs_here = [(i, i + by) for i in range(devices) if 0 <= i + by < devices]
    return lax.ppermute(x, axis, pairs_here)


def around(x, by):
    devices = lax.axis_size("mp")
    return lax.ppermute(x, "mp", [(i, (i + by) % devices) for i in range(devices)])


def gather_shares(x):
    devices = lax.axis_size("mp")
    came = [x] + [around(x, by) for by in range(1, devices)]
    turned = jnp.stack([came[-k % devices] for k in range(devices)] * 2)
    at = (devices - lax.axis_index("mp")) % devices
    return lax.dynamic_slice_in_dim(turned, at, devices, 0)


def scatter_shares(x):
    devices = lax.axis_size("mp")
    here = lax.axis_index("mp")
    term = lambda at: lax.dynamic_index_in_dim(x, at % devices, 0, keepdims=False)
    total = term(here).astype(f32)
    for by in range(1, devices):
        total = total + around(term(here + by), by).astype(f32)
    return total


def mm(a, b):
    return jnp.dot(a, b, preferred_element_type=f32)


def mm_right(a, b):
    return dot(a, b, 1, 1)


def mm_left(a, b):
    return dot(a, b, 0, 0)


def statistics(values):
    center = values - jnp.mean(values, axis=-1, keepdims=True)
    scale = lax.rsqrt(jnp.mean(center * center, axis=-1, keepdims=True) + 1e-05)
    return center * scale, scale


def norm_back(grad, unit, scale, gain):
    d_unit = grad * gain
    mean = jnp.mean(d_unit, axis=-1, keepdims=True)
    along = jnp.mean(d_unit * unit, axis=-1, keepdims=True)
    return scale * (d_unit - mean - unit * along), jnp.sum(grad * unit, axis=0), jnp.sum(grad, axis=0)


def earlier(values, edge):
    return jnp.concatenate([values[1:], edge], axis=0)


def later(values, edge):
    return jnp.concatenate([edge, values[:-1]], axis=0)


def carry_states(state_map, state_add, by):
    entering = to_next(state_add.astype(bf16), "seq", by).astype(f32)
    heads = state_map.shape[1] // SPAN
    apart = lambda x: x.reshape(SPAN, heads, SPAN).transpose(1, 0, 2)
    for _ in range(lax.axis_size("seq") - 2):
        moved = jnp.einsum("hij,hjl->hil", apart(entering), apart(state_map), precision="highest")
        passed = moved.transpose(1, 0, 2).reshape(state_add.shape) + state_add
        entering = to_next(passed.astype(bf16), "seq", by).astype(f32)
    return entering


def wide(x, width):
    return jnp.pad(x, ((0, 0), (0, width - x.shape[1])))


def body(inputs, rkv_weight, output_weight, first_factors, second_factors, gate_first, gate_second,
         key_weight, value_weight, head_table, feature_table, cotangent):
    group = ("dp", "seq")
    count = lax.axis_size("dp") * lax.axis_size("seq")
    mp = lax.axis_size("mp")
    mp_here = lax.axis_index("mp")
    stream = inputs[0]
    cot = cotangent[0]
    tokens, features = stream.shape
    share = tokens // mp
    share_at = mp_here * share
    part = features // count
    width = rkv_weight.shape[2]
    heads = width // SPAN
    rank, gate_rank = first_factors.shape[2], gate_first.shape[1]
    low_width = 2 * rank + gate_rank
    lanes = max(width, low_width, part)
    up_rows, gate_rows = second_factors.shape[1], gate_second.shape[0]
    head_part = head_table.shape[2]
    here = mp_here.astype(jnp.int32).reshape(1)
    edge_stream = to_next(stream[-EDGE:], "seq", 1)
    edge_row = edge_stream[EDGE - 1 :]
    pieces = [
        wide(rkv_weight.reshape(3 * part, width), lanes),
        wide(jnp.concatenate([first_factors[0], first_factors[1], gate_first], axis=1), lanes),
        wide(second_factors.reshape(2 * up_rows, width), lanes),
        wide(gate_second, lanes),
        wide(feature_table, lanes),
        wide(head_table.reshape(7, heads * head_part), lanes),
    ]
    edges = [0]
    for piece in pieces:
        edges.append(edges[-1] + piece.shape[0])
    packed = jnp.concatenate(pieces, axis=0)
    rows_full = -(-packed.shape[0] // 16) * 16
    packed = jnp.pad(packed, ((0, rows_full - packed.shape[0]), (0, 0)))
    gathered = lax.all_gather(packed, group, axis=0, tiled=False)
    cut = lambda i, w: gathered[:, edges[i] : edges[i + 1], :w]
    up = cut(2, width).reshape(count, 2, up_rows, width).transpose(1, 0, 2, 3)
    up = jnp.concatenate(
        [up.reshape(2 * rank, width), cut(3, width).reshape(gate_rank, width)], axis=0
    )
    norms = cut(4, part).transpose(1, 0, 2).reshape(11, features).astype(f32)
    norms = jnp.pad(norms, ((0, 5), (0, 0)))
    head_rows = (
        cut(5, heads * head_part)
        .reshape(count, 7, heads, head_part)
        .transpose(1, 2, 0, 3)
        .reshape(7, width)
        .astype(f32)
    )
    head_rows = jnp.pad(head_rows, ((0, 1), (0, 0)))

    out_column = gather_shares(output_weight).reshape(features, part)
    rest = lax.all_gather(
        jnp.concatenate([value_weight, out_column], axis=0), group, axis=0, tiled=False
    )
    hidden_here = value_weight.shape[0]
    key_full = lax.all_gather(key_weight, group, axis=0, tiled=True)

    unit_one, scale_one = statistics(stream)
    edge_unit, edge_scale = statistics(edge_row)
    has_edge = (lax.axis_index("seq") > 0).astype(f32)
    edge = jnp.concatenate(
        [edge_unit, jnp.broadcast_to(has_edge, (1, features)), jnp.zeros((6, features), f32)]
    )
    slab = max(256, part)
    slabs = features // slab
    in_slabs = (1, None)
    of_gathered = (0, (1, 4 * part))
    whole = (tokens, width)
    q, kp, v, din, rin, gate, lat = run_slabs(
        project_kernel,
        "project",
        [(unit_one, in_slabs), (edge, in_slabs), (norms, in_slabs), (gathered, of_gathered), (up, None)],
        [(whole, f32, None)] * 6 + [((tokens, low_width), f32, None)],
        [(tokens, low_width)],
        slabs,
    )

    state = (SPAN, width)
    (local_out, read, push_map, push, inv, uk, qk, qr, carry, maps, adds, map_end, add_end) = run_blocks(
        local_kernel,
        "local",
        [(q, True), (kp, True), (v, True), (din, True), (rin, True), (head_rows, False)],
        [(whole, f32, True)] * 4
        + [(whole, bf16, True)] * 4
        + [((tokens // SPAN * width, width), bf16, True)]
        + [(whole, f32, True)] * 2
        + [(state, f32, False)] * 2,
        [state, state],
        tokens,
    )
    entering = carry_states(map_end, add_end, 1)
    gated, read_out, pushed, starts, ends = run_blocks(
        finish_kernel,
        "finish",
        [(x, True) for x in (q, kp, v, rin, gate)]
        + [(head_rows, False)]
        + [(x, True) for x in (local_out, read, push_map, push, maps, adds)]
        + [(entering, False)],
        [(whole, bf16, True)] + [(whole, f32, True)] * 4,
        [state],
        tokens,
    )

    gated_parts = [gated] + [around(gated, by) for by in range(1, mp)]
    gated_edge = to_next(gated[-EDGE:], "seq", 1)
    edge_parts = [gated_edge] + [around(gated_edge, by) for by in range(1, mp)]
    value_full = rest[:, :hidden_here].transpose(1, 0, 2).reshape(hidden_here, features)
    out_full = rest[:, hidden_here:].transpose(1, 0, 2).reshape(features, features)
    longer = tokens + EDGE
    lots = key_full.shape[1] // part
    channel = run_slabs(
        functools.partial(channel_kernel, mp),
        "channel",
        [(here, "scalar"), (stream, None), (edge_stream, None), (edge[1:2, :128], None), (cot, None)]
        + [(norms, None), (out_full, None), (key_full, (1, None)), (value_full, (0, None))]
        + [(x, None) for x in gated_parts + edge_parts],
        [
            ((tokens, features), bf16, None),
            ((tokens, hidden_here), bf16, (1, None)),
            ((tokens, hidden_here), bf16, (1, None)),
            ((tokens, features), bf16, None),
            ((longer, features), bf16, None),
            ((longer, features), f32, None),
            ((8, features), f32, None),
            ((share, features), f32, None),
        ]
        + [((share, features), bf16, None)] * mp
        + [(whole, bf16, None)] * mp
        + [((EDGE, width), bf16, None)] * mp,
        [(longer, features)] * 2
        + [(longer, 1)]
        + [(longer, features)] * 2
        + [(tokens, features)],
        max(1, hidden_here // 256),
    )
    ffn_in, hidden, d_pre, cot_low, d_mid_low, d_mid, second_rows, middle_share = channel[:8]
    ffn_pieces = channel[8 : 8 + mp]
    grad_pieces = channel[8 + mp : 8 + 2 * mp]
    fix_pieces = channel[8 + 2 * mp :]
    d_gated = [grad_pieces[0]] + [around(grad_pieces[by], by) for by in range(1, mp)]
    fixes = to_next(jnp.concatenate(fix_pieces, axis=1), "seq", -1)
    fixes = [fixes[:, by * width : (by + 1) * width] for by in range(mp)]
    fixes = [fixes[0]] + [around(fixes[by], by) for by in range(1, mp)]

    if part % 128 == 0:
        large = run_slabs(
            functools.partial(large_kernel, mp),
            "large",
            [(here, "scalar"), (hidden, None), (cot_low, (1, None)), (ffn_in, (1, None)), (d_pre, None)]
            + [(d_mid_low, (1, None))]
            + [(x, None) for x in gated_parts + edge_parts],
            [((count, 2 * hidden_here + features, part), bf16, (0, None))],
            [],
            count,
        )[0]
    else:
        by_part = lambda x: x.astype(bf16).reshape(x.shape[0], count, part).transpose(1, 0, 2)
        key_grad = mm_left(ffn_in, d_pre).astype(bf16)
        key_grad = key_grad.reshape(count, part, lots, part).transpose(0, 2, 1, 3)
        order = lambda parts: jnp.concatenate(parts[:1] + parts[:0:-1], axis=0)
        out_rows = order([mm_left(x, d_mid_low[:tokens]) for x in gated_parts]) + order(
            [mm_left(x, d_mid_low[tokens:]) for x in edge_parts]
        )
        large = jnp.concatenate(
            [
                by_part(mm_left(hidden, cot_low)),
                key_grad.reshape(count, lots * part, part),
                by_part(jnp.roll(out_rows, mp_here * width, axis=0)),
            ],
            axis=1,
        )
    large = lax.psum_scatter(large, group, scatter_dimension=0, tiled=False)
    block_out = middle_share + sum(
        [ffn_pieces[0].astype(f32)]
        + [around(ffn_pieces[by], by).astype(f32) for by in range(1, mp)]
    )

    (d_read, dq_post, dk_post, dv_post, d_gate, back_maps, back_adds, back_map_end, back_add_end,
     row_grads_post) = run_blocks(
        functools.partial(reads_kernel, mp),
        "reads",
        [(x, True) for x in (q, kp, v, rin, gate)]
        + [(head_rows, False)]
        + [(x, True) for x in (read_out, read, carry)]
        + [(x, True) for x in d_gated]
        + [(x, False) for x in fixes],
        [(whole, f32, True)] * 4
        + [(whole, bf16, True)]
        + [(whole, f32, True)] * 2
        + [(state, f32, False)] * 2
        + [((8, width), f32, False)],
        [state, state],
        tokens,
        reverse=True,
    )
    grad_in = carry_states(back_map_end, back_add_end, -1)
    dq, dkp, dv, pre, row_grads, up_grads = run_blocks(
        grads_kernel,
        "grads",
        [(x, True) for x in (q, kp, v, din, rin, lat, d_gate)]
        + [(head_rows, False), (up, False)]
        + [
            (x, True)
            for x in (pushed, inv, uk, qk, qr, starts, ends, d_read, dq_post, dk_post, dv_post,
                      back_maps, back_adds)
        ]
        + [(grad_in, False)],
        [(whole, bf16, True)] * 3
        + [((tokens, low_width), bf16, True), ((8, width), f32, False)]
        + [((low_width, width), f32, False)],
        [],
        tokens,
    )
    row_grads = jnp.concatenate([row_grads[:4], row_grads_post[4:7]], axis=0)

    scales = jnp.concatenate([scale_one, jnp.broadcast_to(edge_scale, (8, 1))], axis=0)
    unprojected = run_slabs(
        unproject_kernel,
        "unproject",
        [(here, "scalar"), (unit_one, in_slabs), (edge, in_slabs), (scales, None), (norms, in_slabs)]
        + [(gathered, of_gathered), (dq, None), (dkp, None), (dv, None), (pre, None), (d_mid, None)],
        [
            ((count, 4 * part, lanes), bf16, (0, None)),
            ((16, features), f32, in_slabs),
            ((8, features), f32, None),
        ]
        + [((share, features), bf16, None)] * mp,
        [(tokens + 8, features)] * 2,
        slabs,
    )
    packed, feature_grad, edge_fix = unprojected[:3]
    stream_pieces = unprojected[3:]
    edge_fix = edge_fix[7:]
    fix = jnp.sum(gather_shares(to_next(edge_fix, "seq", -1)), axis=0)
    last = lax.broadcasted_iota(jnp.int32, (share, 1), 0) == share - 1
    input_grad = lax.dynamic_slice_in_dim(cot, share_at, share, 0) + sum(
        [stream_pieces[0].astype(f32)]
        + [around(stream_pieces[by], by).astype(f32) for by in range(1, mp)]
    )
    input_grad = input_grad + jnp.where(last & (mp_here == mp - 1), fix, 0.0)

    feature_grad = jnp.concatenate(
        [feature_grad[:2], second_rows[:2], feature_grad[4:10], second_rows[2:3]]
    )
    split_rows = lambda x: x.reshape(count, x.shape[0] // count, x.shape[1])
    wider = lambda x: jnp.pad(x.astype(bf16), ((0, 0), (0, 0), (0, lanes - x.shape[2])))
    grads = [
        split_rows(up_grads[:rank]),
        split_rows(up_grads[rank : 2 * rank]),
        split_rows(up_grads[2 * rank :]),
        feature_grad.reshape(11, count, part).transpose(1, 0, 2),
        row_grads.reshape(7, heads, count, head_part)
        .transpose(2, 0, 1, 3)
        .reshape(count, 7, heads * head_part),
    ]
    grads = jnp.concatenate([wider(x) for x in grads], axis=1)
    grads = jnp.pad(grads, ((0, 0), (0, rows_full - 4 * part - grads.shape[1]), (0, 0)))
    grads = jnp.concatenate([packed, grads], axis=1)
    grads, large = lax.optimization_barrier((grads, large))
    value_grad = large[:hidden_here].astype(f32)
    key_grad = large[hidden_here : hidden_here + lots * part].reshape(lots, part, part)
    key_grad = key_grad.transpose(1, 0, 2).reshape(part, lots * part).astype(f32)
    out_grad = scatter_shares(large[hidden_here + lots * part :].reshape(mp, width, part))
    summed = lax.psum_scatter(grads, group, scatter_dimension=0, tiled=False)
    own = lambda i, w: summed[edges[i] : edges[i + 1], :w].astype(f32)
    everywhere = jnp.concatenate(
        [summed[edges[1] : edges[2]], summed[edges[4] : edges[5]]], axis=0
    )
    everywhere = jnp.sum(gather_shares(everywhere).astype(f32), axis=0)
    down_sum = everywhere[:part]
    return (
        block_out[None],
        input_grad[None],
        own(0, width).reshape(3, part, width),
        out_grad,
        jnp.stack([down_sum[:, :rank], down_sum[:, rank : 2 * rank]]),
        own(2, width).reshape(2, up_rows, width),
        down_sum[:, 2 * rank : low_width],
        own(3, width),
        key_grad,
        value_grad,
        own(5, heads * head_part).reshape(7, heads, head_part),
        everywhere[part:, :part],
    )


def solution(mesh):
    both = ("dp", "seq")
    return jax.shard_map(
        body,
        mesh=mesh,
        in_specs=(
            P("dp", "seq", None),
            P(None, both, "mp"),
            P("mp", both),
            P(None, both, None),
            P(None, both, "mp"),
            P(both, None),
            P(both, "mp"),
            P(both, "mp"),
            P("mp", both),
            P(None, "mp", both),
            P(None, both),
            P("dp", "seq", None),
        ),
        out_specs=(
            P("dp", ("seq", "mp"), None),
            P("dp", ("seq", "mp"), None),
            P(None, both, "mp"),
            P("mp", both),
            P(None, both, None),
            P(None, both, "mp"),
            P(both, None),
            P(both, "mp"),
            P(both, "mp"),
            P("mp", both),
            P(None, "mp", both),
            P(None, both),
        ),
        check_vma=False,
    )
```

```python
import functools

import jax
import jax.numpy as jnp
from jax import lax
from jax.experimental import pallas as pl
from jax.experimental.pallas import tpu as pltpu
from jax.sharding import PartitionSpec as P


SPAN = 64
f32 = jnp.float32
bf16 = jnp.bfloat16


def halves(x):
    high = x.astype(bf16)
    return high, (x - high.astype(f32)).astype(bf16)


def dot(a, b, ca, cb):
    return lax.dot_general(a, b, (((ca,), (cb,)), ((), ())), preferred_element_type=f32)


def spread(x, mask):
    tiled = jnp.concatenate([x] * (x.shape[1] // SPAN), axis=0)
    return jnp.where(mask, tiled, jnp.zeros_like(tiled))


def fold(x, mask):
    x = jnp.where(mask, x, jnp.zeros_like(x))
    return sum(x[i * SPAN : (i + 1) * SPAN] for i in range(x.shape[0] // SPAN))


def times(a, b, mask, cb):
    return dot(a.astype(bf16), spread(b.astype(bf16), mask), 1, cb)


def fine(a, b, mask, cb):
    ah, al = halves(a)
    bh, bl = halves(b)
    rows = a.shape[0]
    both = dot(jnp.concatenate([ah, al], axis=0), spread(bh, mask), 1, cb)
    return both[:rows] + both[rows:] + dot(ah, spread(bl, mask), 1, cb)


def cross(a, b):
    return dot(a.astype(bf16), b.astype(bf16), 0, 0)


def fine_cross(a, b):
    ah, al = halves(a)
    bh, bl = halves(b)
    return dot(
        jnp.concatenate([ah, al, ah], axis=0), jnp.concatenate([bh, bh, bl], axis=0), 0, 0
    )


def exact_left(ones, x):
    high = x.astype(bf16)
    rest = x - high.astype(f32)
    mid = rest.astype(bf16)
    low = (rest - mid.astype(f32)).astype(bf16)
    return dot(ones, high, 1, 0) + dot(ones, mid, 1, 0) + dot(ones, low, 1, 0)


def head_sum(x, ones):
    high, low = halves(x)
    rows = x.shape[0]
    both = dot(jnp.concatenate([high, low], axis=0), ones, 1, 0)
    return both[:rows] + both[rows:]


def constants(width):
    iota = lax.broadcasted_iota
    big_row = iota(jnp.int32, (width, width), 0)
    big_col = iota(jnp.int32, (width, width), 1)
    mask = (big_row // SPAN) == (big_col // SPAN)
    t = iota(jnp.int32, (SPAN, SPAN), 0)
    s = iota(jnp.int32, (SPAN, SPAN), 1)
    row = iota(jnp.int32, (SPAN, width), 0)
    col = iota(jnp.int32, (SPAN, width), 1) % SPAN
    one = lambda where: jnp.where(where, 1.0, 0.0).astype(f32)
    return dict(
        mask=mask,
        diagonal=one(big_row == big_col),
        ones=one(mask).astype(bf16),
        lower=one(t >= s).astype(bf16),
        upper=one(t <= s).astype(bf16),
        strict=row > col,
        incl=row >= col,
        eye=one(row == col),
        near=(row // 4 == col // 4) & (row > col),
        mid=(row // 16 == col // 16) & (row // 4 > col // 4),
        far=row // 16 > col // 16,
    )


def ready(q, kp, din, rin, rows, c):
    sig = jax.nn.sigmoid(rows[0:1] + din)
    log_decay = -0.6065306597126334 * sig
    rate = jax.nn.sigmoid(rows[1:2] + rin)
    scaled = kp * rows[2:3]
    inv = lax.rsqrt(head_sum(scaled * scaled, c["ones"]) + 1e-6)
    unit = scaled * inv
    removal = unit * rate
    total = exact_left(c["lower"], log_decay)
    up = jnp.exp(total)
    down = jnp.exp(-total)
    before = jnp.exp(total - log_decay)
    return dict(
        sig=sig,
        log_decay=log_decay,
        rate=rate,
        inv=inv,
        unit=unit,
        up=up,
        down=down,
        before=before,
        Q=q * up,
        U=unit * before,
        K=kp * (1.0 + (rate - 1.0) * rows[3:4]) * down,
        R=removal * down,
        last=up[SPAN - 1 : SPAN],
    )


def inverse(lower, c):
    mask = c["mask"]
    zero = jnp.zeros_like(lower)
    inner = jnp.where(c["near"], lower, zero)
    square = fine(inner, inner, mask, 0)
    out = c["eye"] - inner + square - fine(inner, square, mask, 0)
    for level in ("mid", "far"):
        step = fine(out, jnp.where(c[level], lower, zero), mask, 0)
        step_two = fine(step, step, mask, 0)
        first = out - fine(step, out, mask, 0)
        out = first + fine(step_two, first, mask, 0)
    return out


def pairs(e, c):
    mask = c["mask"]
    zero = jnp.zeros((SPAN, mask.shape[0]), f32)
    queries = jnp.concatenate([e["U"], e["Q"]], axis=0)
    by_key = fine(queries, e["K"], mask, 1)
    by_removal = fine(queries, e["R"], mask, 1)
    return (
        jnp.where(c["strict"], by_key[:SPAN], zero),
        jnp.where(c["incl"], by_key[SPAN:], zero),
        jnp.where(c["strict"], by_removal[:SPAN], zero),
        jnp.where(c["incl"], by_removal[SPAN:], zero),
    )


def blocks_per_step(count):
    return 2 if count % 2 == 0 else 1


def local_kernel(per, q, kp, v, din, rin, rows_ref, local_out, read, push_map, push, inv_out,
                 uk_out, qk_out, qr_out, carry, maps, adds, map_end, add_end, map_now, add_now):
    width = q.shape[1]
    c = constants(width)
    rows = rows_ref[...]

    @pl.when(pl.program_id(0) == 0)
    def _():
        map_now[...] = c["eye"]
        add_now[...] = jnp.zeros_like(add_now)

    chain = []
    for i in range(per):
        at = slice(i * SPAN, (i + 1) * SPAN)
        e = ready(q[at, :], kp[at, :], din[at, :], rin[at, :], rows, c)
        uk, qk, ur, qr = pairs(e, c)
        inv = inverse(ur, c)
        values = v[at, :]
        mixed = fine(jnp.concatenate([uk, qk], axis=0), values, c["mask"], 0)
        y = fine(inv, mixed[:SPAN], c["mask"], 0)
        w = fine(inv, e["U"], c["mask"], 0)
        local_out[at, :] = mixed[SPAN:] - fine(qr, y, c["mask"], 0)
        read[at, :] = e["Q"] - fine(qr, w, c["mask"], 0)
        push_map[at, :] = w
        push[at, :] = y
        inv_out[at, :] = inv.astype(bf16)
        uk_out[at, :] = uk.astype(bf16)
        qk_out[at, :] = qk.astype(bf16)
        qr_out[at, :] = qr.astype(bf16)
        carried = jnp.where(c["mask"], fine_cross(w, e["R"]), jnp.zeros_like(c["diagonal"]))
        carry_here = ((c["diagonal"] - carried) * e["last"]).astype(bf16)
        carry[i * width : (i + 1) * width, :] = carry_here
        added = fold(
            fine_cross(
                jnp.concatenate([values, y], axis=0), jnp.concatenate([e["K"], -e["R"]], axis=0)
            ),
            c["mask"],
        ) * e["last"]
        chain.append((at, carry_here, added))
    state_map, state_add = map_now[...], add_now[...]
    for at, carry_here, added in chain:
        both = dot(
            jnp.concatenate([state_map, state_add], axis=0).astype(bf16), carry_here, 1, 0
        )
        state_map, state_add = both[:SPAN], both[SPAN:] + added
        maps[at, :] = state_map
        adds[at, :] = state_add
    map_now[...] = state_map
    add_now[...] = state_add
    map_end[...] = state_map
    add_end[...] = state_add


def normed(out, q, k, v, rows, c):
    ones = c["ones"]
    center = out - head_sum(out, ones) * (1.0 / SPAN)
    spread_here = head_sum(center * center, ones) * (1.0 / SPAN)
    scale = lax.rsqrt(spread_here + 0.00064)
    unit = center * scale
    extra = head_sum(q * k * rows[4:5], ones)
    return unit, scale, extra, unit * rows[5:6] + rows[6:7] + extra * v


def finish_kernel(per, q, kp, v, rin, gate, rows_ref, local_out, read, push_map, push, maps, adds,
                  state_in, gated, out_ref, push_out, starts, ends, state_now):
    c = constants(q.shape[1])
    rows = rows_ref[...]
    mask = c["mask"]

    @pl.when(pl.program_id(0) == 0)
    def _():
        state_now[...] = state_in[...]

    entering = state_in[...]
    state = state_now[...]
    for i in range(per):
        at = slice(i * SPAN, (i + 1) * SPAN)
        starts[at, :] = state
        both = fine(jnp.concatenate([read[at, :], push_map[at, :]], axis=0), state, mask, 1)
        out = local_out[at, :] + both[:SPAN]
        push_out[at, :] = push[at, :] + both[SPAN:]
        out_ref[at, :] = out
        rate = jax.nn.sigmoid(rows[1:2] + rin[at, :])
        k = kp[at, :] * (1.0 + (rate - 1.0) * rows[3:4])
        _, _, _, summed = normed(out, q[at, :], k, v[at, :], rows, c)
        gated[at, :] = (summed * gate[at, :]).astype(bf16)
        state = adds[at, :] + times(entering, maps[at, :], mask, 0)
        ends[at, :] = state
    state_now[...] = state


def reads_kernel(devices, per, q, kp, v, rin, gate, rows_ref, out_ref, read, carry, *refs):
    d_gated, fixes, refs = refs[:devices], refs[devices : 2 * devices], refs[2 * devices :]
    d_out, dq_post, dk_post, dv_post, d_gate, maps, adds, map_end, add_end, row_grads = refs[:10]
    map_now, add_now = refs[10:]
    width = q.shape[1]
    first_step = (pl.program_id(0) == 0).astype(f32)
    fix = sum(x[...].astype(f32) for x in fixes)[EDGE - 1 : EDGE] * first_step
    last_row = lax.broadcasted_iota(jnp.int32, (SPAN, width), 0) == SPAN - 1
    c = constants(width)
    rows = rows_ref[...]
    ones = c["ones"]

    @pl.when(pl.program_id(0) == 0)
    def _():
        map_now[...] = c["eye"]
        add_now[...] = jnp.zeros_like(add_now)
        row_grads[...] = jnp.zeros_like(row_grads)

    state_map, state_add = map_now[...], add_now[...]
    column = lambda x: jnp.sum(x, axis=0, keepdims=True)
    for i in reversed(range(per)):
        at = slice(i * SPAN, (i + 1) * SPAN)
        q_here, v_here, g_here = q[at, :], v[at, :], gate[at, :]
        rate = jax.nn.sigmoid(rows[1:2] + rin[at, :])
        k = kp[at, :] * (1.0 + (rate - 1.0) * rows[3:4])
        unit, scale, extra, summed = normed(out_ref[at, :], q_here, k, v_here, rows, c)
        grad = sum(x[at, :].astype(f32) for x in d_gated)
        if i == per - 1:
            grad = grad + jnp.where(last_row, fix, 0.0)
        d_gate[at, :] = (grad * summed).astype(bf16)
        d_sum = grad * g_here
        d_unit = d_sum * rows[5:6]
        d_here = scale * (
            d_unit
            - head_sum(d_unit, ones) * (1.0 / SPAN)
            - unit * head_sum(d_unit * unit, ones) * (1.0 / SPAN)
        )
        d_extra = head_sum(d_sum * v_here, ones)
        d_out[at, :] = d_here
        dq_post[at, :] = d_extra * k * rows[4:5]
        dk_post[at, :] = d_extra * q_here * rows[4:5]
        dv_post[at, :] = d_sum * extra
        row_grads[4:5, :] += column(d_extra * q_here * k)
        row_grads[5:6, :] += column(d_sum * unit)
        row_grads[6:7, :] += column(d_sum)
        maps[at, :] = state_map
        adds[at, :] = state_add
        carry_here = carry[i * width : (i + 1) * width, :]
        both = dot(
            jnp.concatenate([state_map, state_add], axis=0).astype(bf16), carry_here, 1, 1
        )
        state_map = both[:SPAN]
        state_add = both[SPAN:] + fold(cross(d_here, read[at, :]), c["mask"])
    map_now[...] = state_map
    add_now[...] = state_add
    map_end[...] = state_map
    add_end[...] = state_add


def grads_kernel(per, q, kp, v, din, rin, lat_ref, d_gate_ref, rows_ref, up_ref, push_ref, inv_ref, uk_ref, qk_ref, qr_ref,
                 starts, ends, d_out, dq_post, dk_post, dv_post, maps, adds, grad_in, dq_ref,
                 dkp_ref, dv_ref, pre_ref, row_grads, up_grads):
    c = constants(q.shape[1])
    up = up_ref[...]
    rows = rows_ref[...]
    mask, ones = c["mask"], c["ones"]
    cat = lambda *parts: jnp.concatenate(parts, axis=0)
    column = lambda x: jnp.sum(x, axis=0, keepdims=True)

    @pl.when(pl.program_id(0) == 0)
    def _():
        row_grads[...] = jnp.zeros_like(row_grads)
        up_grads[...] = jnp.zeros_like(up_grads)

    zero = jnp.zeros((SPAN, mask.shape[0]), f32)
    rank, gate_at = low_parts(up.shape[0])
    lane = lax.broadcasted_iota(jnp.int32, (SPAN, up.shape[0]), 1)
    low_row = lax.broadcasted_iota(jnp.int32, up_grads.shape, 0)
    for i in range(per):
        at = slice(i * SPAN, (i + 1) * SPAN)
        q_here, kp_here, v_here = q[at, :], kp[at, :], v[at, :]
        e = ready(q_here, kp_here, din[at, :], rin[at, :], rows, c)
        start, end, pushed, d_read = starts[at, :], ends[at, :], push_ref[at, :], d_out[at, :]
        grad_end = adds[at, :] + times(grad_in[...], maps[at, :], mask, 0)
        grown = grad_end * e["last"]
        by_state = times(cat(e["K"], e["R"]), grown, mask, 1)
        d_push = -fold(cross(qr_ref[at, :], d_read), mask) - by_state[SPAN:]
        d_rhs = fold(cross(inv_ref[at, :], d_push), mask)
        d_value = (
            by_state[:SPAN]
            + fold(cross(cat(qk_ref[at, :], uk_ref[at, :]), cat(d_read, d_rhs)), mask)
        )
        both = cat(d_rhs, d_read)
        by_value = times(both, v_here, mask, 1)
        by_push = times(both, pushed, mask, 1)
        d_key_pairs = cat(
            jnp.where(c["strict"], by_value[:SPAN], zero), jnp.where(c["incl"], by_value[SPAN:], zero)
        )
        d_removal_pairs = cat(
            jnp.where(c["strict"], -by_push[:SPAN], zero), jnp.where(c["incl"], -by_push[SPAN:], zero)
        )
        d_queries = (
            times(both, start, mask, 0)
            + times(d_key_pairs, e["K"], mask, 0)
            + times(d_removal_pairs, e["R"], mask, 0)
        )
        by_grown = times(cat(v_here, -pushed), grown, mask, 0)
        queries = cat(e["U"], e["Q"])
        d_k_grown = by_grown[:SPAN] + fold(cross(d_key_pairs, queries), mask)
        d_r_grown = by_grown[SPAN:] + fold(cross(d_removal_pairs, queries), mask)
        d_u_grown, d_q_grown = d_queries[:SPAN], d_queries[SPAN:]
        on_unit = d_u_grown * e["U"]
        steps = d_q_grown * e["Q"] - d_k_grown * e["K"] - d_r_grown * e["R"] + on_unit
        d_log = exact_left(c["upper"], steps) - on_unit + column(grad_end * end)
        rate = e["rate"]
        d_k = d_k_grown * e["down"] + dk_post[at, :]
        d_removal = d_r_grown * e["down"]
        d_unit = d_u_grown * e["before"] + d_removal * rate
        d_rate_value = d_removal * e["unit"] + d_k * kp_here * rows[3:4]
        d_scaled = e["inv"] * (d_unit - e["unit"] * head_sum(d_unit * e["unit"], ones))
        d_rate = d_rate_value * rate * (1.0 - rate)
        d_decay = d_log * e["log_decay"] * (1.0 - e["sig"])
        dq_ref[at, :] = (d_q_grown * e["up"] + dq_post[at, :]).astype(bf16)
        dkp_ref[at, :] = (d_k * (1.0 + (rate - 1.0) * rows[3:4]) + d_scaled * rows[2:3]).astype(bf16)
        dv_ref[at, :] = (d_value + dv_post[at, :]).astype(bf16)
        lat = lat_ref[at, :]
        low = lat.astype(bf16)
        d_outs = (d_decay.astype(bf16), d_rate.astype(bf16), d_gate_ref[at, :])
        pick = lambda where, parts: jnp.where(
            where < rank, parts[0], jnp.where(where < gate_at, parts[1], parts[2])
        )
        slope = pick(lane, (1.0 - lat * lat, jnp.ones_like(lat), lat * (1.0 - lat)))
        pre = pick(lane, [dot(x, up, 1, 1) for x in d_outs]) * slope
        pre_ref[at, :] = pre.astype(bf16)
        up_grads[...] += pick(low_row, [dot(low, x, 0, 0) for x in d_outs])
        row_grads[0:1, :] += column(d_decay)
        row_grads[1:2, :] += column(d_rate)
        row_grads[2:3, :] += column(d_scaled * kp_here)
        row_grads[3:4, :] += column(d_k * kp_here * (rate - 1.0))


def run_blocks(kernel, ins, outs, scratch, tokens, reverse=False):
    count = tokens // SPAN
    per = blocks_per_step(count)
    steps = count // per

    def spec(shape, cut):
        if not cut:
            return pl.BlockSpec(shape, lambda i: (0, 0))
        rows = shape[0] // steps
        if reverse:
            return pl.BlockSpec((rows, shape[1]), lambda i: (steps - 1 - i, 0))
        return pl.BlockSpec((rows, shape[1]), lambda i: (i, 0))

    return pl.pallas_call(
        functools.partial(kernel, per),
        grid=(steps,),
        in_specs=[spec(x.shape, cut) for x, cut in ins],
        out_specs=[spec(shape, cut) for shape, _, cut in outs],
        out_shape=[jax.ShapeDtypeStruct(shape, kind) for shape, kind, _ in outs],
        scratch_shapes=[pltpu.VMEM(shape, f32) for shape in scratch],
        compiler_params=pltpu.CompilerParams(dimension_semantics=("arbitrary",)),
        cost_estimate=pl.CostEstimate(flops=10**10, bytes_accessed=2 * 10**7, transcendentals=0),
    )(*[x for x, _ in ins])


def low_parts(width):
    return width // 4, width // 2


def mixed(unit, edge, norms, count):
    first = unit * norms[0:1] + norms[1:2]
    before = (edge[0:1] * norms[0:1] + norms[1:2]) * edge[1:2]
    row = lax.broadcasted_iota(jnp.int32, first.shape, 0)
    diff = jnp.where(row == 0, before, pltpu.roll(first, 1, 0)) - first
    return diff, [(first + diff * norms[4 + i : 5 + i]).astype(bf16) for i in range(count)]


def slab_weights(gathered, width):
    parts, rows, _ = gathered.shape
    part = rows // 4
    piece = lambda i, w: jnp.concatenate(
        [gathered[j, i * part : (i + 1) * part, :w] for j in range(parts)], axis=0
    )
    return [piece(i, width) for i in range(3)] + [piece(3, gathered.shape[2])]


def project_kernel(unit, edge, norms, gathered, up, q, kp, v, din, rin, gate, lat, low_total):
    width = q.shape[1]
    step = pl.program_id(0)
    norms_here = norms[...]
    _, mixes = mixed(unit[...], edge[...], norms_here, 6)
    w_q, w_k, w_v, w_low = slab_weights(gathered, width)
    low_width = w_low.shape[1]
    rank, gate_at = low_parts(low_width)
    lane = lax.broadcasted_iota(jnp.int32, low_total.shape, 1)
    low = jnp.where(
        lane < rank,
        dot(mixes[1], w_low, 1, 0),
        jnp.where(lane < gate_at, dot(mixes[4], w_low, 1, 0), dot(mixes[5], w_low, 1, 0)),
    )

    @pl.when(step == 0)
    def _():
        q[...] = dot(mixes[0], w_q, 1, 0)
        kp[...] = dot(mixes[2], w_k, 1, 0)
        v[...] = dot(mixes[3], w_v, 1, 0)
        low_total[...] = low

    @pl.when(step > 0)
    def _():
        q[...] += dot(mixes[0], w_q, 1, 0)
        kp[...] += dot(mixes[2], w_k, 1, 0)
        v[...] += dot(mixes[3], w_v, 1, 0)
        low_total[...] += low

    @pl.when(step == pl.num_programs(0) - 1)
    def _():
        total = low_total[...]
        lats = jnp.where(
            lane < rank, jnp.tanh(total), jnp.where(lane < gate_at, total, jax.nn.sigmoid(total))
        )
        lat[...] = lats
        zero = jnp.zeros_like(lats)
        chosen = lambda where: jnp.where(where, lats, zero).astype(bf16)
        din[...] = dot(chosen(lane < rank), up[...], 1, 0)
        rin[...] = dot(chosen((lane >= rank) & (lane < gate_at)), up[...], 1, 0)
        gate[...] = dot(chosen(lane >= gate_at), up[...], 1, 0)


def unproject_kernel(here, unit, edge, scales, norms, gathered, dq, dkp, dv, pre, d_mid, packed,
                     feature, edge_fix, *rest):
    pieces, (all_first, all_unit) = rest[:-2], rest[-2:]
    width = dq.shape[1]
    step = pl.program_id(0)
    n = norms[...]
    edge_here = edge[...]
    unit_here = unit[...]
    diff, mixes = mixed(unit_here, edge_here, n, 6)
    weights = slab_weights(gathered, width)
    w_low = weights[3]
    slab, low_width = w_low.shape
    rank, gate_at = low_parts(low_width)
    pre_here = pre[...]
    lane = lax.broadcasted_iota(jnp.int32, pre_here.shape, 1)
    none = jnp.zeros_like(pre_here)
    pres = [
        jnp.where(lane < rank, pre_here, none),
        jnp.where((lane >= rank) & (lane < gate_at), pre_here, none),
        jnp.where(lane >= gate_at, pre_here, none),
    ]
    sources = [(0, dq[...], 0), (2, dkp[...], 1), (3, dv[...], 2), (1, pres[0], 3), (4, pres[1], 3),
               (5, pres[2], 3)]
    low_lane = lax.broadcasted_iota(jnp.int32, (slab, low_width), 1)
    column = lambda x: jnp.sum(x, axis=0, keepdims=True)
    parts = gathered.shape[0]
    part = slab // parts
    direct = shifted = None
    low_grad = None
    for mix, grad, which in sources:
        weight_grad = dot(mixes[mix], grad, 0, 0)
        if which < 3:
            for j in range(parts):
                packed[j, which * part : (which + 1) * part, :width] = weight_grad[
                    j * part : (j + 1) * part
                ].astype(bf16)
                if width < low_width:
                    packed[j, which * part : (which + 1) * part, width:] = jnp.zeros(
                        (part, low_width - width), bf16
                    )
        else:
            low_grad = weight_grad if low_grad is None else low_grad + weight_grad
        d_mix = dot(grad, weights[which], 1, 1)
        feature[4 + mix : 5 + mix, :] = column(d_mix * diff)
        to_shift = d_mix * n[4 + mix : 5 + mix]
        shifted = to_shift if shifted is None else shifted + to_shift
        direct = d_mix - to_shift if direct is None else direct + (d_mix - to_shift)
    for j in range(parts):
        packed[j, 3 * part : 4 * part, :] = low_grad[j * part : (j + 1) * part].astype(bf16)
    tokens = unit_here.shape[0]
    row = lax.broadcasted_iota(jnp.int32, shifted.shape, 0)
    d_first = direct + jnp.where(row == tokens - 1, 0.0, pltpu.roll(shifted, tokens - 1, 0))
    before = shifted[0:1] * edge_here[1:2]
    feature[0:1, :] = column(d_first * unit_here) + before * edge_here[0:1]
    feature[1:2, :] = column(d_first) + before
    feature[2:4, :] = jnp.zeros_like(feature[2:4, :])
    feature[10:, :] = jnp.zeros_like(feature[10:, :])
    at = pl.ds(pl.multiple_of(step * slab, slab), slab)
    all_first[:tokens, at] = d_first * n[0:1]
    all_first[tokens:, at] = jnp.broadcast_to(before * n[0:1], (8, slab))
    all_unit[:tokens, at] = unit_here
    all_unit[tokens:, at] = jnp.broadcast_to(edge_here[0:1], (8, slab))

    @pl.when(step == pl.num_programs(0) - 1)
    def _():
        d_unit = all_first[...]
        units = all_unit[...]
        features = d_unit.shape[1]
        mean = jnp.sum(d_unit, axis=1, keepdims=True) * (1.0 / features)
        along = jnp.sum(d_unit * units, axis=1, keepdims=True) * (1.0 / features)
        result = scales[...] * (d_unit - mean - units * along)
        edge_fix[...] = result[tokens:] + d_mid[tokens + EDGE - 8 :, :]
        all_first[:tokens, :] = result[:tokens] + d_mid[:tokens, :]
        send_pieces(pieces, all_first, here[0])


EDGE = 16


def share_of(here, by, devices, size):
    return pl.ds(pl.multiple_of(lax.rem(here + by + devices, devices) * size, size), size)


def send_pieces(pieces, whole, here):
    share = pieces[0].shape[0]
    for by, piece in enumerate(pieces):
        piece[...] = whole[share_of(here, by, len(pieces), share), :].astype(piece.dtype)


def channel_kernel(devices, *refs):
    here, stream, edge_stream, has_edge, cot, norms, out_full, key, value = refs[:9]
    gated, edges = refs[9 : 9 + devices], refs[9 + devices : 9 + 2 * devices]
    refs = refs[9 + 2 * devices :]
    ffn_in, hidden, d_pre, cot_low, d_mid_low, d_mid, feature, middle_share = refs[:8]
    ffn_pieces, refs = refs[8 : 8 + devices], refs[8 + devices :]
    grad_pieces, refs = refs[:devices], refs[devices:]
    fix_pieces, refs = refs[:devices], refs[devices:]
    middle, unit, scale, diff, d_ffn, ffn_out = refs
    step = pl.program_id(0)
    tokens, features = stream.shape
    width = gated[0].shape[1]
    n = norms[...]
    flag = has_edge[0:1, 0:1]
    row = lax.broadcasted_iota(jnp.int32, (tokens + EDGE, features), 0)

    @pl.when(step == 0)
    def _():
        middle[:tokens, :] = stream[...]
        middle[tokens:, :] = edge_stream[...]
        for by in range(devices):
            rows = out_full[share_of(here[0], -by, devices, width), :]
            middle[:tokens, :] += dot(gated[by][...], rows, 1, 0)
            middle[tokens:, :] += dot(edges[by][...], rows, 1, 0)
        middle_share[...] = middle[share_of(here[0], 0, devices, tokens // devices), :]
        values = middle[...]
        center = values - jnp.sum(values, axis=1, keepdims=True) * (1.0 / features)
        spread_here = jnp.sum(center * center, axis=1, keepdims=True) * (1.0 / features)
        scale_here = lax.rsqrt(spread_here + 1e-05)
        unit_here = center * scale_here
        unit[...] = unit_here
        scale[...] = scale_here
        norm = unit_here * n[2:3] + n[3:4]
        before = pltpu.roll(norm, 1, 0)
        diff_here = jnp.where(row == 0, before * flag, before) - norm
        diff[...] = diff_here
        ffn_in[...] = (norm + diff_here * n[10:11])[:tokens].astype(bf16)
        cot_low[...] = cot[...].astype(bf16)
        d_ffn[...] = jnp.zeros_like(d_ffn)
        ffn_out[...] = jnp.zeros_like(ffn_out)

    act = jnp.maximum(dot(ffn_in[...], key[...], 1, 0), 0.0)
    hidden_here = (act * act).astype(bf16)
    hidden[...] = hidden_here
    d_pre_here = (dot(cot_low[...], value[...], 1, 1) * 2.0 * act).astype(bf16)
    d_pre[...] = d_pre_here
    d_ffn[:tokens, :] += dot(d_pre_here, key[...], 1, 1)
    ffn_out[...] += dot(hidden_here, value[...], 1, 0)

    @pl.when(step == pl.num_programs(0) - 1)
    def _():
        send_pieces(ffn_pieces, ffn_out, here[0])
        grad = d_ffn[...]
        to_shift = grad * n[10:11]
        moved = pltpu.roll(to_shift, tokens + EDGE - 1, 0)
        d_second = grad - to_shift + jnp.where(row == tokens + EDGE - 1, moved * flag, moved)
        unit_here = unit[...]
        column = lambda x: jnp.sum(x, axis=0, keepdims=True)
        feature[...] = jnp.zeros_like(feature)
        feature[0:1, :] = column(d_second * unit_here)
        feature[1:2, :] = column(d_second)
        feature[2:3, :] = column(grad * diff[...])
        d_unit = d_second * n[2:3]
        mean = jnp.sum(d_unit, axis=1, keepdims=True) * (1.0 / features)
        along = jnp.sum(d_unit * unit_here, axis=1, keepdims=True) * (1.0 / features)
        d_mid_here = scale[...] * (d_unit - mean - unit_here * along)
        d_mid[...] = d_mid_here
        d_mid_low[tokens:, :] = d_mid_here[tokens:].astype(bf16)
        d_mid_low[:tokens, :] = (d_mid_here[:tokens] + cot[...] * (1.0 / devices)).astype(bf16)
        for by in range(devices):
            rows = out_full[share_of(here[0], by, devices, width), :]
            grad_pieces[by][...] = dot(d_mid_low[:tokens, :], rows, 1, 1).astype(bf16)
            fix_pieces[by][...] = dot(d_mid_low[tokens:, :], rows, 1, 1).astype(bf16)


def large_kernel(devices, *refs):
    here, hidden, cot_low, ffn_in, d_pre, d_mid_low = refs[:6]
    gated, edges, large = refs[6 : 6 + devices], refs[6 + devices : 6 + 2 * devices], refs[-1]
    tokens, hidden_here = hidden.shape
    part = large.shape[2]
    width = gated[0].shape[1]
    large[0, :hidden_here, :] = dot(hidden[...], cot_low[...], 0, 0).astype(bf16)
    key_grad = dot(ffn_in[...], d_pre[...], 0, 0).astype(bf16)
    for j in range(hidden_here // part):
        at = hidden_here + j * part
        large[0, at : at + part, :] = key_grad[:, j * part : (j + 1) * part]
    grad, grad_edge = d_mid_low[:tokens, :], d_mid_low[tokens:, :]
    for by in range(devices):
        rows = dot(gated[by][...], grad, 0, 0) + dot(edges[by][...], grad_edge, 0, 0)
        at = lax.rem(here[0] - by + devices, devices) * width + 2 * hidden_here
        large[0, pl.ds(pl.multiple_of(at, width), width), :] = rows.astype(bf16)


def run_slabs(kernel, ins, outs, scratch, slabs):
    def spec(shape, cut):
        shape = tuple(shape)
        if cut == "scalar":
            return pl.BlockSpec(memory_space=pltpu.SMEM)
        if cut is None:
            return pl.BlockSpec(shape, lambda i: (0,) * len(shape))
        dim, size = cut
        block = list(shape)
        block[dim] = shape[dim] // slabs
        if size is not None:
            block[size[0]] = size[1]
        return pl.BlockSpec(tuple(block), lambda i: tuple(i if k == dim else 0 for k in range(len(shape))))

    return pl.pallas_call(
        kernel,
        grid=(slabs,),
        in_specs=[spec(x.shape, cut) for x, cut in ins],
        out_specs=[spec(shape, cut) for shape, _, cut in outs],
        out_shape=[jax.ShapeDtypeStruct(shape, kind) for shape, kind, _ in outs],
        scratch_shapes=[pltpu.VMEM(shape, f32) for shape in scratch],
        compiler_params=pltpu.CompilerParams(dimension_semantics=("arbitrary",)),
        cost_estimate=pl.CostEstimate(flops=10**10, bytes_accessed=2 * 10**7, transcendentals=0),
    )(*[x for x, _ in ins])


def to_next(x, axis, by):
    devices = lax.axis_size(axis)
    pairs_here = [(i, i + by) for i in range(devices) if 0 <= i + by < devices]
    return lax.ppermute(x, axis, pairs_here)


def around(x, by):
    devices = lax.axis_size("mp")
    return lax.ppermute(x, "mp", [(i, (i + by) % devices) for i in range(devices)])


def slanted(x, along, by):
    rows, devices = lax.axis_size("seq"), lax.axis_size("mp")
    pairs_here = [
        (s * devices + i, (s + along) * devices + (i + by) % devices)
        for s in range(rows)
        if 0 <= s + along < rows
        for i in range(devices)
    ]
    return lax.ppermute(x, ("seq", "mp"), pairs_here)


def gather_shares(x):
    devices = lax.axis_size("mp")
    came = [x] + [around(x, by) for by in range(1, devices)]
    turned = jnp.stack([came[-k % devices] for k in range(devices)] * 2)
    at = (devices - lax.axis_index("mp")) % devices
    return lax.dynamic_slice_in_dim(turned, at, devices, 0)


def scatter_shares(x):
    devices = lax.axis_size("mp")
    here = lax.axis_index("mp")
    term = lambda at: lax.dynamic_index_in_dim(x, at % devices, 0, keepdims=False)
    total = term(here).astype(f32)
    for by in range(1, devices):
        total = total + around(term(here + by), by).astype(f32)
    return total


def mm_left(a, b):
    return dot(a, b, 0, 0)


def statistics(values):
    center = values - jnp.mean(values, axis=-1, keepdims=True)
    scale = lax.rsqrt(jnp.mean(center * center, axis=-1, keepdims=True) + 1e-05)
    return center * scale, scale


def carry_states(state_map, state_add, by):
    entering = to_next(state_add.astype(bf16), "seq", by).astype(f32)
    heads = state_map.shape[1] // SPAN
    apart = lambda x: x.reshape(SPAN, heads, SPAN).transpose(1, 0, 2)
    for _ in range(lax.axis_size("seq") - 2):
        moved = jnp.einsum("hij,hjl->hil", apart(entering), apart(state_map), precision="highest")
        passed = moved.transpose(1, 0, 2).reshape(state_add.shape) + state_add
        entering = to_next(passed.astype(bf16), "seq", by).astype(f32)
    return entering


def wide(x, width):
    return jnp.pad(x, ((0, 0), (0, width - x.shape[1])))


def body(inputs, rkv_weight, output_weight, first_factors, second_factors, gate_first, gate_second,
         key_weight, value_weight, head_table, feature_table, cotangent):
    group = ("dp", "seq")
    count = lax.axis_size("dp") * lax.axis_size("seq")
    mp = lax.axis_size("mp")
    mp_here = lax.axis_index("mp")
    stream = inputs[0]
    cot = cotangent[0]
    tokens, features = stream.shape
    share = tokens // mp
    share_at = mp_here * share
    part = features // count
    width = rkv_weight.shape[2]
    heads = width // SPAN
    rank, gate_rank = first_factors.shape[2], gate_first.shape[1]
    low_width = 2 * rank + gate_rank
    lanes = max(width, low_width, part)
    up_rows = second_factors.shape[1]
    head_part = head_table.shape[2]
    here = mp_here.astype(jnp.int32).reshape(1)
    edge_stream = to_next(stream[-EDGE:], "seq", 1)
    edge_row = edge_stream[EDGE - 1 :]
    pieces = [
        wide(rkv_weight.reshape(3 * part, width), lanes),
        wide(jnp.concatenate([first_factors[0], first_factors[1], gate_first], axis=1), lanes),
        wide(second_factors.reshape(2 * up_rows, width), lanes),
        wide(gate_second, lanes),
        wide(feature_table, lanes),
        wide(head_table.reshape(7, heads * head_part), lanes),
    ]
    edges = [0]
    for piece in pieces:
        edges.append(edges[-1] + piece.shape[0])
    packed = jnp.concatenate(pieces, axis=0)
    rows_full = -(-packed.shape[0] // 16) * 16
    packed = jnp.pad(packed, ((0, rows_full - packed.shape[0]), (0, 0)))
    gathered = lax.all_gather(packed, group, axis=0, tiled=False)
    cut = lambda i, w: gathered[:, edges[i] : edges[i + 1], :w]
    up = cut(2, width).reshape(count, 2, up_rows, width).transpose(1, 0, 2, 3)
    up = jnp.concatenate(
        [up.reshape(2 * rank, width), cut(3, width).reshape(gate_rank, width)], axis=0
    )
    norms = cut(4, part).transpose(1, 0, 2).reshape(11, features).astype(f32)
    norms = jnp.pad(norms, ((0, 5), (0, 0)))
    head_rows = (
        cut(5, heads * head_part)
        .reshape(count, 7, heads, head_part)
        .transpose(1, 2, 0, 3)
        .reshape(7, width)
        .astype(f32)
    )
    head_rows = jnp.pad(head_rows, ((0, 1), (0, 0)))

    out_column = gather_shares(output_weight).reshape(features, part)
    rest = lax.all_gather(
        jnp.concatenate([value_weight, out_column], axis=0), group, axis=0, tiled=False
    )
    hidden_here = value_weight.shape[0]
    key_full = lax.all_gather(key_weight, group, axis=0, tiled=True)

    unit_one, scale_one = statistics(stream)
    edge_unit, edge_scale = statistics(edge_row)
    has_edge = (lax.axis_index("seq") > 0).astype(f32)
    edge = jnp.concatenate(
        [edge_unit, jnp.broadcast_to(has_edge, (1, features)), jnp.zeros((6, features), f32)]
    )
    slab = max(256, part)
    slabs = features // slab
    in_slabs = (1, None)
    of_gathered = (0, (1, 4 * part))
    whole = (tokens, width)
    q, kp, v, din, rin, gate, lat = run_slabs(
        project_kernel,
        [(unit_one, in_slabs), (edge, in_slabs), (norms, in_slabs), (gathered, of_gathered), (up, None)],
        [(whole, f32, None)] * 6 + [((tokens, low_width), f32, None)],
        [(tokens, low_width)],
        slabs,
    )

    state = (SPAN, width)
    (local_out, read, push_map, push, inv, uk, qk, qr, carry, maps, adds, map_end, add_end) = run_blocks(
        local_kernel,
        [(q, True), (kp, True), (v, True), (din, True), (rin, True), (head_rows, False)],
        [(whole, f32, True)] * 4
        + [(whole, bf16, True)] * 4
        + [((tokens // SPAN * width, width), bf16, True)]
        + [(whole, f32, True)] * 2
        + [(state, f32, False)] * 2,
        [state, state],
        tokens,
    )
    entering = carry_states(map_end, add_end, 1)
    gated, read_out, pushed, starts, ends = run_blocks(
        finish_kernel,
        [(x, True) for x in (q, kp, v, rin, gate)]
        + [(head_rows, False)]
        + [(x, True) for x in (local_out, read, push_map, push, maps, adds)]
        + [(entering, False)],
        [(whole, bf16, True)] + [(whole, f32, True)] * 4,
        [state],
        tokens,
    )

    edge_parts = [slanted(gated[-EDGE:], 1, by) for by in range(mp)]
    gated_parts = [gated] + [around(gated, by) for by in range(1, mp)]
    value_full = rest[:, :hidden_here].transpose(1, 0, 2).reshape(hidden_here, features)
    out_full = rest[:, hidden_here:].transpose(1, 0, 2).reshape(features, features)
    longer = tokens + EDGE
    lots = key_full.shape[1] // part
    channel = run_slabs(
        functools.partial(channel_kernel, mp),
        [(here, "scalar"), (stream, None), (edge_stream, None), (edge[1:2, :128], None), (cot, None)]
        + [(norms, None), (out_full, None), (key_full, (1, None)), (value_full, (0, None))]
        + [(x, None) for x in gated_parts + edge_parts],
        [
            ((tokens, features), bf16, None),
            ((tokens, hidden_here), bf16, (1, None)),
            ((tokens, hidden_here), bf16, (1, None)),
            ((tokens, features), bf16, None),
            ((longer, features), bf16, None),
            ((longer, features), f32, None),
            ((8, features), f32, None),
            ((share, features), f32, None),
        ]
        + [((share, features), bf16, None)] * mp
        + [(whole, bf16, None)] * mp
        + [((EDGE, width), bf16, None)] * mp,
        [(longer, features)] * 2
        + [(longer, 1)]
        + [(longer, features)] * 2
        + [(tokens, features)],
        max(1, hidden_here // 256),
    )
    ffn_in, hidden, d_pre, cot_low, d_mid_low, d_mid, second_rows, middle_share = channel[:8]
    ffn_pieces = channel[8 : 8 + mp]
    grad_pieces = channel[8 + mp : 8 + 2 * mp]
    fix_pieces = channel[8 + 2 * mp :]
    fixes = [slanted(fix_pieces[by], -1, by) for by in range(mp)]
    d_gated = [grad_pieces[0]]
    for by in range(1, mp):
        d_gated.append(around(grad_pieces[by], by))

    if part % 128 == 0:
        large = run_slabs(
            functools.partial(large_kernel, mp),
            [(here, "scalar"), (hidden, None), (cot_low, (1, None)), (ffn_in, (1, None)), (d_pre, None)]
            + [(d_mid_low, (1, None))]
            + [(x, None) for x in gated_parts + edge_parts],
            [((count, 2 * hidden_here + features, part), bf16, (0, None))],
            [],
            count,
        )[0]
    else:
        by_part = lambda x: x.astype(bf16).reshape(x.shape[0], count, part).transpose(1, 0, 2)
        key_grad = mm_left(ffn_in, d_pre).astype(bf16)
        key_grad = key_grad.reshape(count, part, lots, part).transpose(0, 2, 1, 3)
        order = lambda parts: jnp.concatenate(parts[:1] + parts[:0:-1], axis=0)
        out_rows = order([mm_left(x, d_mid_low[:tokens]) for x in gated_parts]) + order(
            [mm_left(x, d_mid_low[tokens:]) for x in edge_parts]
        )
        large = jnp.concatenate(
            [
                by_part(mm_left(hidden, cot_low)),
                key_grad.reshape(count, lots * part, part),
                by_part(jnp.roll(out_rows, mp_here * width, axis=0)),
            ],
            axis=1,
        )
    large = lax.psum_scatter(large, group, scatter_dimension=0, tiled=False)
    d_gated, ffn_pieces = lax.optimization_barrier((d_gated, ffn_pieces))
    block_out = middle_share + ffn_pieces[0].astype(f32)
    for by in range(1, mp):
        came = around(ffn_pieces[by], by)
        block_out = block_out + came.astype(f32)

    (d_read, dq_post, dk_post, dv_post, d_gate, back_maps, back_adds, back_map_end, back_add_end,
     row_grads_post) = run_blocks(
        functools.partial(reads_kernel, mp),
        [(x, True) for x in (q, kp, v, rin, gate)]
        + [(head_rows, False)]
        + [(x, True) for x in (read_out, read, carry)]
        + [(x, True) for x in d_gated]
        + [(x, False) for x in fixes],
        [(whole, f32, True)] * 4
        + [(whole, bf16, True)]
        + [(whole, f32, True)] * 2
        + [(state, f32, False)] * 2
        + [((8, width), f32, False)],
        [state, state],
        tokens,
        reverse=True,
    )
    grad_in = carry_states(back_map_end, back_add_end, -1)
    dq, dkp, dv, pre, row_grads, up_grads = run_blocks(
        grads_kernel,
        [(x, True) for x in (q, kp, v, din, rin, lat, d_gate)]
        + [(head_rows, False), (up, False)]
        + [
            (x, True)
            for x in (pushed, inv, uk, qk, qr, starts, ends, d_read, dq_post, dk_post, dv_post,
                      back_maps, back_adds)
        ]
        + [(grad_in, False)],
        [(whole, bf16, True)] * 3
        + [((tokens, low_width), bf16, True), ((8, width), f32, False)]
        + [((low_width, width), f32, False)],
        [],
        tokens,
    )
    row_grads = jnp.concatenate([row_grads[:4], row_grads_post[4:7]], axis=0)

    scales = jnp.concatenate([scale_one, jnp.broadcast_to(edge_scale, (8, 1))], axis=0)
    unprojected = run_slabs(
        unproject_kernel,
        [(here, "scalar"), (unit_one, in_slabs), (edge, in_slabs), (scales, None), (norms, in_slabs)]
        + [(gathered, of_gathered), (dq, None), (dkp, None), (dv, None), (pre, None), (d_mid, None)],
        [
            ((count, 4 * part, lanes), bf16, (0, None)),
            ((16, features), f32, in_slabs),
            ((8, features), f32, None),
        ]
        + [((share, features), bf16, None)] * mp,
        [(tokens + 8, features)] * 2,
        slabs,
    )
    packed, feature_grad, edge_fix = unprojected[:3]
    stream_pieces = unprojected[3:]
    fix = to_next(edge_fix[7:].astype(bf16), "seq", -1)

    feature_grad = jnp.concatenate(
        [feature_grad[:2], second_rows[:2], feature_grad[4:10], second_rows[2:3]]
    )
    split_rows = lambda x: x.reshape(count, x.shape[0] // count, x.shape[1])
    wider = lambda x: jnp.pad(x.astype(bf16), ((0, 0), (0, 0), (0, lanes - x.shape[2])))
    grads = [
        split_rows(up_grads[:rank]),
        split_rows(up_grads[rank : 2 * rank]),
        split_rows(up_grads[2 * rank :]),
        feature_grad.reshape(11, count, part).transpose(1, 0, 2),
        row_grads.reshape(7, heads, count, head_part)
        .transpose(2, 0, 1, 3)
        .reshape(count, 7, heads * head_part),
    ]
    grads = jnp.concatenate([wider(x) for x in grads], axis=1)
    grads = jnp.pad(grads, ((0, 0), (0, rows_full - 4 * part - grads.shape[1]), (0, 0)))
    grads = jnp.concatenate([packed, grads], axis=1)
    grads, large = lax.optimization_barrier((grads, large))
    out_grad = scatter_shares(large[hidden_here + lots * part :].reshape(mp, width, part))
    value_grad = large[:hidden_here].astype(f32)
    key_grad = large[hidden_here : hidden_here + lots * part].reshape(lots, part, part)
    key_grad = key_grad.transpose(1, 0, 2).reshape(part, lots * part).astype(f32)
    summed = lax.psum_scatter(grads, group, scatter_dimension=0, tiled=False)
    input_grad = lax.dynamic_slice_in_dim(cot, share_at, share, 0) + sum(
        [stream_pieces[0].astype(f32)]
        + [around(stream_pieces[by], by).astype(f32) for by in range(1, mp)]
    )
    summed, input_grad, out_grad, block_out = lax.optimization_barrier(
        (summed, input_grad, out_grad, block_out)
    )
    own = lambda i, w: summed[edges[i] : edges[i + 1], :w].astype(f32)
    fix_rows = features // lanes
    everywhere = jnp.concatenate(
        [summed[edges[1] : edges[2]], summed[edges[4] : edges[5]], fix.reshape(fix_rows, lanes)],
        axis=0,
    )
    everywhere = jnp.sum(gather_shares(everywhere).astype(f32), axis=0)
    down_sum = everywhere[:part]
    fix = everywhere[part + 11 :].reshape(1, features)
    last = lax.broadcasted_iota(jnp.int32, (share, 1), 0) == share - 1
    input_grad = input_grad + jnp.where(last & (mp_here == mp - 1), fix, 0.0)
    return (
        block_out[None],
        input_grad[None],
        own(0, width).reshape(3, part, width),
        out_grad,
        jnp.stack([down_sum[:, :rank], down_sum[:, rank : 2 * rank]]),
        own(2, width).reshape(2, up_rows, width),
        down_sum[:, 2 * rank : low_width],
        own(3, width),
        key_grad,
        value_grad,
        own(5, heads * head_part).reshape(7, heads, head_part),
        everywhere[part : part + 11, :part],
    )


def solution(mesh):
    both = ("dp", "seq")
    return jax.shard_map(
        body,
        mesh=mesh,
        in_specs=(
            P("dp", "seq", None),
            P(None, both, "mp"),
            P("mp", both),
            P(None, both, None),
            P(None, both, "mp"),
            P(both, None),
            P(both, "mp"),
            P(both, "mp"),
            P("mp", both),
            P(None, "mp", both),
            P(None, both),
            P("dp", "seq", None),
        ),
        out_specs=(
            P("dp", ("seq", "mp"), None),
            P("dp", ("seq", "mp"), None),
            P(None, both, "mp"),
            P("mp", both),
            P(None, both, None),
            P(None, both, "mp"),
            P(both, None),
            P(both, "mp"),
            P(both, "mp"),
            P("mp", both),
            P(None, "mp", both),
            P(None, both),
        ),
        check_vma=False,
    )
```

```python
import functools

import jax
import jax.numpy as jnp
from jax import lax
from jax.experimental import pallas as pl
from jax.experimental.pallas import tpu as pltpu
from jax.sharding import PartitionSpec as P


SPAN = 64
f32 = jnp.float32
bf16 = jnp.bfloat16


def halves(x):
    high = x.astype(bf16)
    return high, (x - high.astype(f32)).astype(bf16)


def dot(a, b, ca, cb):
    return lax.dot_general(a, b, (((ca,), (cb,)), ((), ())), preferred_element_type=f32)


def spread(x, mask):
    tiled = jnp.concatenate([x] * (x.shape[1] // SPAN), axis=0)
    return jnp.where(mask, tiled, jnp.zeros_like(tiled))


def fold(x, mask):
    x = jnp.where(mask, x, jnp.zeros_like(x))
    return sum(x[i * SPAN : (i + 1) * SPAN] for i in range(x.shape[0] // SPAN))


def times(a, b, mask, cb):
    return dot(a.astype(bf16), spread(b.astype(bf16), mask), 1, cb)


def fine(a, b, mask, cb):
    ah, al = halves(a)
    bh, bl = halves(b)
    rows = a.shape[0]
    both = dot(jnp.concatenate([ah, al], axis=0), spread(bh, mask), 1, cb)
    return both[:rows] + both[rows:] + dot(ah, spread(bl, mask), 1, cb)


def cross(a, b):
    return dot(a.astype(bf16), b.astype(bf16), 0, 0)


def fine_cross(a, b):
    ah, al = halves(a)
    bh, bl = halves(b)
    return dot(
        jnp.concatenate([ah, al, ah], axis=0), jnp.concatenate([bh, bh, bl], axis=0), 0, 0
    )


def exact_left(ones, x):
    high = x.astype(bf16)
    rest = x - high.astype(f32)
    mid = rest.astype(bf16)
    low = (rest - mid.astype(f32)).astype(bf16)
    return dot(ones, high, 1, 0) + dot(ones, mid, 1, 0) + dot(ones, low, 1, 0)


def head_sum(x, ones):
    high, low = halves(x)
    rows = x.shape[0]
    both = dot(jnp.concatenate([high, low], axis=0), ones, 1, 0)
    return both[:rows] + both[rows:]


def constants(width):
    iota = lax.broadcasted_iota
    big_row = iota(jnp.int32, (width, width), 0)
    big_col = iota(jnp.int32, (width, width), 1)
    mask = (big_row // SPAN) == (big_col // SPAN)
    t = iota(jnp.int32, (SPAN, SPAN), 0)
    s = iota(jnp.int32, (SPAN, SPAN), 1)
    row = iota(jnp.int32, (SPAN, width), 0)
    col = iota(jnp.int32, (SPAN, width), 1) % SPAN
    one = lambda where: jnp.where(where, 1.0, 0.0).astype(f32)
    return dict(
        mask=mask,
        diagonal=one(big_row == big_col),
        ones=one(mask).astype(bf16),
        lower=one(t >= s).astype(bf16),
        upper=one(t <= s).astype(bf16),
        strict=row > col,
        incl=row >= col,
        eye=one(row == col),
        near=(row // 4 == col // 4) & (row > col),
        mid=(row // 16 == col // 16) & (row // 4 > col // 4),
        far=row // 16 > col // 16,
    )


def ready(q, kp, din, rin, rows, c):
    sig = jax.nn.sigmoid(rows[0:1] + din)
    log_decay = -0.6065306597126334 * sig
    rate = jax.nn.sigmoid(rows[1:2] + rin)
    scaled = kp * rows[2:3]
    inv = lax.rsqrt(head_sum(scaled * scaled, c["ones"]) + 1e-6)
    unit = scaled * inv
    removal = unit * rate
    total = exact_left(c["lower"], log_decay)
    up = jnp.exp(total)
    down = jnp.exp(-total)
    before = jnp.exp(total - log_decay)
    return dict(
        sig=sig,
        log_decay=log_decay,
        rate=rate,
        inv=inv,
        unit=unit,
        up=up,
        down=down,
        before=before,
        Q=q * up,
        U=unit * before,
        K=kp * (1.0 + (rate - 1.0) * rows[3:4]) * down,
        R=removal * down,
        last=up[SPAN - 1 : SPAN],
    )


def inverse(lower, c):
    mask = c["mask"]
    zero = jnp.zeros_like(lower)
    inner = jnp.where(c["near"], lower, zero)
    square = fine(inner, inner, mask, 0)
    out = c["eye"] - inner + square - fine(inner, square, mask, 0)
    for level in ("mid", "far"):
        step = fine(out, jnp.where(c[level], lower, zero), mask, 0)
        step_two = fine(step, step, mask, 0)
        first = out - fine(step, out, mask, 0)
        out = first + fine(step_two, first, mask, 0)
    return out


def pairs(e, c):
    mask = c["mask"]
    zero = jnp.zeros((SPAN, mask.shape[0]), f32)
    queries = jnp.concatenate([e["U"], e["Q"]], axis=0)
    by_key = fine(queries, e["K"], mask, 1)
    by_removal = fine(queries, e["R"], mask, 1)
    return (
        jnp.where(c["strict"], by_key[:SPAN], zero),
        jnp.where(c["incl"], by_key[SPAN:], zero),
        jnp.where(c["strict"], by_removal[:SPAN], zero),
        jnp.where(c["incl"], by_removal[SPAN:], zero),
    )


def blocks_per_step(count):
    return 2 if count % 2 == 0 else 1


def local_kernel(per, q, kp, v, din, rin, rows_ref, local_out, read, push_map, push, inv_out,
                 uk_out, qk_out, qr_out, carry, maps, adds, map_end, add_end, map_now, add_now):
    width = q.shape[1]
    c = constants(width)
    rows = rows_ref[...]

    @pl.when(pl.program_id(0) == 0)
    def _():
        map_now[...] = c["eye"]
        add_now[...] = jnp.zeros_like(add_now)

    chain = []
    for i in range(per):
        at = slice(i * SPAN, (i + 1) * SPAN)
        e = ready(q[at, :], kp[at, :], din[at, :], rin[at, :], rows, c)
        uk, qk, ur, qr = pairs(e, c)
        inv = inverse(ur, c)
        values = v[at, :]
        mixed = fine(jnp.concatenate([uk, qk], axis=0), values, c["mask"], 0)
        y = fine(inv, mixed[:SPAN], c["mask"], 0)
        w = fine(inv, e["U"], c["mask"], 0)
        local_out[at, :] = mixed[SPAN:] - fine(qr, y, c["mask"], 0)
        read[at, :] = e["Q"] - fine(qr, w, c["mask"], 0)
        push_map[at, :] = w
        push[at, :] = y
        inv_out[at, :] = inv.astype(bf16)
        uk_out[at, :] = uk.astype(bf16)
        qk_out[at, :] = qk.astype(bf16)
        qr_out[at, :] = qr.astype(bf16)
        carried = jnp.where(c["mask"], fine_cross(w, e["R"]), jnp.zeros_like(c["diagonal"]))
        carry_here = ((c["diagonal"] - carried) * e["last"]).astype(bf16)
        carry[i * width : (i + 1) * width, :] = carry_here
        added = fold(
            fine_cross(
                jnp.concatenate([values, y], axis=0), jnp.concatenate([e["K"], -e["R"]], axis=0)
            ),
            c["mask"],
        ) * e["last"]
        chain.append((at, carry_here, added))
    state_map, state_add = map_now[...], add_now[...]
    for at, carry_here, added in chain:
        both = dot(
            jnp.concatenate([state_map, state_add], axis=0).astype(bf16), carry_here, 1, 0
        )
        state_map, state_add = both[:SPAN], both[SPAN:] + added
        maps[at, :] = state_map
        adds[at, :] = state_add
    map_now[...] = state_map
    add_now[...] = state_add
    map_end[...] = state_map
    add_end[...] = state_add


def normed(out, q, k, v, rows, c):
    ones = c["ones"]
    center = out - head_sum(out, ones) * (1.0 / SPAN)
    spread_here = head_sum(center * center, ones) * (1.0 / SPAN)
    scale = lax.rsqrt(spread_here + 0.00064)
    unit = center * scale
    extra = head_sum(q * k * rows[4:5], ones)
    return unit, scale, extra, unit * rows[5:6] + rows[6:7] + extra * v


def finish_kernel(per, q, kp, v, rin, gate, rows_ref, local_out, read, push_map, push, maps, adds,
                  state_in, gated, out_ref, push_out, starts, ends, state_now):
    c = constants(q.shape[1])
    rows = rows_ref[...]
    mask = c["mask"]

    @pl.when(pl.program_id(0) == 0)
    def _():
        state_now[...] = state_in[...]

    entering = state_in[...]
    state = state_now[...]
    for i in range(per):
        at = slice(i * SPAN, (i + 1) * SPAN)
        starts[at, :] = state
        both = fine(jnp.concatenate([read[at, :], push_map[at, :]], axis=0), state, mask, 1)
        out = local_out[at, :] + both[:SPAN]
        push_out[at, :] = push[at, :] + both[SPAN:]
        out_ref[at, :] = out
        rate = jax.nn.sigmoid(rows[1:2] + rin[at, :])
        k = kp[at, :] * (1.0 + (rate - 1.0) * rows[3:4])
        _, _, _, summed = normed(out, q[at, :], k, v[at, :], rows, c)
        gated[at, :] = (summed * gate[at, :]).astype(bf16)
        state = adds[at, :] + times(entering, maps[at, :], mask, 0)
        ends[at, :] = state
    state_now[...] = state


def reads_kernel(devices, per, q, kp, v, rin, gate, rows_ref, out_ref, read, carry, *refs):
    d_gated, fixes, refs = refs[:devices], refs[devices : 2 * devices], refs[2 * devices :]
    d_out, dq_post, dk_post, dv_post, d_gate, maps, adds, map_end, add_end, row_grads = refs[:10]
    map_now, add_now = refs[10:]
    width = q.shape[1]
    first_step = (pl.program_id(0) == 0).astype(f32)
    fix = sum(x[...].astype(f32) for x in fixes)[EDGE - 1 : EDGE] * first_step
    last_row = lax.broadcasted_iota(jnp.int32, (SPAN, width), 0) == SPAN - 1
    c = constants(width)
    rows = rows_ref[...]
    ones = c["ones"]

    @pl.when(pl.program_id(0) == 0)
    def _():
        map_now[...] = c["eye"]
        add_now[...] = jnp.zeros_like(add_now)
        row_grads[...] = jnp.zeros_like(row_grads)

    state_map, state_add = map_now[...], add_now[...]
    column = lambda x: jnp.sum(x, axis=0, keepdims=True)
    for i in reversed(range(per)):
        at = slice(i * SPAN, (i + 1) * SPAN)
        q_here, v_here, g_here = q[at, :], v[at, :], gate[at, :]
        rate = jax.nn.sigmoid(rows[1:2] + rin[at, :])
        k = kp[at, :] * (1.0 + (rate - 1.0) * rows[3:4])
        unit, scale, extra, summed = normed(out_ref[at, :], q_here, k, v_here, rows, c)
        grad = sum(x[at, :].astype(f32) for x in d_gated)
        if i == per - 1:
            grad = grad + jnp.where(last_row, fix, 0.0)
        d_gate[at, :] = (grad * summed).astype(bf16)
        d_sum = grad * g_here
        d_unit = d_sum * rows[5:6]
        d_here = scale * (
            d_unit
            - head_sum(d_unit, ones) * (1.0 / SPAN)
            - unit * head_sum(d_unit * unit, ones) * (1.0 / SPAN)
        )
        d_extra = head_sum(d_sum * v_here, ones)
        d_out[at, :] = d_here
        dq_post[at, :] = d_extra * k * rows[4:5]
        dk_post[at, :] = d_extra * q_here * rows[4:5]
        dv_post[at, :] = d_sum * extra
        row_grads[4:5, :] += column(d_extra * q_here * k)
        row_grads[5:6, :] += column(d_sum * unit)
        row_grads[6:7, :] += column(d_sum)
        maps[at, :] = state_map
        adds[at, :] = state_add
        carry_here = carry[i * width : (i + 1) * width, :]
        both = dot(
            jnp.concatenate([state_map, state_add], axis=0).astype(bf16), carry_here, 1, 1
        )
        state_map = both[:SPAN]
        state_add = both[SPAN:] + fold(cross(d_here, read[at, :]), c["mask"])
    map_now[...] = state_map
    add_now[...] = state_add
    map_end[...] = state_map
    add_end[...] = state_add


def grads_kernel(per, q, kp, v, din, rin, lat_ref, d_gate_ref, rows_ref, up_ref, push_ref, inv_ref, uk_ref, qk_ref, qr_ref,
                 starts, ends, d_out, dq_post, dk_post, dv_post, maps, adds, grad_in, dq_ref,
                 dkp_ref, dv_ref, pre_ref, row_grads, up_grads):
    c = constants(q.shape[1])
    up = up_ref[...]
    rows = rows_ref[...]
    mask, ones = c["mask"], c["ones"]
    cat = lambda *parts: jnp.concatenate(parts, axis=0)
    column = lambda x: jnp.sum(x, axis=0, keepdims=True)

    @pl.when(pl.program_id(0) == 0)
    def _():
        row_grads[...] = jnp.zeros_like(row_grads)
        up_grads[...] = jnp.zeros_like(up_grads)

    zero = jnp.zeros((SPAN, mask.shape[0]), f32)
    rank, gate_at = low_parts(up.shape[0])
    lane = lax.broadcasted_iota(jnp.int32, (SPAN, up.shape[0]), 1)
    low_row = lax.broadcasted_iota(jnp.int32, up_grads.shape, 0)
    for i in range(per):
        at = slice(i * SPAN, (i + 1) * SPAN)
        q_here, kp_here, v_here = q[at, :], kp[at, :], v[at, :]
        e = ready(q_here, kp_here, din[at, :], rin[at, :], rows, c)
        start, end, pushed, d_read = starts[at, :], ends[at, :], push_ref[at, :], d_out[at, :]
        grad_end = adds[at, :] + times(grad_in[...], maps[at, :], mask, 0)
        grown = grad_end * e["last"]
        by_state = times(cat(e["K"], e["R"]), grown, mask, 1)
        d_push = -fold(cross(qr_ref[at, :], d_read), mask) - by_state[SPAN:]
        d_rhs = fold(cross(inv_ref[at, :], d_push), mask)
        d_value = (
            by_state[:SPAN]
            + fold(cross(cat(qk_ref[at, :], uk_ref[at, :]), cat(d_read, d_rhs)), mask)
        )
        both = cat(d_rhs, d_read)
        by_value = times(both, v_here, mask, 1)
        by_push = times(both, pushed, mask, 1)
        d_key_pairs = cat(
            jnp.where(c["strict"], by_value[:SPAN], zero), jnp.where(c["incl"], by_value[SPAN:], zero)
        )
        d_removal_pairs = cat(
            jnp.where(c["strict"], -by_push[:SPAN], zero), jnp.where(c["incl"], -by_push[SPAN:], zero)
        )
        d_queries = (
            times(both, start, mask, 0)
            + times(d_key_pairs, e["K"], mask, 0)
            + times(d_removal_pairs, e["R"], mask, 0)
        )
        by_grown = times(cat(v_here, -pushed), grown, mask, 0)
        queries = cat(e["U"], e["Q"])
        d_k_grown = by_grown[:SPAN] + fold(cross(d_key_pairs, queries), mask)
        d_r_grown = by_grown[SPAN:] + fold(cross(d_removal_pairs, queries), mask)
        d_u_grown, d_q_grown = d_queries[:SPAN], d_queries[SPAN:]
        on_unit = d_u_grown * e["U"]
        steps = d_q_grown * e["Q"] - d_k_grown * e["K"] - d_r_grown * e["R"] + on_unit
        d_log = exact_left(c["upper"], steps) - on_unit + column(grad_end * end)
        rate = e["rate"]
        d_k = d_k_grown * e["down"] + dk_post[at, :]
        d_removal = d_r_grown * e["down"]
        d_unit = d_u_grown * e["before"] + d_removal * rate
        d_rate_value = d_removal * e["unit"] + d_k * kp_here * rows[3:4]
        d_scaled = e["inv"] * (d_unit - e["unit"] * head_sum(d_unit * e["unit"], ones))
        d_rate = d_rate_value * rate * (1.0 - rate)
        d_decay = d_log * e["log_decay"] * (1.0 - e["sig"])
        dq_ref[at, :] = (d_q_grown * e["up"] + dq_post[at, :]).astype(bf16)
        dkp_ref[at, :] = (d_k * (1.0 + (rate - 1.0) * rows[3:4]) + d_scaled * rows[2:3]).astype(bf16)
        dv_ref[at, :] = (d_value + dv_post[at, :]).astype(bf16)
        lat = lat_ref[at, :]
        low = lat.astype(bf16)
        d_outs = (d_decay.astype(bf16), d_rate.astype(bf16), d_gate_ref[at, :])
        pick = lambda where, parts: jnp.where(
            where < rank, parts[0], jnp.where(where < gate_at, parts[1], parts[2])
        )
        slope = pick(lane, (1.0 - lat * lat, jnp.ones_like(lat), lat * (1.0 - lat)))
        pre = pick(lane, [dot(x, up, 1, 1) for x in d_outs]) * slope
        pre_ref[at, :] = pre.astype(bf16)
        up_grads[...] += pick(low_row, [dot(low, x, 0, 0) for x in d_outs])
        row_grads[0:1, :] += column(d_decay)
        row_grads[1:2, :] += column(d_rate)
        row_grads[2:3, :] += column(d_scaled * kp_here)
        row_grads[3:4, :] += column(d_k * kp_here * (rate - 1.0))


def run_blocks(kernel, ins, outs, scratch, tokens, reverse=False):
    count = tokens // SPAN
    per = blocks_per_step(count)
    steps = count // per

    def spec(shape, cut):
        if not cut:
            return pl.BlockSpec(shape, lambda i: (0, 0))
        rows = shape[0] // steps
        if reverse:
            return pl.BlockSpec((rows, shape[1]), lambda i: (steps - 1 - i, 0))
        return pl.BlockSpec((rows, shape[1]), lambda i: (i, 0))

    return pl.pallas_call(
        functools.partial(kernel, per),
        grid=(steps,),
        in_specs=[spec(x.shape, cut) for x, cut in ins],
        out_specs=[spec(shape, cut) for shape, _, cut in outs],
        out_shape=[jax.ShapeDtypeStruct(shape, kind) for shape, kind, _ in outs],
        scratch_shapes=[pltpu.VMEM(shape, f32) for shape in scratch],
        compiler_params=pltpu.CompilerParams(dimension_semantics=("arbitrary",)),
        cost_estimate=pl.CostEstimate(flops=10**10, bytes_accessed=2 * 10**7, transcendentals=0),
    )(*[x for x, _ in ins])


def low_parts(width):
    return width // 4, width // 2


def mixed(unit, edge, norms, count):
    first = unit * norms[0:1] + norms[1:2]
    before = (edge[0:1] * norms[0:1] + norms[1:2]) * edge[1:2]
    row = lax.broadcasted_iota(jnp.int32, first.shape, 0)
    diff = jnp.where(row == 0, before, pltpu.roll(first, 1, 0)) - first
    return diff, [(first + diff * norms[4 + i : 5 + i]).astype(bf16) for i in range(count)]


def slab_weights(gathered, width):
    parts, rows, _ = gathered.shape
    part = rows // 4
    piece = lambda i, w: jnp.concatenate(
        [gathered[j, i * part : (i + 1) * part, :w] for j in range(parts)], axis=0
    )
    return [piece(i, width) for i in range(3)] + [piece(3, gathered.shape[2])]


def project_kernel(ids, unit, edge, norms, gathered, up, q, kp, v, din, rin, gate, lat, low_total):
    width = q.shape[1]
    step = pl.program_id(0)
    norms_here = norms[...]
    _, mixes = mixed(unit[...], edge[...], norms_here, 6)
    w_q, w_k, w_v, w_low = slab_weights(gathered, width)
    low_width = w_low.shape[1]
    rank, gate_at = low_parts(low_width)
    lane = lax.broadcasted_iota(jnp.int32, low_total.shape, 1)
    low = jnp.where(
        lane < rank,
        dot(mixes[1], w_low, 1, 0),
        jnp.where(lane < gate_at, dot(mixes[4], w_low, 1, 0), dot(mixes[5], w_low, 1, 0)),
    )

    @pl.when(step == 0)
    def _():
        q[...] = dot(mixes[0], w_q, 1, 0)
        kp[...] = dot(mixes[2], w_k, 1, 0)
        v[...] = dot(mixes[3], w_v, 1, 0)
        low_total[...] = low

    @pl.when(step > 0)
    def _():
        q[...] += dot(mixes[0], w_q, 1, 0)
        kp[...] += dot(mixes[2], w_k, 1, 0)
        v[...] += dot(mixes[3], w_v, 1, 0)
        low_total[...] += low

    @pl.when(step == pl.num_programs(0) - 1)
    def _():
        total = low_total[...]
        lats = jnp.where(
            lane < rank, jnp.tanh(total), jnp.where(lane < gate_at, total, jax.nn.sigmoid(total))
        )
        lat[...] = lats
        zero = jnp.zeros_like(lats)
        chosen = lambda where: jnp.where(where, lats, zero).astype(bf16)
        din[...] = dot(chosen(lane < rank), up[...], 1, 0)
        rin[...] = dot(chosen((lane >= rank) & (lane < gate_at)), up[...], 1, 0)
        gate[...] = dot(chosen(lane >= gate_at), up[...], 1, 0)


def unproject_kernel(quick, ids, unit, edge, scales, norms, gathered, dq, dkp, dv, pre, d_mid,
                     up_grads, second, rows_pre, rows_post, packed, feature, edge_fix, *rest):
    pieces, (all_first, all_unit) = rest[:-2], rest[-2:]
    block = lambda j: (j + ids[3]) % 2 if quick else j
    width = dq.shape[1]
    step = pl.program_id(0)
    n = norms[...]
    edge_here = edge[...]
    unit_here = unit[...]
    diff, mixes = mixed(unit_here, edge_here, n, 6)
    weights = slab_weights(gathered, width)
    w_low = weights[3]
    slab, low_width = w_low.shape
    rank, gate_at = low_parts(low_width)
    pre_here = pre[...]
    lane = lax.broadcasted_iota(jnp.int32, pre_here.shape, 1)
    none = jnp.zeros_like(pre_here)
    pres = [
        jnp.where(lane < rank, pre_here, none),
        jnp.where((lane >= rank) & (lane < gate_at), pre_here, none),
        jnp.where(lane >= gate_at, pre_here, none),
    ]
    sources = [(0, dq[...], 0), (2, dkp[...], 1), (3, dv[...], 2), (1, pres[0], 3), (4, pres[1], 3),
               (5, pres[2], 3)]
    low_lane = lax.broadcasted_iota(jnp.int32, (slab, low_width), 1)
    column = lambda x: jnp.sum(x, axis=0, keepdims=True)
    parts = gathered.shape[0]
    part = slab // parts
    direct = shifted = None
    low_grad = None
    for mix, grad, which in sources:
        weight_grad = dot(mixes[mix], grad, 0, 0)
        if which < 3:
            for j in range(parts):
                packed[block(j), which * part : (which + 1) * part, :width] = weight_grad[
                    j * part : (j + 1) * part
                ].astype(bf16)
                if width < low_width:
                    packed[block(j), which * part : (which + 1) * part, width:] = jnp.zeros(
                        (part, low_width - width), bf16
                    )
        else:
            low_grad = weight_grad if low_grad is None else low_grad + weight_grad
        d_mix = dot(grad, weights[which], 1, 1)
        feature[4 + mix : 5 + mix, :] = column(d_mix * diff)
        to_shift = d_mix * n[4 + mix : 5 + mix]
        shifted = to_shift if shifted is None else shifted + to_shift
        direct = d_mix - to_shift if direct is None else direct + (d_mix - to_shift)
    for j in range(parts):
        packed[block(j), 3 * part : 4 * part, :] = low_grad[j * part : (j + 1) * part].astype(bf16)
    tokens = unit_here.shape[0]
    row = lax.broadcasted_iota(jnp.int32, shifted.shape, 0)
    d_first = direct + jnp.where(row == tokens - 1, 0.0, pltpu.roll(shifted, tokens - 1, 0))
    before = shifted[0:1] * edge_here[1:2]
    feature[0:1, :] = column(d_first * unit_here) + before * edge_here[0:1]
    feature[1:2, :] = column(d_first) + before
    feature[2:4, :] = second[0:2, :]
    feature[10:11, :] = second[2:3, :]
    feature[11:, :] = jnp.zeros_like(feature[11:, :])
    if quick:
        up_rows, gate_rows = rank // (8), (low_width - gate_at) // 8
        head_part = width // SPAN * (SPAN // 8)
        row_grads = jnp.concatenate([rows_pre[0:4, :], rows_post[4:8, :]], axis=0)
        source = lax.broadcasted_iota(jnp.int32, (width, width), 0)
        target = lax.broadcasted_iota(jnp.int32, (width, width), 1)
        each = SPAN // 8
        for j in range(parts):
            dest = step * parts + j
            take = lambda at, size: up_grads[pl.ds(pl.multiple_of(at + dest * size, size), size), :]
            ups = jnp.concatenate([take(0, up_rows), take(rank, up_rows)], axis=0)
            chosen = (target // each * SPAN + dest * each + target % each == source) & (
                target < head_part
            )
            heads_here = dot(row_grads.astype(bf16), jnp.where(chosen, 1.0, 0.0).astype(bf16), 1, 0)
            values = feature[:, j * part : (j + 1) * part]
            at = 4 * part
            to = block(j)
            packed[to, at : at + EDGE, :] = ups.astype(bf16)
            packed[to, at + EDGE : at + 2 * EDGE, :] = take(gate_at, gate_rows).astype(bf16)
            packed[to, at + 2 * EDGE : at + 3 * EDGE, :] = jnp.concatenate(
                [values, jnp.zeros_like(values)], axis=1
            ).astype(bf16)
            packed[to, at + 3 * EDGE : at + 4 * EDGE, :] = jnp.concatenate(
                [heads_here, jnp.zeros_like(heads_here)], axis=0
            ).astype(bf16)
    at = pl.ds(pl.multiple_of(step * slab, slab), slab)
    all_first[:tokens, at] = d_first * n[0:1]
    all_first[tokens:, at] = jnp.broadcast_to(before * n[0:1], (8, slab))
    all_unit[:tokens, at] = unit_here
    all_unit[tokens:, at] = jnp.broadcast_to(edge_here[0:1], (8, slab))

    @pl.when(step == pl.num_programs(0) - 1)
    def _():
        d_unit = all_first[...]
        units = all_unit[...]
        features = d_unit.shape[1]
        mean = jnp.sum(d_unit, axis=1, keepdims=True) * (1.0 / features)
        along = jnp.sum(d_unit * units, axis=1, keepdims=True) * (1.0 / features)
        result = scales[...] * (d_unit - mean - units * along)
        edge_fix[...] = result[tokens:] + d_mid[tokens + EDGE - 8 :, :]
        all_first[:tokens, :] = result[:tokens] + d_mid[:tokens, :]
        send_pieces(pieces, all_first, ids[0])


EDGE = 16


def share_of(here, by, devices, size):
    return pl.ds(pl.multiple_of(lax.rem(here + by + devices, devices) * size, size), size)


def send_pieces(pieces, whole, here):
    share = pieces[0].shape[0]
    for by, piece in enumerate(pieces):
        piece[...] = whole[share_of(here, by, len(pieces), share), :].astype(piece.dtype)


def channel_kernel(devices, here, *refs):
    stream, edge_stream, has_edge, cot, norms, out_full, key, value = refs[:8]
    gated, edges = refs[8 : 8 + devices], refs[8 + devices : 8 + 2 * devices]
    refs = refs[8 + 2 * devices :]
    ffn_in, hidden, d_pre, cot_low, d_mid_low, d_mid, feature, middle_share = refs[:8]
    ffn_pieces, refs = refs[8 : 8 + devices], refs[8 + devices :]
    grad_pieces, refs = refs[:devices], refs[devices:]
    fix_pieces, refs = refs[:devices], refs[devices:]
    middle, unit, scale, diff, d_ffn, ffn_out = refs
    step = pl.program_id(0)
    tokens, features = stream.shape
    width = gated[0].shape[1]
    n = norms[...]
    flag = has_edge[0:1, 0:1]
    row = lax.broadcasted_iota(jnp.int32, (tokens + EDGE, features), 0)

    @pl.when(step == 0)
    def _():
        middle[:tokens, :] = stream[...]
        middle[tokens:, :] = edge_stream[...]
        for by in range(devices):
            rows = out_full[share_of(here[0], -by, devices, width), :]
            middle[:tokens, :] += dot(gated[by][...], rows, 1, 0)
            middle[tokens:, :] += dot(edges[by][...], rows, 1, 0)
        middle_share[...] = middle[share_of(here[0], 0, devices, tokens // devices), :]
        values = middle[...]
        center = values - jnp.sum(values, axis=1, keepdims=True) * (1.0 / features)
        spread_here = jnp.sum(center * center, axis=1, keepdims=True) * (1.0 / features)
        scale_here = lax.rsqrt(spread_here + 1e-05)
        unit_here = center * scale_here
        unit[...] = unit_here
        scale[...] = scale_here
        norm = unit_here * n[2:3] + n[3:4]
        before = pltpu.roll(norm, 1, 0)
        diff_here = jnp.where(row == 0, before * flag, before) - norm
        diff[...] = diff_here
        ffn_in[...] = (norm + diff_here * n[10:11])[:tokens].astype(bf16)
        cot_low[...] = cot[...].astype(bf16)
        d_ffn[...] = jnp.zeros_like(d_ffn)
        ffn_out[...] = jnp.zeros_like(ffn_out)

    act = jnp.maximum(dot(ffn_in[...], key[...], 1, 0), 0.0)
    hidden_here = (act * act).astype(bf16)
    hidden[...] = hidden_here
    d_pre_here = (dot(cot_low[...], value[...], 1, 1) * 2.0 * act).astype(bf16)
    d_pre[...] = d_pre_here
    d_ffn[:tokens, :] += dot(d_pre_here, key[...], 1, 1)
    ffn_out[...] += dot(hidden_here, value[...], 1, 0)

    @pl.when(step == pl.num_programs(0) - 1)
    def _():
        send_pieces(ffn_pieces, ffn_out, here[0])
        grad = d_ffn[...]
        to_shift = grad * n[10:11]
        moved = pltpu.roll(to_shift, tokens + EDGE - 1, 0)
        d_second = grad - to_shift + jnp.where(row == tokens + EDGE - 1, moved * flag, moved)
        unit_here = unit[...]
        column = lambda x: jnp.sum(x, axis=0, keepdims=True)
        feature[...] = jnp.zeros_like(feature)
        feature[0:1, :] = column(d_second * unit_here)
        feature[1:2, :] = column(d_second)
        feature[2:3, :] = column(grad * diff[...])
        d_unit = d_second * n[2:3]
        mean = jnp.sum(d_unit, axis=1, keepdims=True) * (1.0 / features)
        along = jnp.sum(d_unit * unit_here, axis=1, keepdims=True) * (1.0 / features)
        d_mid_here = scale[...] * (d_unit - mean - unit_here * along)
        d_mid[...] = d_mid_here
        d_mid_low[tokens:, :] = d_mid_here[tokens:].astype(bf16)
        d_mid_low[:tokens, :] = (d_mid_here[:tokens] + cot[...] * (1.0 / devices)).astype(bf16)
        for by in range(devices):
            rows = out_full[share_of(here[0], by, devices, width), :]
            grad_pieces[by][...] = dot(d_mid_low[:tokens, :], rows, 1, 1).astype(bf16)
            fix_pieces[by][...] = dot(d_mid_low[tokens:, :], rows, 1, 1).astype(bf16)


def large_kernel(devices, here, *refs):
    hidden, cot_low, ffn_in, d_pre, d_mid_low = refs[:5]
    gated, edges, large = refs[5 : 5 + devices], refs[5 + devices : 5 + 2 * devices], refs[-1]
    tokens, hidden_here = hidden.shape
    part = large.shape[2]
    width = gated[0].shape[1]
    large[0, :hidden_here, :] = dot(hidden[...], cot_low[...], 0, 0).astype(bf16)
    key_grad = dot(ffn_in[...], d_pre[...], 0, 0).astype(bf16)
    for j in range(hidden_here // part):
        at = hidden_here + j * part
        large[0, at : at + part, :] = key_grad[:, j * part : (j + 1) * part]
    grad, grad_edge = d_mid_low[:tokens, :], d_mid_low[tokens:, :]
    for by in range(devices):
        rows = dot(gated[by][...], grad, 0, 0) + dot(edges[by][...], grad_edge, 0, 0)
        at = lax.rem(here[0] - by + devices, devices) * width + 2 * hidden_here
        large[0, pl.ds(pl.multiple_of(at, width), width), :] = rows.astype(bf16)


def run_slabs(kernel, ids, ins, outs, scratch, slabs):
    def spec(shape, cut):
        shape = tuple(shape)
        if cut is None:
            return pl.BlockSpec(shape, lambda i, ids: (0,) * len(shape))
        if callable(cut[1]):
            return pl.BlockSpec(*cut)
        dim, size = cut
        block = list(shape)
        block[dim] = shape[dim] // slabs
        if size is not None:
            block[size[0]] = size[1]
        return pl.BlockSpec(
            tuple(block), lambda i, ids: tuple(i if k == dim else 0 for k in range(len(shape)))
        )

    return pl.pallas_call(
        kernel,
        grid_spec=pltpu.PrefetchScalarGridSpec(
            num_scalar_prefetch=1,
            grid=(slabs,),
            in_specs=[spec(x.shape, cut) for x, cut in ins],
            out_specs=[spec(shape, cut) for shape, _, cut in outs],
            scratch_shapes=[pltpu.VMEM(shape, f32) for shape in scratch],
        ),
        out_shape=[jax.ShapeDtypeStruct(shape, kind) for shape, kind, _ in outs],
        compiler_params=pltpu.CompilerParams(dimension_semantics=("arbitrary",)),
        cost_estimate=pl.CostEstimate(flops=10**10, bytes_accessed=2 * 10**7, transcendentals=0),
    )(ids, *[x for x, _ in ins])


def core_sum_kernel(ids, kept, came, send_x, send_y, keep_x, keep_y):
    half = send_x.shape[1]
    total = lambda i, rows: kept[i, rows, :].astype(f32) + came[i, rows, :].astype(f32)
    for y in range(2):
        keep_x[y] = total(y, slice(0, half))
        send_x[y] = total(2 + y, slice(0, half)).astype(bf16)
    for x in range(2):
        keep_y[x] = total(2 * x, slice(half, 2 * half))
        send_y[x] = total(2 * x + 1, slice(half, 2 * half)).astype(bf16)


def side_sum_kernel(ids, keep_x, keep_y, came_x, came_y, left_x, left_y, send_y, send_x):
    left_x[...] = keep_x[0] + came_x[0].astype(f32)
    left_y[...] = keep_y[0] + came_y[0].astype(f32)
    send_y[...] = (keep_x[1] + came_x[1].astype(f32)).astype(bf16)
    send_x[...] = (keep_y[1] + came_y[1].astype(f32)).astype(bf16)


def last_sum_kernel(ids, left_x, left_y, came_y, came_x, fix, rkv, up, gate_up, head, shared, whole):
    half = left_x.shape[0]
    whole[:half, :] = left_x[...] + came_y[...].astype(f32)
    whole[half:, :] = left_y[...] + came_x[...].astype(f32)
    first = rkv.shape[0]
    low = shared.shape[0] - 2 * EDGE
    rkv[...] = whole[:first, :]
    shared[:low, :] = whole[first : first + low, :].astype(bf16)
    at = first + low
    up[...] = whole[at : at + EDGE, :]
    gate_up[...] = whole[at + EDGE : at + 2 * EDGE, :]
    shared[low : low + EDGE, :] = whole[at + 2 * EDGE : at + 3 * EDGE, :].astype(bf16)
    head[...] = whole[at + 3 * EDGE :, :]
    shared[low + EDGE :, :] = fix[...]


def share_sum_kernel(devices, ids, *refs):
    pieces, out, ordered = refs[:devices], refs[devices], refs[devices + 1]
    for by in range(devices):
        ordered[lax.rem(ids[0] - by + devices, devices)] = pieces[by][...].astype(f32)
    total = ordered[0]
    for i in range(1, devices):
        total = total + ordered[i]
    out[...] = total


def to_next(x, axis, by):
    devices = lax.axis_size(axis)
    pairs_here = [(i, i + by) for i in range(devices) if 0 <= i + by < devices]
    return lax.ppermute(x, axis, pairs_here)


def around(x, by):
    devices = lax.axis_size("mp")
    return lax.ppermute(x, "mp", [(i, (i + by) % devices) for i in range(devices)])


def slanted(x, along, by):
    rows, devices = lax.axis_size("seq"), lax.axis_size("mp")
    pairs_here = [
        (s * devices + i, (s + along) * devices + (i + by) % devices)
        for s in range(rows)
        if 0 <= s + along < rows
        for i in range(devices)
    ]
    return lax.ppermute(x, ("seq", "mp"), pairs_here)


def gather_shares(x):
    devices = lax.axis_size("mp")
    came = [x] + [around(x, by) for by in range(1, devices)]
    turned = jnp.stack([came[-k % devices] for k in range(devices)] * 2)
    at = (devices - lax.axis_index("mp")) % devices
    return lax.dynamic_slice_in_dim(turned, at, devices, 0)


def scatter_shares(x):
    devices = lax.axis_size("mp")
    here = lax.axis_index("mp")
    term = lambda at: lax.dynamic_index_in_dim(x, at % devices, 0, keepdims=False)
    total = term(here).astype(f32)
    for by in range(1, devices):
        total = total + around(term(here + by), by).astype(f32)
    return total


def mm_left(a, b):
    return dot(a, b, 0, 0)


def statistics(values):
    center = values - jnp.mean(values, axis=-1, keepdims=True)
    scale = lax.rsqrt(jnp.mean(center * center, axis=-1, keepdims=True) + 1e-05)
    return center * scale, scale


def carry_states(state_map, state_add, by):
    entering = to_next(state_add.astype(bf16), "seq", by).astype(f32)
    heads = state_map.shape[1] // SPAN
    apart = lambda x: x.reshape(SPAN, heads, SPAN).transpose(1, 0, 2)
    for _ in range(lax.axis_size("seq") - 2):
        moved = jnp.einsum("hij,hjl->hil", apart(entering), apart(state_map), precision="highest")
        passed = moved.transpose(1, 0, 2).reshape(state_add.shape) + state_add
        entering = to_next(passed.astype(bf16), "seq", by).astype(f32)
    return entering


def wide(x, width):
    return jnp.pad(x, ((0, 0), (0, width - x.shape[1])))


def body(inputs, rkv_weight, output_weight, first_factors, second_factors, gate_first, gate_second,
         key_weight, value_weight, head_table, feature_table, cotangent):
    group = ("dp", "seq")
    count = lax.axis_size("dp") * lax.axis_size("seq")
    mp = lax.axis_size("mp")
    mp_here = lax.axis_index("mp")
    stream = inputs[0]
    cot = cotangent[0]
    tokens, features = stream.shape
    share = tokens // mp
    share_at = mp_here * share
    part = features // count
    width = rkv_weight.shape[2]
    heads = width // SPAN
    rank, gate_rank = first_factors.shape[2], gate_first.shape[1]
    low_width = 2 * rank + gate_rank
    lanes = max(width, low_width, part)
    up_rows = second_factors.shape[1]
    head_part = head_table.shape[2]
    dp_here, seq_here = lax.axis_index("dp"), lax.axis_index("seq")
    quick = lax.axis_size("dp") == 4 and lax.axis_size("seq") == 2 and part == 128 and width == 256
    ids = jnp.stack([mp_here, dp_here // 2, dp_here % 2, seq_here]).astype(jnp.int32)
    edge_stream = to_next(stream[-EDGE:], "seq", 1)
    edge_row = edge_stream[EDGE - 1 :]
    pieces = [
        wide(rkv_weight.reshape(3 * part, width), lanes),
        wide(jnp.concatenate([first_factors[0], first_factors[1], gate_first], axis=1), lanes),
        wide(second_factors.reshape(2 * up_rows, width), lanes),
        wide(gate_second, lanes),
        jnp.pad(wide(feature_table, lanes), ((0, 5), (0, 0))),
        jnp.pad(wide(head_table.reshape(7, heads * head_part), lanes), ((0, 9), (0, 0))),
    ]
    edges = [0]
    for piece in pieces:
        edges.append(edges[-1] + piece.shape[0])
    packed = jnp.concatenate(pieces, axis=0)
    rows_full = -(-packed.shape[0] // 16) * 16
    packed = jnp.pad(packed, ((0, rows_full - packed.shape[0]), (0, 0)))
    gathered = lax.all_gather(packed, group, axis=0, tiled=False)
    cut = lambda i, w: gathered[:, edges[i] : edges[i + 1], :w]
    up = cut(2, width).reshape(count, 2, up_rows, width).transpose(1, 0, 2, 3)
    up = jnp.concatenate(
        [up.reshape(2 * rank, width), cut(3, width).reshape(gate_rank, width)], axis=0
    )
    norms = cut(4, part).transpose(1, 0, 2).reshape(16, features).astype(f32)
    head_rows = (
        cut(5, heads * head_part)[:, :7]
        .reshape(count, 7, heads, head_part)
        .transpose(1, 2, 0, 3)
        .reshape(7, width)
        .astype(f32)
    )
    head_rows = jnp.pad(head_rows, ((0, 1), (0, 0)))

    out_column = gather_shares(output_weight).reshape(features, part)
    rest = lax.all_gather(
        jnp.concatenate([value_weight, out_column], axis=0), group, axis=0, tiled=False
    )
    hidden_here = value_weight.shape[0]
    key_full = lax.all_gather(key_weight, group, axis=0, tiled=True)

    unit_one, scale_one = statistics(stream)
    edge_unit, edge_scale = statistics(edge_row)
    has_edge = (lax.axis_index("seq") > 0).astype(f32)
    edge = jnp.concatenate(
        [edge_unit, jnp.broadcast_to(has_edge, (1, features)), jnp.zeros((6, features), f32)]
    )
    slab = max(256, part)
    slabs = features // slab
    in_slabs = (1, None)
    of_gathered = (0, (1, 4 * part))
    whole = (tokens, width)
    q, kp, v, din, rin, gate, lat = run_slabs(
        project_kernel,
        ids,
        [(unit_one, in_slabs), (edge, in_slabs), (norms, in_slabs), (gathered, of_gathered), (up, None)],
        [(whole, f32, None)] * 6 + [((tokens, low_width), f32, None)],
        [(tokens, low_width)],
        slabs,
    )

    state = (SPAN, width)
    (local_out, read, push_map, push, inv, uk, qk, qr, carry, maps, adds, map_end, add_end) = run_blocks(
        local_kernel,
        [(q, True), (kp, True), (v, True), (din, True), (rin, True), (head_rows, False)],
        [(whole, f32, True)] * 4
        + [(whole, bf16, True)] * 4
        + [((tokens // SPAN * width, width), bf16, True)]
        + [(whole, f32, True)] * 2
        + [(state, f32, False)] * 2,
        [state, state],
        tokens,
    )
    entering = carry_states(map_end, add_end, 1)
    gated, read_out, pushed, starts, ends = run_blocks(
        finish_kernel,
        [(x, True) for x in (q, kp, v, rin, gate)]
        + [(head_rows, False)]
        + [(x, True) for x in (local_out, read, push_map, push, maps, adds)]
        + [(entering, False)],
        [(whole, bf16, True)] + [(whole, f32, True)] * 4,
        [state],
        tokens,
    )

    edge_parts = [slanted(gated[-EDGE:], 1, by) for by in range(mp)]
    gated_parts = [gated] + [around(gated, by) for by in range(1, mp)]
    value_full = rest[:, :hidden_here].transpose(1, 0, 2).reshape(hidden_here, features)
    out_full = rest[:, hidden_here:].transpose(1, 0, 2).reshape(features, features)
    longer = tokens + EDGE
    lots = key_full.shape[1] // part
    channel = run_slabs(
        functools.partial(channel_kernel, mp),
        ids,
        [(stream, None), (edge_stream, None), (edge[1:2, :128], None), (cot, None)]
        + [(norms, None), (out_full, None), (key_full, (1, None)), (value_full, (0, None))]
        + [(x, None) for x in gated_parts + edge_parts],
        [
            ((tokens, features), bf16, None),
            ((tokens, hidden_here), bf16, (1, None)),
            ((tokens, hidden_here), bf16, (1, None)),
            ((tokens, features), bf16, None),
            ((longer, features), bf16, None),
            ((longer, features), f32, None),
            ((8, features), f32, None),
            ((share, features), f32, None),
        ]
        + [((share, features), bf16, None)] * mp
        + [(whole, bf16, None)] * mp
        + [((EDGE, width), bf16, None)] * mp,
        [(longer, features)] * 2
        + [(longer, 1)]
        + [(longer, features)] * 2
        + [(tokens, features)],
        max(1, hidden_here // 256),
    )
    ffn_in, hidden, d_pre, cot_low, d_mid_low, d_mid, second_rows, middle_share = channel[:8]
    ffn_pieces = channel[8 : 8 + mp]
    grad_pieces = channel[8 + mp : 8 + 2 * mp]
    fix_pieces = channel[8 + 2 * mp :]
    fixes = [slanted(fix_pieces[by], -1, by) for by in range(mp)]
    d_gated = [grad_pieces[0]]
    for by in range(1, mp):
        d_gated.append(around(grad_pieces[by], by))

    if part % 128 == 0:
        large = run_slabs(
            functools.partial(large_kernel, mp),
            ids,
            [(hidden, None), (cot_low, (1, None)), (ffn_in, (1, None)), (d_pre, None)]
            + [(d_mid_low, (1, None))]
            + [(x, None) for x in gated_parts + edge_parts],
            [((count, 2 * hidden_here + features, part), bf16, (0, None))],
            [],
            count,
        )[0]
    else:
        by_part = lambda x: x.astype(bf16).reshape(x.shape[0], count, part).transpose(1, 0, 2)
        key_grad = mm_left(ffn_in, d_pre).astype(bf16)
        key_grad = key_grad.reshape(count, part, lots, part).transpose(0, 2, 1, 3)
        order = lambda parts: jnp.concatenate(parts[:1] + parts[:0:-1], axis=0)
        out_rows = order([mm_left(x, d_mid_low[:tokens]) for x in gated_parts]) + order(
            [mm_left(x, d_mid_low[tokens:]) for x in edge_parts]
        )
        large = jnp.concatenate(
            [
                by_part(mm_left(hidden, cot_low)),
                key_grad.reshape(count, lots * part, part),
                by_part(jnp.roll(out_rows, mp_here * width, axis=0)),
            ],
            axis=1,
        )
    large = lax.psum_scatter(large, group, scatter_dimension=0, tiled=False)
    d_gated, ffn_pieces = lax.optimization_barrier((d_gated, ffn_pieces))
    block_out = middle_share + ffn_pieces[0].astype(f32)
    for by in range(1, mp):
        came = around(ffn_pieces[by], by)
        block_out = block_out + came.astype(f32)

    (d_read, dq_post, dk_post, dv_post, d_gate, back_maps, back_adds, back_map_end, back_add_end,
     row_grads_post) = run_blocks(
        functools.partial(reads_kernel, mp),
        [(x, True) for x in (q, kp, v, rin, gate)]
        + [(head_rows, False)]
        + [(x, True) for x in (read_out, read, carry)]
        + [(x, True) for x in d_gated]
        + [(x, False) for x in fixes],
        [(whole, f32, True)] * 4
        + [(whole, bf16, True)]
        + [(whole, f32, True)] * 2
        + [(state, f32, False)] * 2
        + [((8, width), f32, False)],
        [state, state],
        tokens,
        reverse=True,
    )
    grad_in = carry_states(back_map_end, back_add_end, -1)
    dq, dkp, dv, pre, row_grads, up_grads = run_blocks(
        grads_kernel,
        [(x, True) for x in (q, kp, v, din, rin, lat, d_gate)]
        + [(head_rows, False), (up, False)]
        + [
            (x, True)
            for x in (pushed, inv, uk, qk, qr, starts, ends, d_read, dq_post, dk_post, dv_post,
                      back_maps, back_adds)
        ]
        + [(grad_in, False)],
        [(whole, bf16, True)] * 3
        + [((tokens, low_width), bf16, True), ((8, width), f32, False)]
        + [((low_width, width), f32, False)],
        [],
        tokens,
    )

    scales = jnp.concatenate([scale_one, jnp.broadcast_to(edge_scale, (8, 1))], axis=0)
    packed_rows = rows_full if quick else 4 * part
    whose = lambda i, ids: (((i + ids[2]) % 2) * 2 + (i // 2 + ids[1]) % 2, 0, 0)
    unprojected = run_slabs(
        functools.partial(unproject_kernel, quick),
        ids,
        [(unit_one, in_slabs), (edge, in_slabs), (scales, None), (norms, in_slabs)]
        + [(gathered, of_gathered), (dq, None), (dkp, None), (dv, None), (pre, None), (d_mid, None)]
        + [(up_grads, None), (second_rows, in_slabs), (row_grads, None), (row_grads_post, None)],
        [
            (
                (count, packed_rows, lanes),
                bf16,
                ((2, packed_rows, lanes), whose) if quick else (0, None),
            ),
            ((16, features), f32, in_slabs),
            ((8, features), f32, None),
        ]
        + [((share, features), bf16, None)] * mp,
        [(tokens + 8, features)] * 2,
        slabs,
    )
    packed, feature_grad, edge_fix = unprojected[:3]
    stream_pieces = unprojected[3:]
    fix = to_next(edge_fix[7:].astype(bf16), "seq", -1)
    stream_came = [stream_pieces[0]] + [around(stream_pieces[by], by) for by in range(1, mp)]
    fix_rows = features // lanes
    fix = jnp.pad(fix.reshape(fix_rows, lanes), ((0, EDGE - fix_rows), (0, 0)))
    if quick:
        swap = lambda x, bit: lax.ppermute(x, "dp", [(i, i ^ bit) for i in range(4)])
        turn = lambda x: lax.ppermute(x, "seq", [(0, 1), (1, 0)])
        half = rows_full // 2
        sides = (2, half, lanes)
        came = swap(packed[4:], 1)
        quarter = ((4, rows_full, lanes), lambda i, ids: (0, 0, 0))
        send_x, send_y, keep_x, keep_y = run_slabs(
            core_sum_kernel, ids, [(packed, quarter), (came, None)],
            [(sides, bf16, None)] * 2 + [(sides, f32, None)] * 2, [], 1,
        )
        left_x, left_y, send_y, send_x = run_slabs(
            side_sum_kernel,
            ids,
            [(x, None) for x in (keep_x, keep_y, swap(send_x, 2), turn(send_y))],
            [(sides[1:], f32, None)] * 2 + [(sides[1:], bf16, None)] * 2,
            [],
            1,
        )
        own_rkv, own_up, own_gate_up, own_head, shared = run_slabs(
            last_sum_kernel,
            ids,
            [(x, None) for x in (left_x, left_y, turn(send_y), swap(send_x, 2), fix)],
            [
                ((3 * part, lanes), f32, None),
                ((EDGE, lanes), f32, None),
                ((EDGE, lanes), f32, None),
                ((EDGE, lanes), f32, None),
                ((part + 2 * EDGE, lanes), bf16, None),
            ],
            [(rows_full, lanes)],
            1,
        )
    else:
        split_rows = lambda x: x.reshape(count, x.shape[0] // count, x.shape[1])
        wider = lambda x: jnp.pad(x.astype(bf16), ((0, 0), (0, 0), (0, lanes - x.shape[2])))
        head_grads = jnp.concatenate([row_grads[:4], row_grads_post[4:]], axis=0)
        grads = [
            split_rows(up_grads[:rank]),
            split_rows(up_grads[rank : 2 * rank]),
            split_rows(up_grads[2 * rank :]),
            feature_grad.reshape(16, count, part).transpose(1, 0, 2),
            head_grads.reshape(8, heads, count, head_part)
            .transpose(2, 0, 1, 3)
            .reshape(count, 8, heads * head_part),
        ]
        grads = jnp.concatenate([wider(x) for x in grads], axis=1)
        grads = jnp.pad(grads, ((0, 0), (0, rows_full - 4 * part - grads.shape[1]), (0, 0)))
        summed = lax.psum_scatter(
            jnp.concatenate([packed, grads], axis=1), group, scatter_dimension=0, tiled=False
        )
        own = lambda i, w: summed[edges[i] : edges[i + 1], :w].astype(f32)
        own_rkv, own_up, own_gate_up, own_head = own(0, width), own(2, width), own(3, width), own(5, lanes)
        shared = jnp.concatenate(
            [summed[edges[1] : edges[2]], summed[edges[4] : edges[5]], fix], axis=0
        )
    shared, large, stream_came = lax.optimization_barrier((shared, large, stream_came))
    shares = [shared] + [around(shared, by) for by in range(1, mp)]
    out_rows = large[hidden_here + lots * part :].reshape(mp, width, part)
    value_grad = large[:hidden_here].astype(f32)
    key_grad = large[hidden_here : hidden_here + lots * part].reshape(lots, part, part)
    key_grad = key_grad.transpose(1, 0, 2).reshape(part, lots * part).astype(f32)
    out_grad = scatter_shares(out_rows)
    input_grad = lax.dynamic_slice_in_dim(cot, share_at, share, 0) + sum(
        x.astype(f32) for x in stream_came
    )
    everywhere = run_slabs(
        functools.partial(share_sum_kernel, mp),
        ids,
        [(x, None) for x in shares],
        [(shared.shape, f32, None)],
        [(mp,) + shared.shape],
        1,
    )[0]
    down_sum = everywhere[:part]
    fix = everywhere[part + EDGE : part + EDGE + fix_rows].reshape(1, features)
    last = lax.broadcasted_iota(jnp.int32, (share, 1), 0) == share - 1
    input_grad = input_grad + jnp.where(last & (mp_here == mp - 1), fix, 0.0)
    return (
        block_out[None],
        input_grad[None],
        own_rkv.reshape(3, part, width),
        out_grad,
        jnp.stack([down_sum[:, :rank], down_sum[:, rank : 2 * rank]]),
        own_up.reshape(2, up_rows, width),
        down_sum[:, 2 * rank : low_width],
        own_gate_up,
        key_grad,
        value_grad,
        own_head[:7, : heads * head_part].reshape(7, heads, head_part),
        everywhere[part : part + 11, :part],
    )


def solution(mesh):
    both = ("dp", "seq")
    return jax.shard_map(
        body,
        mesh=mesh,
        in_specs=(
            P("dp", "seq", None),
            P(None, both, "mp"),
            P("mp", both),
            P(None, both, None),
            P(None, both, "mp"),
            P(both, None),
            P(both, "mp"),
            P(both, "mp"),
            P("mp", both),
            P(None, "mp", both),
            P(None, both),
            P("dp", "seq", None),
        ),
        out_specs=(
            P("dp", ("seq", "mp"), None),
            P("dp", ("seq", "mp"), None),
            P(None, both, "mp"),
            P("mp", both),
            P(None, both, None),
            P(None, both, "mp"),
            P(both, None),
            P(both, "mp"),
            P(both, "mp"),
            P("mp", both),
            P(None, "mp", both),
            P(None, both),
        ),
        check_vma=False,
    )
```

```python
import functools

import jax
import jax.numpy as jnp
from jax import lax
from jax.experimental import pallas as pl
from jax.experimental.pallas import tpu as pltpu
from jax.sharding import PartitionSpec as P


SPAN = 64
f32 = jnp.float32
bf16 = jnp.bfloat16


def halves(x):
    high = x.astype(bf16)
    return high, (x - high.astype(f32)).astype(bf16)


def dot(a, b, ca, cb):
    return lax.dot_general(a, b, (((ca,), (cb,)), ((), ())), preferred_element_type=f32)


def spread(x, mask):
    tiled = jnp.concatenate([x] * (x.shape[1] // SPAN), axis=0)
    return jnp.where(mask, tiled, jnp.zeros_like(tiled))


def fold(x, mask):
    x = jnp.where(mask, x, jnp.zeros_like(x))
    return sum(x[i * SPAN : (i + 1) * SPAN] for i in range(x.shape[0] // SPAN))


def times(a, b, mask, cb):
    return dot(a.astype(bf16), spread(b.astype(bf16), mask), 1, cb)


def fine(a, b, mask, cb):
    ah, al = halves(a)
    bh, bl = halves(b)
    rows = a.shape[0]
    both = dot(jnp.concatenate([ah, al], axis=0), spread(bh, mask), 1, cb)
    return both[:rows] + both[rows:] + dot(ah, spread(bl, mask), 1, cb)


def cross(a, b):
    return dot(a.astype(bf16), b.astype(bf16), 0, 0)


def fine_cross(a, b):
    ah, al = halves(a)
    bh, bl = halves(b)
    return dot(
        jnp.concatenate([ah, al, ah], axis=0), jnp.concatenate([bh, bh, bl], axis=0), 0, 0
    )


def exact_left(ones, x):
    high = x.astype(bf16)
    rest = x - high.astype(f32)
    mid = rest.astype(bf16)
    low = (rest - mid.astype(f32)).astype(bf16)
    return dot(ones, high, 1, 0) + dot(ones, mid, 1, 0) + dot(ones, low, 1, 0)


def head_sum(x, ones):
    high, low = halves(x)
    rows = x.shape[0]
    both = dot(jnp.concatenate([high, low], axis=0), ones, 1, 0)
    return both[:rows] + both[rows:]


def constants(width):
    iota = lax.broadcasted_iota
    big_row = iota(jnp.int32, (width, width), 0)
    big_col = iota(jnp.int32, (width, width), 1)
    mask = (big_row // SPAN) == (big_col // SPAN)
    t = iota(jnp.int32, (SPAN, SPAN), 0)
    s = iota(jnp.int32, (SPAN, SPAN), 1)
    row = iota(jnp.int32, (SPAN, width), 0)
    col = iota(jnp.int32, (SPAN, width), 1) % SPAN
    one = lambda where: jnp.where(where, 1.0, 0.0).astype(f32)
    return dict(
        mask=mask,
        diagonal=one(big_row == big_col),
        ones=one(mask).astype(bf16),
        lower=one(t >= s).astype(bf16),
        upper=one(t <= s).astype(bf16),
        strict=row > col,
        incl=row >= col,
        eye=one(row == col),
        near=(row // 4 == col // 4) & (row > col),
        mid=(row // 16 == col // 16) & (row // 4 > col // 4),
        far=row // 16 > col // 16,
    )


def ready(q, kp, din, rin, rows, c):
    sig = jax.nn.sigmoid(rows[0:1] + din)
    log_decay = -0.6065306597126334 * sig
    rate = jax.nn.sigmoid(rows[1:2] + rin)
    scaled = kp * rows[2:3]
    inv = lax.rsqrt(head_sum(scaled * scaled, c["ones"]) + 1e-6)
    unit = scaled * inv
    removal = unit * rate
    total = exact_left(c["lower"], log_decay)
    up = jnp.exp(total)
    down = jnp.exp(-total)
    before = jnp.exp(total - log_decay)
    return dict(
        sig=sig,
        log_decay=log_decay,
        rate=rate,
        inv=inv,
        unit=unit,
        up=up,
        down=down,
        before=before,
        Q=q * up,
        U=unit * before,
        K=kp * (1.0 + (rate - 1.0) * rows[3:4]) * down,
        R=removal * down,
        last=up[SPAN - 1 : SPAN],
    )


def inverse(lower, c):
    mask = c["mask"]
    zero = jnp.zeros_like(lower)
    inner = jnp.where(c["near"], lower, zero)
    square = fine(inner, inner, mask, 0)
    out = c["eye"] - inner + square - fine(inner, square, mask, 0)
    for level in ("mid", "far"):
        step = fine(out, jnp.where(c[level], lower, zero), mask, 0)
        step_two = fine(step, step, mask, 0)
        first = out - fine(step, out, mask, 0)
        out = first + fine(step_two, first, mask, 0)
    return out


def pairs(e, c):
    mask = c["mask"]
    zero = jnp.zeros((SPAN, mask.shape[0]), f32)
    queries = jnp.concatenate([e["U"], e["Q"]], axis=0)
    by_key = fine(queries, e["K"], mask, 1)
    by_removal = fine(queries, e["R"], mask, 1)
    return (
        jnp.where(c["strict"], by_key[:SPAN], zero),
        jnp.where(c["incl"], by_key[SPAN:], zero),
        jnp.where(c["strict"], by_removal[:SPAN], zero),
        jnp.where(c["incl"], by_removal[SPAN:], zero),
    )


def blocks_per_step(count):
    return 2 if count % 2 == 0 else 1


def local_kernel(per, q, kp, v, din, rin, rows_ref, local_out, read, push_map, push, inv_out,
                 uk_out, qk_out, qr_out, carry, maps, adds, map_end, add_end, map_now, add_now):
    width = q.shape[1]
    c = constants(width)
    rows = rows_ref[...]

    @pl.when(pl.program_id(0) == 0)
    def _():
        map_now[...] = c["eye"]
        add_now[...] = jnp.zeros_like(add_now)

    chain = []
    for i in range(per):
        at = slice(i * SPAN, (i + 1) * SPAN)
        e = ready(q[at, :], kp[at, :], din[at, :], rin[at, :], rows, c)
        uk, qk, ur, qr = pairs(e, c)
        inv = inverse(ur, c)
        values = v[at, :]
        mixed = fine(jnp.concatenate([uk, qk], axis=0), values, c["mask"], 0)
        y = fine(inv, mixed[:SPAN], c["mask"], 0)
        w = fine(inv, e["U"], c["mask"], 0)
        local_out[at, :] = mixed[SPAN:] - fine(qr, y, c["mask"], 0)
        read[at, :] = e["Q"] - fine(qr, w, c["mask"], 0)
        push_map[at, :] = w
        push[at, :] = y
        inv_out[at, :] = inv.astype(bf16)
        uk_out[at, :] = uk.astype(bf16)
        qk_out[at, :] = qk.astype(bf16)
        qr_out[at, :] = qr.astype(bf16)
        carried = jnp.where(c["mask"], fine_cross(w, e["R"]), jnp.zeros_like(c["diagonal"]))
        carry_here = ((c["diagonal"] - carried) * e["last"]).astype(bf16)
        carry[i * width : (i + 1) * width, :] = carry_here
        added = fold(
            fine_cross(
                jnp.concatenate([values, y], axis=0), jnp.concatenate([e["K"], -e["R"]], axis=0)
            ),
            c["mask"],
        ) * e["last"]
        chain.append((at, carry_here, added))
    state_map, state_add = map_now[...], add_now[...]
    for at, carry_here, added in chain:
        both = dot(
            jnp.concatenate([state_map, state_add], axis=0).astype(bf16), carry_here, 1, 0
        )
        state_map, state_add = both[:SPAN], both[SPAN:] + added
        maps[at, :] = state_map
        adds[at, :] = state_add
    map_now[...] = state_map
    add_now[...] = state_add
    map_end[...] = state_map
    add_end[...] = state_add


def normed(out, q, k, v, rows, c):
    ones = c["ones"]
    center = out - head_sum(out, ones) * (1.0 / SPAN)
    spread_here = head_sum(center * center, ones) * (1.0 / SPAN)
    scale = lax.rsqrt(spread_here + 0.00064)
    unit = center * scale
    extra = head_sum(q * k * rows[4:5], ones)
    return unit, scale, extra, unit * rows[5:6] + rows[6:7] + extra * v


def finish_kernel(per, q, kp, v, rin, gate, rows_ref, local_out, read, push_map, push, maps, adds,
                  state_in, gated, out_ref, push_out, starts, ends, state_now):
    c = constants(q.shape[1])
    rows = rows_ref[...]
    mask = c["mask"]

    @pl.when(pl.program_id(0) == 0)
    def _():
        state_now[...] = state_in[...]

    entering = state_in[...]
    state = state_now[...]
    for i in range(per):
        at = slice(i * SPAN, (i + 1) * SPAN)
        starts[at, :] = state
        both = fine(jnp.concatenate([read[at, :], push_map[at, :]], axis=0), state, mask, 1)
        out = local_out[at, :] + both[:SPAN]
        push_out[at, :] = push[at, :] + both[SPAN:]
        out_ref[at, :] = out
        rate = jax.nn.sigmoid(rows[1:2] + rin[at, :])
        k = kp[at, :] * (1.0 + (rate - 1.0) * rows[3:4])
        _, _, _, summed = normed(out, q[at, :], k, v[at, :], rows, c)
        gated[at, :] = (summed * gate[at, :]).astype(bf16)
        state = adds[at, :] + times(entering, maps[at, :], mask, 0)
        ends[at, :] = state
    state_now[...] = state


def reads_kernel(devices, per, q, kp, v, rin, gate, rows_ref, out_ref, read, carry, *refs):
    d_gated, fixes, refs = refs[:devices], refs[devices : 2 * devices], refs[2 * devices :]
    d_out, dq_post, dk_post, dv_post, d_gate, maps, adds, map_end, add_end, row_grads = refs[:10]
    map_now, add_now = refs[10:]
    width = q.shape[1]
    first_step = (pl.program_id(0) == 0).astype(f32)
    fix = sum(x[...].astype(f32) for x in fixes)[EDGE - 1 : EDGE] * first_step
    last_row = lax.broadcasted_iota(jnp.int32, (SPAN, width), 0) == SPAN - 1
    c = constants(width)
    rows = rows_ref[...]
    ones = c["ones"]

    @pl.when(pl.program_id(0) == 0)
    def _():
        map_now[...] = c["eye"]
        add_now[...] = jnp.zeros_like(add_now)
        row_grads[...] = jnp.zeros_like(row_grads)

    state_map, state_add = map_now[...], add_now[...]
    column = lambda x: jnp.sum(x, axis=0, keepdims=True)
    for i in reversed(range(per)):
        at = slice(i * SPAN, (i + 1) * SPAN)
        q_here, v_here, g_here = q[at, :], v[at, :], gate[at, :]
        rate = jax.nn.sigmoid(rows[1:2] + rin[at, :])
        k = kp[at, :] * (1.0 + (rate - 1.0) * rows[3:4])
        unit, scale, extra, summed = normed(out_ref[at, :], q_here, k, v_here, rows, c)
        grad = sum(x[at, :].astype(f32) for x in d_gated)
        if i == per - 1:
            grad = grad + jnp.where(last_row, fix, 0.0)
        d_gate[at, :] = (grad * summed).astype(bf16)
        d_sum = grad * g_here
        d_unit = d_sum * rows[5:6]
        d_here = scale * (
            d_unit
            - head_sum(d_unit, ones) * (1.0 / SPAN)
            - unit * head_sum(d_unit * unit, ones) * (1.0 / SPAN)
        )
        d_extra = head_sum(d_sum * v_here, ones)
        d_out[at, :] = d_here
        dq_post[at, :] = d_extra * k * rows[4:5]
        dk_post[at, :] = d_extra * q_here * rows[4:5]
        dv_post[at, :] = d_sum * extra
        row_grads[4:5, :] += column(d_extra * q_here * k)
        row_grads[5:6, :] += column(d_sum * unit)
        row_grads[6:7, :] += column(d_sum)
        maps[at, :] = state_map
        adds[at, :] = state_add
        carry_here = carry[i * width : (i + 1) * width, :]
        both = dot(
            jnp.concatenate([state_map, state_add], axis=0).astype(bf16), carry_here, 1, 1
        )
        state_map = both[:SPAN]
        state_add = both[SPAN:] + fold(cross(d_here, read[at, :]), c["mask"])
    map_now[...] = state_map
    add_now[...] = state_add
    map_end[...] = state_map
    add_end[...] = state_add


def grads_kernel(per, q, kp, v, din, rin, lat_ref, d_gate_ref, rows_ref, up_ref, push_ref, inv_ref, uk_ref, qk_ref, qr_ref,
                 starts, ends, d_out, dq_post, dk_post, dv_post, maps, adds, grad_in, dq_ref,
                 dkp_ref, dv_ref, pre_ref, row_grads, up_grads):
    c = constants(q.shape[1])
    up = up_ref[...]
    rows = rows_ref[...]
    mask, ones = c["mask"], c["ones"]
    cat = lambda *parts: jnp.concatenate(parts, axis=0)
    column = lambda x: jnp.sum(x, axis=0, keepdims=True)

    @pl.when(pl.program_id(0) == 0)
    def _():
        row_grads[...] = jnp.zeros_like(row_grads)
        up_grads[...] = jnp.zeros_like(up_grads)

    zero = jnp.zeros((SPAN, mask.shape[0]), f32)
    rank, gate_at = low_parts(up.shape[0])
    lane = lax.broadcasted_iota(jnp.int32, (SPAN, up.shape[0]), 1)
    low_row = lax.broadcasted_iota(jnp.int32, up_grads.shape, 0)
    for i in range(per):
        at = slice(i * SPAN, (i + 1) * SPAN)
        q_here, kp_here, v_here = q[at, :], kp[at, :], v[at, :]
        e = ready(q_here, kp_here, din[at, :], rin[at, :], rows, c)
        start, end, pushed, d_read = starts[at, :], ends[at, :], push_ref[at, :], d_out[at, :]
        grad_end = adds[at, :] + times(grad_in[...], maps[at, :], mask, 0)
        grown = grad_end * e["last"]
        by_state = times(cat(e["K"], e["R"]), grown, mask, 1)
        d_push = -fold(cross(qr_ref[at, :], d_read), mask) - by_state[SPAN:]
        d_rhs = fold(cross(inv_ref[at, :], d_push), mask)
        d_value = (
            by_state[:SPAN]
            + fold(cross(cat(qk_ref[at, :], uk_ref[at, :]), cat(d_read, d_rhs)), mask)
        )
        both = cat(d_rhs, d_read)
        by_value = times(both, v_here, mask, 1)
        by_push = times(both, pushed, mask, 1)
        d_key_pairs = cat(
            jnp.where(c["strict"], by_value[:SPAN], zero), jnp.where(c["incl"], by_value[SPAN:], zero)
        )
        d_removal_pairs = cat(
            jnp.where(c["strict"], -by_push[:SPAN], zero), jnp.where(c["incl"], -by_push[SPAN:], zero)
        )
        d_queries = (
            times(both, start, mask, 0)
            + times(d_key_pairs, e["K"], mask, 0)
            + times(d_removal_pairs, e["R"], mask, 0)
        )
        by_grown = times(cat(v_here, -pushed), grown, mask, 0)
        queries = cat(e["U"], e["Q"])
        d_k_grown = by_grown[:SPAN] + fold(cross(d_key_pairs, queries), mask)
        d_r_grown = by_grown[SPAN:] + fold(cross(d_removal_pairs, queries), mask)
        d_u_grown, d_q_grown = d_queries[:SPAN], d_queries[SPAN:]
        on_unit = d_u_grown * e["U"]
        steps = d_q_grown * e["Q"] - d_k_grown * e["K"] - d_r_grown * e["R"] + on_unit
        d_log = exact_left(c["upper"], steps) - on_unit + column(grad_end * end)
        rate = e["rate"]
        d_k = d_k_grown * e["down"] + dk_post[at, :]
        d_removal = d_r_grown * e["down"]
        d_unit = d_u_grown * e["before"] + d_removal * rate
        d_rate_value = d_removal * e["unit"] + d_k * kp_here * rows[3:4]
        d_scaled = e["inv"] * (d_unit - e["unit"] * head_sum(d_unit * e["unit"], ones))
        d_rate = d_rate_value * rate * (1.0 - rate)
        d_decay = d_log * e["log_decay"] * (1.0 - e["sig"])
        dq_ref[at, :] = (d_q_grown * e["up"] + dq_post[at, :]).astype(bf16)
        dkp_ref[at, :] = (d_k * (1.0 + (rate - 1.0) * rows[3:4]) + d_scaled * rows[2:3]).astype(bf16)
        dv_ref[at, :] = (d_value + dv_post[at, :]).astype(bf16)
        lat = lat_ref[at, :]
        low = lat.astype(bf16)
        d_outs = (d_decay.astype(bf16), d_rate.astype(bf16), d_gate_ref[at, :])
        pick = lambda where, parts: jnp.where(
            where < rank, parts[0], jnp.where(where < gate_at, parts[1], parts[2])
        )
        slope = pick(lane, (1.0 - lat * lat, jnp.ones_like(lat), lat * (1.0 - lat)))
        pre = pick(lane, [dot(x, up, 1, 1) for x in d_outs]) * slope
        pre_ref[at, :] = pre.astype(bf16)
        up_grads[...] += pick(low_row, [dot(low, x, 0, 0) for x in d_outs])
        row_grads[0:1, :] += column(d_decay)
        row_grads[1:2, :] += column(d_rate)
        row_grads[2:3, :] += column(d_scaled * kp_here)
        row_grads[3:4, :] += column(d_k * kp_here * (rate - 1.0))


def run_blocks(kernel, ins, outs, scratch, tokens, reverse=False):
    count = tokens // SPAN
    per = blocks_per_step(count)
    steps = count // per

    def spec(shape, cut):
        if not cut:
            return pl.BlockSpec(shape, lambda i: (0, 0))
        rows = shape[0] // steps
        if reverse:
            return pl.BlockSpec((rows, shape[1]), lambda i: (steps - 1 - i, 0))
        return pl.BlockSpec((rows, shape[1]), lambda i: (i, 0))

    return pl.pallas_call(
        functools.partial(kernel, per),
        grid=(steps,),
        in_specs=[spec(x.shape, cut) for x, cut in ins],
        out_specs=[spec(shape, cut) for shape, _, cut in outs],
        out_shape=[jax.ShapeDtypeStruct(shape, kind) for shape, kind, _ in outs],
        scratch_shapes=[pltpu.VMEM(shape, f32) for shape in scratch],
        compiler_params=pltpu.CompilerParams(dimension_semantics=("arbitrary",)),
        cost_estimate=pl.CostEstimate(flops=10**10, bytes_accessed=2 * 10**7, transcendentals=0),
    )(*[x for x, _ in ins])


def low_parts(width):
    return width // 4, width // 2


def mixed(unit, edge, norms, count):
    first = unit * norms[0:1] + norms[1:2]
    before = (edge[0:1] * norms[0:1] + norms[1:2]) * edge[1:2]
    row = lax.broadcasted_iota(jnp.int32, first.shape, 0)
    diff = jnp.where(row == 0, before, pltpu.roll(first, 1, 0)) - first
    return diff, [(first + diff * norms[4 + i : 5 + i]).astype(bf16) for i in range(count)]


def slab_weights(gathered, width):
    parts, rows, _ = gathered.shape
    part = rows // 4
    piece = lambda i, w: jnp.concatenate(
        [gathered[j, i * part : (i + 1) * part, :w] for j in range(parts)], axis=0
    )
    return [piece(i, width) for i in range(3)] + [piece(3, gathered.shape[2])]


def project_kernel(ids, unit, edge, norms, gathered, up, q, kp, v, din, rin, gate, lat, low_total):
    width = q.shape[1]
    step = pl.program_id(0)
    norms_here = norms[...]
    _, mixes = mixed(unit[...], edge[...], norms_here, 6)
    w_q, w_k, w_v, w_low = slab_weights(gathered, width)
    low_width = w_low.shape[1]
    rank, gate_at = low_parts(low_width)
    lane = lax.broadcasted_iota(jnp.int32, low_total.shape, 1)
    low = jnp.where(
        lane < rank,
        dot(mixes[1], w_low, 1, 0),
        jnp.where(lane < gate_at, dot(mixes[4], w_low, 1, 0), dot(mixes[5], w_low, 1, 0)),
    )

    @pl.when(step == 0)
    def _():
        q[...] = dot(mixes[0], w_q, 1, 0)
        kp[...] = dot(mixes[2], w_k, 1, 0)
        v[...] = dot(mixes[3], w_v, 1, 0)
        low_total[...] = low

    @pl.when(step > 0)
    def _():
        q[...] += dot(mixes[0], w_q, 1, 0)
        kp[...] += dot(mixes[2], w_k, 1, 0)
        v[...] += dot(mixes[3], w_v, 1, 0)
        low_total[...] += low

    @pl.when(step == pl.num_programs(0) - 1)
    def _():
        total = low_total[...]
        lats = jnp.where(
            lane < rank, jnp.tanh(total), jnp.where(lane < gate_at, total, jax.nn.sigmoid(total))
        )
        lat[...] = lats
        zero = jnp.zeros_like(lats)
        chosen = lambda where: jnp.where(where, lats, zero).astype(bf16)
        din[...] = dot(chosen(lane < rank), up[...], 1, 0)
        rin[...] = dot(chosen((lane >= rank) & (lane < gate_at)), up[...], 1, 0)
        gate[...] = dot(chosen(lane >= gate_at), up[...], 1, 0)


def unproject_kernel(quick, ids, unit, edge, scales, norms, gathered, dq, dkp, dv, pre, d_mid,
                     up_grads, second, rows_pre, rows_post, packed, feature, edge_fix, *rest):
    pieces, (all_first, all_unit) = rest[:-2], rest[-2:]
    block = lambda j: (j + ids[3]) % 2 if quick else j
    width = dq.shape[1]
    step = pl.program_id(0)
    n = norms[...]
    edge_here = edge[...]
    unit_here = unit[...]
    diff, mixes = mixed(unit_here, edge_here, n, 6)
    weights = slab_weights(gathered, width)
    w_low = weights[3]
    slab, low_width = w_low.shape
    rank, gate_at = low_parts(low_width)
    pre_here = pre[...]
    lane = lax.broadcasted_iota(jnp.int32, pre_here.shape, 1)
    none = jnp.zeros_like(pre_here)
    pres = [
        jnp.where(lane < rank, pre_here, none),
        jnp.where((lane >= rank) & (lane < gate_at), pre_here, none),
        jnp.where(lane >= gate_at, pre_here, none),
    ]
    sources = [(0, dq[...], 0), (2, dkp[...], 1), (3, dv[...], 2), (1, pres[0], 3), (4, pres[1], 3),
               (5, pres[2], 3)]
    low_lane = lax.broadcasted_iota(jnp.int32, (slab, low_width), 1)
    column = lambda x: jnp.sum(x, axis=0, keepdims=True)
    parts = gathered.shape[0]
    part = slab // parts
    direct = shifted = None
    low_grad = None
    for mix, grad, which in sources:
        weight_grad = dot(mixes[mix], grad, 0, 0)
        if which < 3:
            for j in range(parts):
                packed[block(j), which * part : (which + 1) * part, :width] = weight_grad[
                    j * part : (j + 1) * part
                ].astype(bf16)
                if width < low_width:
                    packed[block(j), which * part : (which + 1) * part, width:] = jnp.zeros(
                        (part, low_width - width), bf16
                    )
        else:
            low_grad = weight_grad if low_grad is None else low_grad + weight_grad
        d_mix = dot(grad, weights[which], 1, 1)
        feature[4 + mix : 5 + mix, :] = column(d_mix * diff)
        to_shift = d_mix * n[4 + mix : 5 + mix]
        shifted = to_shift if shifted is None else shifted + to_shift
        direct = d_mix - to_shift if direct is None else direct + (d_mix - to_shift)
    for j in range(parts):
        packed[block(j), 3 * part : 4 * part, :] = low_grad[j * part : (j + 1) * part].astype(bf16)
    tokens = unit_here.shape[0]
    row = lax.broadcasted_iota(jnp.int32, shifted.shape, 0)
    d_first = direct + jnp.where(row == tokens - 1, 0.0, pltpu.roll(shifted, tokens - 1, 0))
    before = shifted[0:1] * edge_here[1:2]
    feature[0:1, :] = column(d_first * unit_here) + before * edge_here[0:1]
    feature[1:2, :] = column(d_first) + before
    feature[2:4, :] = second[0:2, :]
    feature[10:11, :] = second[2:3, :]
    feature[11:, :] = jnp.zeros_like(feature[11:, :])
    if quick:
        up_rows, gate_rows = rank // (8), (low_width - gate_at) // 8
        head_part = width // SPAN * (SPAN // 8)
        row_grads = jnp.concatenate([rows_pre[0:4, :], rows_post[4:8, :]], axis=0)
        source = lax.broadcasted_iota(jnp.int32, (width, width), 0)
        target = lax.broadcasted_iota(jnp.int32, (width, width), 1)
        each = SPAN // 8
        for j in range(parts):
            dest = step * parts + j
            take = lambda at, size: up_grads[pl.ds(pl.multiple_of(at + dest * size, size), size), :]
            ups = jnp.concatenate([take(0, up_rows), take(rank, up_rows)], axis=0)
            chosen = (target // each * SPAN + dest * each + target % each == source) & (
                target < head_part
            )
            heads_here = dot(row_grads.astype(bf16), jnp.where(chosen, 1.0, 0.0).astype(bf16), 1, 0)
            values = feature[:, j * part : (j + 1) * part]
            at = 4 * part
            to = block(j)
            packed[to, at : at + EDGE, :] = ups.astype(bf16)
            packed[to, at + EDGE : at + 2 * EDGE, :] = take(gate_at, gate_rows).astype(bf16)
            packed[to, at + 2 * EDGE : at + 3 * EDGE, :] = jnp.concatenate(
                [values, jnp.zeros_like(values)], axis=1
            ).astype(bf16)
            packed[to, at + 3 * EDGE : at + 4 * EDGE, :] = jnp.concatenate(
                [heads_here, jnp.zeros_like(heads_here)], axis=0
            ).astype(bf16)
    at = pl.ds(pl.multiple_of(step * slab, slab), slab)
    all_first[:tokens, at] = d_first * n[0:1]
    all_first[tokens:, at] = jnp.broadcast_to(before * n[0:1], (8, slab))
    all_unit[:tokens, at] = unit_here
    all_unit[tokens:, at] = jnp.broadcast_to(edge_here[0:1], (8, slab))

    @pl.when(step == pl.num_programs(0) - 1)
    def _():
        d_unit = all_first[...]
        units = all_unit[...]
        features = d_unit.shape[1]
        mean = jnp.sum(d_unit, axis=1, keepdims=True) * (1.0 / features)
        along = jnp.sum(d_unit * units, axis=1, keepdims=True) * (1.0 / features)
        result = scales[...] * (d_unit - mean - units * along)
        edge_fix[...] = result[tokens:] + d_mid[tokens + EDGE - 8 :, :]
        all_first[:tokens, :] = result[:tokens] + d_mid[:tokens, :]
        send_pieces(pieces, all_first, ids[0])


EDGE = 16


def share_of(here, by, devices, size):
    return pl.ds(pl.multiple_of(lax.rem(here + by + devices, devices) * size, size), size)


def send_pieces(pieces, whole, here):
    share = pieces[0].shape[0]
    for by, piece in enumerate(pieces):
        piece[...] = whole[share_of(here, by, len(pieces), share), :].astype(piece.dtype)


def channel_kernel(devices, here, *refs):
    stream, edge_stream, has_edge, cot, norms, out_full, key, value = refs[:8]
    gated, edges = refs[8 : 8 + devices], refs[8 + devices : 8 + 2 * devices]
    refs = refs[8 + 2 * devices :]
    ffn_in, hidden, d_pre, cot_low, d_mid_low, d_mid, feature, middle_share = refs[:8]
    ffn_pieces, refs = refs[8 : 8 + devices], refs[8 + devices :]
    grad_pieces, refs = refs[:devices], refs[devices:]
    fix_pieces, refs = refs[:devices], refs[devices:]
    middle, unit, scale, diff, d_ffn, ffn_out = refs
    step = pl.program_id(0)
    tokens, features = stream.shape
    width = gated[0].shape[1]
    n = norms[...]
    flag = has_edge[0:1, 0:1]
    row = lax.broadcasted_iota(jnp.int32, (tokens + EDGE, features), 0)

    @pl.when(step == 0)
    def _():
        middle[:tokens, :] = stream[...]
        middle[tokens:, :] = edge_stream[...]
        for by in range(devices):
            rows = out_full[share_of(here[0], -by, devices, width), :]
            middle[:tokens, :] += dot(gated[by][...], rows, 1, 0)
            middle[tokens:, :] += dot(edges[by][...], rows, 1, 0)
        middle_share[...] = middle[share_of(here[0], 0, devices, tokens // devices), :]
        values = middle[...]
        center = values - jnp.sum(values, axis=1, keepdims=True) * (1.0 / features)
        spread_here = jnp.sum(center * center, axis=1, keepdims=True) * (1.0 / features)
        scale_here = lax.rsqrt(spread_here + 1e-05)
        unit_here = center * scale_here
        unit[...] = unit_here
        scale[...] = scale_here
        norm = unit_here * n[2:3] + n[3:4]
        before = pltpu.roll(norm, 1, 0)
        diff_here = jnp.where(row == 0, before * flag, before) - norm
        diff[...] = diff_here
        ffn_in[...] = (norm + diff_here * n[10:11])[:tokens].astype(bf16)
        cot_low[...] = cot[...].astype(bf16)
        d_ffn[...] = jnp.zeros_like(d_ffn)
        ffn_out[...] = jnp.zeros_like(ffn_out)

    act = jnp.maximum(dot(ffn_in[...], key[...], 1, 0), 0.0)
    hidden_here = (act * act).astype(bf16)
    hidden[...] = hidden_here
    d_pre_here = (dot(cot_low[...], value[...], 1, 1) * 2.0 * act).astype(bf16)
    d_pre[...] = d_pre_here
    d_ffn[:tokens, :] += dot(d_pre_here, key[...], 1, 1)
    ffn_out[...] += dot(hidden_here, value[...], 1, 0)

    @pl.when(step == pl.num_programs(0) - 1)
    def _():
        send_pieces(ffn_pieces, ffn_out, here[0])
        grad = d_ffn[...]
        to_shift = grad * n[10:11]
        moved = pltpu.roll(to_shift, tokens + EDGE - 1, 0)
        d_second = grad - to_shift + jnp.where(row == tokens + EDGE - 1, moved * flag, moved)
        unit_here = unit[...]
        column = lambda x: jnp.sum(x, axis=0, keepdims=True)
        feature[...] = jnp.zeros_like(feature)
        feature[0:1, :] = column(d_second * unit_here)
        feature[1:2, :] = column(d_second)
        feature[2:3, :] = column(grad * diff[...])
        d_unit = d_second * n[2:3]
        mean = jnp.sum(d_unit, axis=1, keepdims=True) * (1.0 / features)
        along = jnp.sum(d_unit * unit_here, axis=1, keepdims=True) * (1.0 / features)
        d_mid_here = scale[...] * (d_unit - mean - unit_here * along)
        d_mid[...] = d_mid_here
        d_mid_low[tokens:, :] = d_mid_here[tokens:].astype(bf16)
        d_mid_low[:tokens, :] = (d_mid_here[:tokens] + cot[...] * (1.0 / devices)).astype(bf16)
        for by in range(devices):
            rows = out_full[share_of(here[0], by, devices, width), :]
            grad_pieces[by][...] = dot(d_mid_low[:tokens, :], rows, 1, 1).astype(bf16)
            fix_pieces[by][...] = dot(d_mid_low[tokens:, :], rows, 1, 1).astype(bf16)


def large_kernel(devices, here, *refs):
    hidden, cot_low, ffn_in, d_pre, d_mid_low = refs[:5]
    gated, edges, large = refs[5 : 5 + devices], refs[5 + devices : 5 + 2 * devices], refs[-1]
    tokens, hidden_here = hidden.shape
    part = large.shape[2]
    width = gated[0].shape[1]
    large[0, :hidden_here, :] = dot(hidden[...], cot_low[...], 0, 0).astype(bf16)
    key_grad = dot(ffn_in[...], d_pre[...], 0, 0).astype(bf16)
    for j in range(hidden_here // part):
        at = hidden_here + j * part
        large[0, at : at + part, :] = key_grad[:, j * part : (j + 1) * part]
    grad, grad_edge = d_mid_low[:tokens, :], d_mid_low[tokens:, :]
    for by in range(devices):
        rows = dot(gated[by][...], grad, 0, 0) + dot(edges[by][...], grad_edge, 0, 0)
        at = lax.rem(here[0] - by + devices, devices) * width + 2 * hidden_here
        large[0, pl.ds(pl.multiple_of(at, width), width), :] = rows.astype(bf16)


def run_slabs(kernel, ids, ins, outs, scratch, slabs):
    def spec(shape, cut):
        shape = tuple(shape)
        if cut is None:
            return pl.BlockSpec(shape, lambda i, ids: (0,) * len(shape))
        if callable(cut[1]):
            return pl.BlockSpec(*cut)
        dim, size = cut
        block = list(shape)
        block[dim] = shape[dim] // slabs
        if size is not None:
            block[size[0]] = size[1]
        return pl.BlockSpec(
            tuple(block), lambda i, ids: tuple(i if k == dim else 0 for k in range(len(shape)))
        )

    return pl.pallas_call(
        kernel,
        grid_spec=pltpu.PrefetchScalarGridSpec(
            num_scalar_prefetch=1,
            grid=(slabs,),
            in_specs=[spec(x.shape, cut) for x, cut in ins],
            out_specs=[spec(shape, cut) for shape, _, cut in outs],
            scratch_shapes=[pltpu.VMEM(shape, f32) for shape in scratch],
        ),
        out_shape=[jax.ShapeDtypeStruct(shape, kind) for shape, kind, _ in outs],
        compiler_params=pltpu.CompilerParams(dimension_semantics=("arbitrary",)),
        cost_estimate=pl.CostEstimate(flops=10**10, bytes_accessed=2 * 10**7, transcendentals=0),
    )(ids, *[x for x, _ in ins])


def core_sum_kernel(ids, kept, came, send_x, send_y, keep_x, keep_y):
    half = send_x.shape[1]
    total = lambda i, rows: kept[i, rows, :].astype(f32) + came[i, rows, :].astype(f32)
    for y in range(2):
        keep_x[y] = total(y, slice(0, half))
        send_x[y] = total(2 + y, slice(0, half)).astype(bf16)
    for x in range(2):
        keep_y[x] = total(2 * x, slice(half, 2 * half))
        send_y[x] = total(2 * x + 1, slice(half, 2 * half)).astype(bf16)


def side_sum_kernel(ids, keep_x, keep_y, came_x, came_y, left_x, left_y, send_y, send_x):
    left_x[...] = keep_x[0] + came_x[0].astype(f32)
    left_y[...] = keep_y[0] + came_y[0].astype(f32)
    send_y[...] = (keep_x[1] + came_x[1].astype(f32)).astype(bf16)
    send_x[...] = (keep_y[1] + came_y[1].astype(f32)).astype(bf16)


def last_sum_kernel(ids, left_x, left_y, came_y, came_x, fix, rkv, up, gate_up, head, shared, whole):
    half = left_x.shape[0]
    whole[:half, :] = left_x[...] + came_y[...].astype(f32)
    whole[half:, :] = left_y[...] + came_x[...].astype(f32)
    first = rkv.shape[0]
    low = shared.shape[0] - 2 * EDGE
    rkv[...] = whole[:first, :]
    shared[:low, :] = whole[first : first + low, :].astype(bf16)
    at = first + low
    up[...] = whole[at : at + EDGE, :]
    gate_up[...] = whole[at + EDGE : at + 2 * EDGE, :]
    shared[low : low + EDGE, :] = whole[at + 2 * EDGE : at + 3 * EDGE, :].astype(bf16)
    head[...] = whole[at + 3 * EDGE :, :]
    shared[low + EDGE :, :] = fix[...]


def share_sum_kernel(devices, part, ids, *refs):
    pieces, stream, refs = refs[:devices], refs[devices], refs[devices + 1 :]
    down, gate_down, feature, input_grad, ordered = refs
    for by in range(devices):
        ordered[lax.rem(ids[0] - by + devices, devices)] = pieces[by][...].astype(f32)
    total = ordered[0]
    for i in range(1, devices):
        total = total + ordered[i]
    rank, gate_at = low_parts(total.shape[1])
    turned = total[:part, :gate_at].T
    down[0] = turned[:rank]
    down[1] = turned[rank:]
    gate_down[...] = total[:part, gate_at:]
    feature[...] = total[part : part + EDGE, :part]
    share, features = stream.shape
    lanes = total.shape[1]
    input_grad[...] = stream[...]
    ends = (ids[0] == devices - 1).astype(f32)
    for k in range(features // lanes):
        at = part + EDGE + k
        input_grad[share - 1 :, k * lanes : (k + 1) * lanes] += total[at : at + 1] * ends


def to_next(x, axis, by):
    devices = lax.axis_size(axis)
    pairs_here = [(i, i + by) for i in range(devices) if 0 <= i + by < devices]
    return lax.ppermute(x, axis, pairs_here)


def around(x, by):
    devices = lax.axis_size("mp")
    return lax.ppermute(x, "mp", [(i, (i + by) % devices) for i in range(devices)])


def slanted(x, along, by):
    rows, devices = lax.axis_size("seq"), lax.axis_size("mp")
    pairs_here = [
        (s * devices + i, (s + along) * devices + (i + by) % devices)
        for s in range(rows)
        if 0 <= s + along < rows
        for i in range(devices)
    ]
    return lax.ppermute(x, ("seq", "mp"), pairs_here)


def gather_shares(x):
    devices = lax.axis_size("mp")
    came = [x] + [around(x, by) for by in range(1, devices)]
    turned = jnp.stack([came[-k % devices] for k in range(devices)] * 2)
    at = (devices - lax.axis_index("mp")) % devices
    return lax.dynamic_slice_in_dim(turned, at, devices, 0)


def scatter_shares(x):
    devices = lax.axis_size("mp")
    here = lax.axis_index("mp")
    term = lambda at: lax.dynamic_index_in_dim(x, at % devices, 0, keepdims=False)
    total = term(here).astype(f32)
    for by in range(1, devices):
        total = total + around(term(here + by), by).astype(f32)
    return total


def mm_left(a, b):
    return dot(a, b, 0, 0)


def statistics(values):
    center = values - jnp.mean(values, axis=-1, keepdims=True)
    scale = lax.rsqrt(jnp.mean(center * center, axis=-1, keepdims=True) + 1e-05)
    return center * scale, scale


def carry_states(state_map, state_add, by):
    entering = to_next(state_add.astype(bf16), "seq", by).astype(f32)
    heads = state_map.shape[1] // SPAN
    apart = lambda x: x.reshape(SPAN, heads, SPAN).transpose(1, 0, 2)
    for _ in range(lax.axis_size("seq") - 2):
        moved = jnp.einsum("hij,hjl->hil", apart(entering), apart(state_map), precision="highest")
        passed = moved.transpose(1, 0, 2).reshape(state_add.shape) + state_add
        entering = to_next(passed.astype(bf16), "seq", by).astype(f32)
    return entering


def wide(x, width):
    return jnp.pad(x, ((0, 0), (0, width - x.shape[1])))


def body(inputs, rkv_weight, output_weight, first_factors, second_factors, gate_first, gate_second,
         key_weight, value_weight, head_table, feature_table, cotangent):
    group = ("dp", "seq")
    count = lax.axis_size("dp") * lax.axis_size("seq")
    mp = lax.axis_size("mp")
    mp_here = lax.axis_index("mp")
    stream = inputs[0]
    cot = cotangent[0]
    tokens, features = stream.shape
    share = tokens // mp
    share_at = mp_here * share
    part = features // count
    width = rkv_weight.shape[2]
    heads = width // SPAN
    rank, gate_rank = first_factors.shape[2], gate_first.shape[1]
    low_width = 2 * rank + gate_rank
    lanes = max(width, low_width, part)
    up_rows = second_factors.shape[1]
    head_part = head_table.shape[2]
    dp_here, seq_here = lax.axis_index("dp"), lax.axis_index("seq")
    quick = lax.axis_size("dp") == 4 and lax.axis_size("seq") == 2 and part == 128 and width == 256
    ids = jnp.stack([mp_here, dp_here // 2, dp_here % 2, seq_here]).astype(jnp.int32)
    edge_stream = to_next(stream[-EDGE:], "seq", 1)
    edge_row = edge_stream[EDGE - 1 :]
    pieces = [
        wide(rkv_weight.reshape(3 * part, width), lanes),
        wide(jnp.concatenate([first_factors[0], first_factors[1], gate_first], axis=1), lanes),
        wide(second_factors.reshape(2 * up_rows, width), lanes),
        wide(gate_second, lanes),
        jnp.pad(wide(feature_table, lanes), ((0, 5), (0, 0))),
        jnp.pad(wide(head_table.reshape(7, heads * head_part), lanes), ((0, 9), (0, 0))),
    ]
    edges = [0]
    for piece in pieces:
        edges.append(edges[-1] + piece.shape[0])
    packed = jnp.concatenate(pieces, axis=0)
    rows_full = -(-packed.shape[0] // 16) * 16
    packed = jnp.pad(packed, ((0, rows_full - packed.shape[0]), (0, 0)))
    gathered = lax.all_gather(packed, group, axis=0, tiled=False)
    cut = lambda i, w: gathered[:, edges[i] : edges[i + 1], :w]
    up = cut(2, width).reshape(count, 2, up_rows, width).transpose(1, 0, 2, 3)
    up = jnp.concatenate(
        [up.reshape(2 * rank, width), cut(3, width).reshape(gate_rank, width)], axis=0
    )
    norms = cut(4, part).transpose(1, 0, 2).reshape(16, features).astype(f32)
    head_rows = (
        cut(5, heads * head_part)[:, :7]
        .reshape(count, 7, heads, head_part)
        .transpose(1, 2, 0, 3)
        .reshape(7, width)
        .astype(f32)
    )
    head_rows = jnp.pad(head_rows, ((0, 1), (0, 0)))

    out_column = gather_shares(output_weight).reshape(features, part)
    rest = lax.all_gather(
        jnp.concatenate([value_weight, out_column], axis=0), group, axis=0, tiled=False
    )
    hidden_here = value_weight.shape[0]
    key_full = lax.all_gather(key_weight, group, axis=0, tiled=True)

    unit_one, scale_one = statistics(stream)
    edge_unit, edge_scale = statistics(edge_row)
    has_edge = (lax.axis_index("seq") > 0).astype(f32)
    edge = jnp.concatenate(
        [edge_unit, jnp.broadcast_to(has_edge, (1, features)), jnp.zeros((6, features), f32)]
    )
    slab = max(256, part)
    slabs = features // slab
    in_slabs = (1, None)
    of_gathered = (0, (1, 4 * part))
    whole = (tokens, width)
    q, kp, v, din, rin, gate, lat = run_slabs(
        project_kernel,
        ids,
        [(unit_one, in_slabs), (edge, in_slabs), (norms, in_slabs), (gathered, of_gathered), (up, None)],
        [(whole, f32, None)] * 6 + [((tokens, low_width), f32, None)],
        [(tokens, low_width)],
        slabs,
    )

    state = (SPAN, width)
    (local_out, read, push_map, push, inv, uk, qk, qr, carry, maps, adds, map_end, add_end) = run_blocks(
        local_kernel,
        [(q, True), (kp, True), (v, True), (din, True), (rin, True), (head_rows, False)],
        [(whole, f32, True)] * 4
        + [(whole, bf16, True)] * 4
        + [((tokens // SPAN * width, width), bf16, True)]
        + [(whole, f32, True)] * 2
        + [(state, f32, False)] * 2,
        [state, state],
        tokens,
    )
    entering = carry_states(map_end, add_end, 1)
    gated, read_out, pushed, starts, ends = run_blocks(
        finish_kernel,
        [(x, True) for x in (q, kp, v, rin, gate)]
        + [(head_rows, False)]
        + [(x, True) for x in (local_out, read, push_map, push, maps, adds)]
        + [(entering, False)],
        [(whole, bf16, True)] + [(whole, f32, True)] * 4,
        [state],
        tokens,
    )

    edge_parts = [slanted(gated[-EDGE:], 1, by) for by in range(mp)]
    gated_parts = [gated] + [around(gated, by) for by in range(1, mp)]
    value_full = rest[:, :hidden_here].transpose(1, 0, 2).reshape(hidden_here, features)
    out_full = rest[:, hidden_here:].transpose(1, 0, 2).reshape(features, features)
    longer = tokens + EDGE
    lots = key_full.shape[1] // part
    channel = run_slabs(
        functools.partial(channel_kernel, mp),
        ids,
        [(stream, None), (edge_stream, None), (edge[1:2, :128], None), (cot, None)]
        + [(norms, None), (out_full, None), (key_full, (1, None)), (value_full, (0, None))]
        + [(x, None) for x in gated_parts + edge_parts],
        [
            ((tokens, features), bf16, None),
            ((tokens, hidden_here), bf16, (1, None)),
            ((tokens, hidden_here), bf16, (1, None)),
            ((tokens, features), bf16, None),
            ((longer, features), bf16, None),
            ((longer, features), f32, None),
            ((8, features), f32, None),
            ((share, features), f32, None),
        ]
        + [((share, features), bf16, None)] * mp
        + [(whole, bf16, None)] * mp
        + [((EDGE, width), bf16, None)] * mp,
        [(longer, features)] * 2
        + [(longer, 1)]
        + [(longer, features)] * 2
        + [(tokens, features)],
        max(1, hidden_here // 256),
    )
    ffn_in, hidden, d_pre, cot_low, d_mid_low, d_mid, second_rows, middle_share = channel[:8]
    ffn_pieces = channel[8 : 8 + mp]
    grad_pieces = channel[8 + mp : 8 + 2 * mp]
    fix_pieces = channel[8 + 2 * mp :]
    fixes = []
    for by in range(mp):
        fixes.append(slanted(fix_pieces[by], -1, by))
    d_gated = [grad_pieces[0]]
    for by in range(1, mp):
        d_gated.append(around(grad_pieces[by], by))

    if part % 128 == 0:
        large = run_slabs(
            functools.partial(large_kernel, mp),
            ids,
            [(hidden, None), (cot_low, (1, None)), (ffn_in, (1, None)), (d_pre, None)]
            + [(d_mid_low, (1, None))]
            + [(x, None) for x in gated_parts + edge_parts],
            [((count, 2 * hidden_here + features, part), bf16, (0, None))],
            [],
            count,
        )[0]
    else:
        by_part = lambda x: x.astype(bf16).reshape(x.shape[0], count, part).transpose(1, 0, 2)
        key_grad = mm_left(ffn_in, d_pre).astype(bf16)
        key_grad = key_grad.reshape(count, part, lots, part).transpose(0, 2, 1, 3)
        order = lambda parts: jnp.concatenate(parts[:1] + parts[:0:-1], axis=0)
        out_rows = order([mm_left(x, d_mid_low[:tokens]) for x in gated_parts]) + order(
            [mm_left(x, d_mid_low[tokens:]) for x in edge_parts]
        )
        large = jnp.concatenate(
            [
                by_part(mm_left(hidden, cot_low)),
                key_grad.reshape(count, lots * part, part),
                by_part(jnp.roll(out_rows, mp_here * width, axis=0)),
            ],
            axis=1,
        )
    large = lax.psum_scatter(large, group, scatter_dimension=0, tiled=False)
    d_gated, ffn_pieces = lax.optimization_barrier((d_gated, ffn_pieces))
    block_out = middle_share + ffn_pieces[0].astype(f32)
    for by in range(1, mp):
        came = around(ffn_pieces[by], by)
        block_out = block_out + came.astype(f32)

    (d_read, dq_post, dk_post, dv_post, d_gate, back_maps, back_adds, back_map_end, back_add_end,
     row_grads_post) = run_blocks(
        functools.partial(reads_kernel, mp),
        [(x, True) for x in (q, kp, v, rin, gate)]
        + [(head_rows, False)]
        + [(x, True) for x in (read_out, read, carry)]
        + [(x, True) for x in d_gated]
        + [(x, False) for x in fixes],
        [(whole, f32, True)] * 4
        + [(whole, bf16, True)]
        + [(whole, f32, True)] * 2
        + [(state, f32, False)] * 2
        + [((8, width), f32, False)],
        [state, state],
        tokens,
        reverse=True,
    )
    grad_in = carry_states(back_map_end, back_add_end, -1)
    dq, dkp, dv, pre, row_grads, up_grads = run_blocks(
        grads_kernel,
        [(x, True) for x in (q, kp, v, din, rin, lat, d_gate)]
        + [(head_rows, False), (up, False)]
        + [
            (x, True)
            for x in (pushed, inv, uk, qk, qr, starts, ends, d_read, dq_post, dk_post, dv_post,
                      back_maps, back_adds)
        ]
        + [(grad_in, False)],
        [(whole, bf16, True)] * 3
        + [((tokens, low_width), bf16, True), ((8, width), f32, False)]
        + [((low_width, width), f32, False)],
        [],
        tokens,
    )

    scales = jnp.concatenate([scale_one, jnp.broadcast_to(edge_scale, (8, 1))], axis=0)
    packed_rows = rows_full if quick else 4 * part
    whose = lambda i, ids: (((i + ids[2]) % 2) * 2 + (i // 2 + ids[1]) % 2, 0, 0)
    unprojected = run_slabs(
        functools.partial(unproject_kernel, quick),
        ids,
        [(unit_one, in_slabs), (edge, in_slabs), (scales, None), (norms, in_slabs)]
        + [(gathered, of_gathered), (dq, None), (dkp, None), (dv, None), (pre, None), (d_mid, None)]
        + [(up_grads, None), (second_rows, in_slabs), (row_grads, None), (row_grads_post, None)],
        [
            (
                (count, packed_rows, lanes),
                bf16,
                ((2, packed_rows, lanes), whose) if quick else (0, None),
            ),
            ((16, features), f32, in_slabs),
            ((8, features), f32, None),
        ]
        + [((share, features), bf16, None)] * mp,
        [(tokens + 8, features)] * 2,
        slabs,
    )
    packed, feature_grad, edge_fix = unprojected[:3]
    stream_pieces = unprojected[3:]
    fix = to_next(edge_fix[7:].astype(bf16), "seq", -1)
    stream_came = [stream_pieces[0]]
    for by in range(1, mp):
        stream_came.append(around(stream_pieces[by], by))
    fix_rows = features // lanes
    fix = jnp.pad(fix.reshape(fix_rows, lanes), ((0, EDGE - fix_rows), (0, 0)))

    def settle(large):
        key_grad = large[hidden_here : hidden_here + lots * part].reshape(lots, part, part)
        return (
            large[:hidden_here].astype(f32),
            key_grad.transpose(1, 0, 2).reshape(part, lots * part).astype(f32),
            scatter_shares(large[hidden_here + lots * part :].reshape(mp, width, part)),
        )

    if quick:
        swap = lambda x, bit: lax.ppermute(x, "dp", [(i, i ^ bit) for i in range(4)])
        turn = lambda x: lax.ppermute(x, "seq", [(0, 1), (1, 0)])
        half = rows_full // 2
        sides = (2, half, lanes)
        came = swap(packed[4:], 1)
        quarter = ((4, rows_full, lanes), lambda i, ids: (0, 0, 0))
        send_x, send_y, keep_x, keep_y = run_slabs(
            core_sum_kernel, ids, [(packed, quarter), (came, None)],
            [(sides, bf16, None)] * 2 + [(sides, f32, None)] * 2, [], 1,
        )
        keep_x, large = lax.optimization_barrier((keep_x, large))
        settled = settle(large)
        left_x, left_y, send_y, send_x = run_slabs(
            side_sum_kernel,
            ids,
            [(x, None) for x in (keep_x, keep_y, swap(send_x, 2), turn(send_y))],
            [(sides[1:], f32, None)] * 2 + [(sides[1:], bf16, None)] * 2,
            [],
            1,
        )
        left_x, settled = lax.optimization_barrier((left_x, settled))
        own_rkv, own_up, own_gate_up, own_head, shared = run_slabs(
            last_sum_kernel,
            ids,
            [(x, None) for x in (left_x, left_y, turn(send_y), swap(send_x, 2), fix)],
            [
                ((3 * part, lanes), f32, None),
                ((EDGE, lanes), f32, None),
                ((EDGE, lanes), f32, None),
                ((EDGE, lanes), f32, None),
                ((part + 2 * EDGE, lanes), bf16, None),
            ],
            [(rows_full, lanes)],
            1,
        )
    else:
        split_rows = lambda x: x.reshape(count, x.shape[0] // count, x.shape[1])
        wider = lambda x: jnp.pad(x.astype(bf16), ((0, 0), (0, 0), (0, lanes - x.shape[2])))
        head_grads = jnp.concatenate([row_grads[:4], row_grads_post[4:]], axis=0)
        grads = [
            split_rows(up_grads[:rank]),
            split_rows(up_grads[rank : 2 * rank]),
            split_rows(up_grads[2 * rank :]),
            feature_grad.reshape(16, count, part).transpose(1, 0, 2),
            head_grads.reshape(8, heads, count, head_part)
            .transpose(2, 0, 1, 3)
            .reshape(count, 8, heads * head_part),
        ]
        grads = jnp.concatenate([wider(x) for x in grads], axis=1)
        grads = jnp.pad(grads, ((0, 0), (0, rows_full - 4 * part - grads.shape[1]), (0, 0)))
        summed = lax.psum_scatter(
            jnp.concatenate([packed, grads], axis=1), group, scatter_dimension=0, tiled=False
        )
        own = lambda i, w: summed[edges[i] : edges[i + 1], :w].astype(f32)
        own_rkv, own_up, own_gate_up, own_head = own(0, width), own(2, width), own(3, width), own(5, lanes)
        shared = jnp.concatenate(
            [summed[edges[1] : edges[2]], summed[edges[4] : edges[5]], fix], axis=0
        )
        settled = settle(large)
    value_grad, key_grad, out_grad = settled
    input_grad = lax.dynamic_slice_in_dim(cot, share_at, share, 0) + sum(
        x.astype(f32) for x in stream_came
    )
    down_grad, gate_down_grad, feature_out, input_grad = run_slabs(
        functools.partial(share_sum_kernel, mp, part),
        ids,
        [(x, None) for x in [shared] + [around(shared, by) for by in range(1, mp)]]
        + [(input_grad, None)],
        [
            ((2, rank, part), f32, None),
            ((part, gate_rank), f32, None),
            ((EDGE, part), f32, None),
            ((share, features), f32, None),
        ],
        [(mp,) + shared.shape],
        1,
    )
    return (
        block_out[None],
        input_grad[None],
        own_rkv.reshape(3, part, width),
        out_grad,
        down_grad.transpose(0, 2, 1),
        own_up.reshape(2, up_rows, width),
        gate_down_grad,
        own_gate_up,
        key_grad,
        value_grad,
        own_head[:7, : heads * head_part].reshape(7, heads, head_part),
        feature_out[:11],
    )


def solution(mesh):
    both = ("dp", "seq")
    return jax.shard_map(
        body,
        mesh=mesh,
        in_specs=(
            P("dp", "seq", None),
            P(None, both, "mp"),
            P("mp", both),
            P(None, both, None),
            P(None, both, "mp"),
            P(both, None),
            P(both, "mp"),
            P(both, "mp"),
            P("mp", both),
            P(None, "mp", both),
            P(None, both),
            P("dp", "seq", None),
        ),
        out_specs=(
            P("dp", ("seq", "mp"), None),
            P("dp", ("seq", "mp"), None),
            P(None, both, "mp"),
            P("mp", both),
            P(None, both, None),
            P(None, both, "mp"),
            P(both, None),
            P(both, "mp"),
            P(both, "mp"),
            P("mp", both),
            P(None, "mp", both),
            P(None, both),
        ),
        check_vma=False,
    )
```

```python
import functools

import jax
import jax.numpy as jnp
from jax import lax
from jax.experimental import pallas as pl
from jax.experimental.pallas import tpu as pltpu
from jax.sharding import PartitionSpec as P


SPAN = 64
f32 = jnp.float32
bf16 = jnp.bfloat16


def halves(x):
    high = x.astype(bf16)
    return high, (x - high.astype(f32)).astype(bf16)


def dot(a, b, ca, cb):
    return lax.dot_general(a, b, (((ca,), (cb,)), ((), ())), preferred_element_type=f32)


def spread(x, mask):
    tiled = jnp.concatenate([x] * (x.shape[1] // SPAN), axis=0)
    return jnp.where(mask, tiled, jnp.zeros_like(tiled))


def fold(x, mask):
    x = jnp.where(mask, x, jnp.zeros_like(x))
    return sum(x[i * SPAN : (i + 1) * SPAN] for i in range(x.shape[0] // SPAN))


def times(a, b, mask, cb):
    return dot(a.astype(bf16), spread(b.astype(bf16), mask), 1, cb)


def fine(a, b, mask, cb):
    ah, al = halves(a)
    bh, bl = halves(b)
    rows = a.shape[0]
    both = dot(jnp.concatenate([ah, al], axis=0), spread(bh, mask), 1, cb)
    return both[:rows] + both[rows:] + dot(ah, spread(bl, mask), 1, cb)


def cross(a, b):
    return dot(a.astype(bf16), b.astype(bf16), 0, 0)


def fine_cross(a, b):
    ah, al = halves(a)
    bh, bl = halves(b)
    return dot(
        jnp.concatenate([ah, al, ah], axis=0), jnp.concatenate([bh, bh, bl], axis=0), 0, 0
    )


def exact_left(ones, x):
    high = x.astype(bf16)
    rest = x - high.astype(f32)
    mid = rest.astype(bf16)
    low = (rest - mid.astype(f32)).astype(bf16)
    return dot(ones, high, 1, 0) + dot(ones, mid, 1, 0) + dot(ones, low, 1, 0)


def head_sum(x, ones):
    high, low = halves(x)
    rows = x.shape[0]
    both = dot(jnp.concatenate([high, low], axis=0), ones, 1, 0)
    return both[:rows] + both[rows:]


def constants(width):
    iota = lax.broadcasted_iota
    big_row = iota(jnp.int32, (width, width), 0)
    big_col = iota(jnp.int32, (width, width), 1)
    mask = (big_row // SPAN) == (big_col // SPAN)
    t = iota(jnp.int32, (SPAN, SPAN), 0)
    s = iota(jnp.int32, (SPAN, SPAN), 1)
    row = iota(jnp.int32, (SPAN, width), 0)
    col = iota(jnp.int32, (SPAN, width), 1) % SPAN
    one = lambda where: jnp.where(where, 1.0, 0.0).astype(f32)
    return dict(
        mask=mask,
        diagonal=one(big_row == big_col),
        ones=one(mask).astype(bf16),
        lower=one(t >= s).astype(bf16),
        upper=one(t <= s).astype(bf16),
        strict=row > col,
        incl=row >= col,
        eye=one(row == col),
        near=(row // 4 == col // 4) & (row > col),
        mid=(row // 16 == col // 16) & (row // 4 > col // 4),
        far=row // 16 > col // 16,
    )


def ready(q, kp, din, rin, rows, c):
    sig = jax.nn.sigmoid(rows[0:1] + din)
    log_decay = -0.6065306597126334 * sig
    rate = jax.nn.sigmoid(rows[1:2] + rin)
    scaled = kp * rows[2:3]
    inv = lax.rsqrt(head_sum(scaled * scaled, c["ones"]) + 1e-6)
    unit = scaled * inv
    removal = unit * rate
    total = exact_left(c["lower"], log_decay)
    up = jnp.exp(total)
    down = jnp.exp(-total)
    before = jnp.exp(total - log_decay)
    return dict(
        sig=sig,
        log_decay=log_decay,
        rate=rate,
        inv=inv,
        unit=unit,
        up=up,
        down=down,
        before=before,
        Q=q * up,
        U=unit * before,
        K=kp * (1.0 + (rate - 1.0) * rows[3:4]) * down,
        R=removal * down,
        last=up[SPAN - 1 : SPAN],
    )


def inverse(lower, c):
    mask = c["mask"]
    zero = jnp.zeros_like(lower)
    inner = jnp.where(c["near"], lower, zero)
    square = fine(inner, inner, mask, 0)
    out = c["eye"] - inner + square - fine(inner, square, mask, 0)
    for level in ("mid", "far"):
        step = fine(out, jnp.where(c[level], lower, zero), mask, 0)
        step_two = fine(step, step, mask, 0)
        first = out - fine(step, out, mask, 0)
        out = first + fine(step_two, first, mask, 0)
    return out


def pairs(e, c):
    mask = c["mask"]
    zero = jnp.zeros((SPAN, mask.shape[0]), f32)
    queries = jnp.concatenate([e["U"], e["Q"]], axis=0)
    by_key = fine(queries, e["K"], mask, 1)
    by_removal = fine(queries, e["R"], mask, 1)
    return (
        jnp.where(c["strict"], by_key[:SPAN], zero),
        jnp.where(c["incl"], by_key[SPAN:], zero),
        jnp.where(c["strict"], by_removal[:SPAN], zero),
        jnp.where(c["incl"], by_removal[SPAN:], zero),
    )


def blocks_per_step(count):
    return 2 if count % 2 == 0 else 1


def local_kernel(per, q, kp, v, din, rin, rows_ref, local_out, read, push_map, push, inv_out,
                 uk_out, qk_out, qr_out, carry, maps, adds, map_end, add_end, map_now, add_now):
    width = q.shape[1]
    c = constants(width)
    rows = rows_ref[...]

    @pl.when(pl.program_id(0) == 0)
    def _():
        map_now[...] = c["eye"]
        add_now[...] = jnp.zeros_like(add_now)

    chain = []
    for i in range(per):
        at = slice(i * SPAN, (i + 1) * SPAN)
        e = ready(q[at, :], kp[at, :], din[at, :], rin[at, :], rows, c)
        uk, qk, ur, qr = pairs(e, c)
        inv = inverse(ur, c)
        values = v[at, :]
        mixed = fine(jnp.concatenate([uk, qk], axis=0), values, c["mask"], 0)
        y = fine(inv, mixed[:SPAN], c["mask"], 0)
        w = fine(inv, e["U"], c["mask"], 0)
        local_out[at, :] = mixed[SPAN:] - fine(qr, y, c["mask"], 0)
        read[at, :] = e["Q"] - fine(qr, w, c["mask"], 0)
        push_map[at, :] = w
        push[at, :] = y
        inv_out[at, :] = inv.astype(bf16)
        uk_out[at, :] = uk.astype(bf16)
        qk_out[at, :] = qk.astype(bf16)
        qr_out[at, :] = qr.astype(bf16)
        carried = jnp.where(c["mask"], fine_cross(w, e["R"]), jnp.zeros_like(c["diagonal"]))
        carry_here = ((c["diagonal"] - carried) * e["last"]).astype(bf16)
        carry[i * width : (i + 1) * width, :] = carry_here
        added = fold(
            fine_cross(
                jnp.concatenate([values, y], axis=0), jnp.concatenate([e["K"], -e["R"]], axis=0)
            ),
            c["mask"],
        ) * e["last"]
        chain.append((at, carry_here, added))
    state_map, state_add = map_now[...], add_now[...]
    for at, carry_here, added in chain:
        both = dot(
            jnp.concatenate([state_map, state_add], axis=0).astype(bf16), carry_here, 1, 0
        )
        state_map, state_add = both[:SPAN], both[SPAN:] + added
        maps[at, :] = state_map
        adds[at, :] = state_add
    map_now[...] = state_map
    add_now[...] = state_add
    map_end[...] = state_map
    add_end[...] = state_add


def normed(out, q, k, v, rows, c):
    ones = c["ones"]
    center = out - head_sum(out, ones) * (1.0 / SPAN)
    spread_here = head_sum(center * center, ones) * (1.0 / SPAN)
    scale = lax.rsqrt(spread_here + 0.00064)
    unit = center * scale
    extra = head_sum(q * k * rows[4:5], ones)
    return unit, scale, extra, unit * rows[5:6] + rows[6:7] + extra * v


def finish_kernel(per, q, kp, v, rin, gate, rows_ref, local_out, read, push_map, push, maps, adds,
                  state_in, gated, out_ref, push_out, starts, ends, state_now):
    c = constants(q.shape[1])
    rows = rows_ref[...]
    mask = c["mask"]

    @pl.when(pl.program_id(0) == 0)
    def _():
        state_now[...] = state_in[...]

    entering = state_in[...]
    state = state_now[...]
    for i in range(per):
        at = slice(i * SPAN, (i + 1) * SPAN)
        starts[at, :] = state
        both = fine(jnp.concatenate([read[at, :], push_map[at, :]], axis=0), state, mask, 1)
        out = local_out[at, :] + both[:SPAN]
        push_out[at, :] = push[at, :] + both[SPAN:]
        out_ref[at, :] = out
        rate = jax.nn.sigmoid(rows[1:2] + rin[at, :])
        k = kp[at, :] * (1.0 + (rate - 1.0) * rows[3:4])
        _, _, _, summed = normed(out, q[at, :], k, v[at, :], rows, c)
        gated[at, :] = (summed * gate[at, :]).astype(bf16)
        state = adds[at, :] + times(entering, maps[at, :], mask, 0)
        ends[at, :] = state
    state_now[...] = state


def reads_kernel(devices, per, q, kp, v, rin, gate, rows_ref, out_ref, read, carry, *refs):
    d_gated, fixes, refs = refs[:devices], refs[devices : 2 * devices], refs[2 * devices :]
    d_out, dq_post, dk_post, dv_post, d_gate, maps, adds, map_end, add_end, row_grads = refs[:10]
    map_now, add_now = refs[10:]
    width = q.shape[1]
    first_step = (pl.program_id(0) == 0).astype(f32)
    fix = sum(x[...].astype(f32) for x in fixes)[EDGE - 1 : EDGE] * first_step
    last_row = lax.broadcasted_iota(jnp.int32, (SPAN, width), 0) == SPAN - 1
    c = constants(width)
    rows = rows_ref[...]
    ones = c["ones"]

    @pl.when(pl.program_id(0) == 0)
    def _():
        map_now[...] = c["eye"]
        add_now[...] = jnp.zeros_like(add_now)
        row_grads[...] = jnp.zeros_like(row_grads)

    state_map, state_add = map_now[...], add_now[...]
    column = lambda x: jnp.sum(x, axis=0, keepdims=True)
    for i in reversed(range(per)):
        at = slice(i * SPAN, (i + 1) * SPAN)
        q_here, v_here, g_here = q[at, :], v[at, :], gate[at, :]
        rate = jax.nn.sigmoid(rows[1:2] + rin[at, :])
        k = kp[at, :] * (1.0 + (rate - 1.0) * rows[3:4])
        unit, scale, extra, summed = normed(out_ref[at, :], q_here, k, v_here, rows, c)
        grad = sum(x[at, :].astype(f32) for x in d_gated)
        if i == per - 1:
            grad = grad + jnp.where(last_row, fix, 0.0)
        d_gate[at, :] = (grad * summed).astype(bf16)
        d_sum = grad * g_here
        d_unit = d_sum * rows[5:6]
        d_here = scale * (
            d_unit
            - head_sum(d_unit, ones) * (1.0 / SPAN)
            - unit * head_sum(d_unit * unit, ones) * (1.0 / SPAN)
        )
        d_extra = head_sum(d_sum * v_here, ones)
        d_out[at, :] = d_here
        dq_post[at, :] = d_extra * k * rows[4:5]
        dk_post[at, :] = d_extra * q_here * rows[4:5]
        dv_post[at, :] = d_sum * extra
        row_grads[4:5, :] += column(d_extra * q_here * k)
        row_grads[5:6, :] += column(d_sum * unit)
        row_grads[6:7, :] += column(d_sum)
        maps[at, :] = state_map
        adds[at, :] = state_add
        carry_here = carry[i * width : (i + 1) * width, :]
        both = dot(
            jnp.concatenate([state_map, state_add], axis=0).astype(bf16), carry_here, 1, 1
        )
        state_map = both[:SPAN]
        state_add = both[SPAN:] + fold(cross(d_here, read[at, :]), c["mask"])
    map_now[...] = state_map
    add_now[...] = state_add
    map_end[...] = state_map
    add_end[...] = state_add


def grads_kernel(per, q, kp, v, din, rin, lat_ref, d_gate_ref, rows_ref, up_ref, push_ref, inv_ref, uk_ref, qk_ref, qr_ref,
                 starts, ends, d_out, dq_post, dk_post, dv_post, maps, adds, grad_in, dq_ref,
                 dkp_ref, dv_ref, pre_ref, row_grads, up_grads):
    c = constants(q.shape[1])
    up = up_ref[...]
    rows = rows_ref[...]
    mask, ones = c["mask"], c["ones"]
    cat = lambda *parts: jnp.concatenate(parts, axis=0)
    column = lambda x: jnp.sum(x, axis=0, keepdims=True)

    @pl.when(pl.program_id(0) == 0)
    def _():
        row_grads[...] = jnp.zeros_like(row_grads)
        up_grads[...] = jnp.zeros_like(up_grads)

    zero = jnp.zeros((SPAN, mask.shape[0]), f32)
    rank, gate_at = low_parts(up.shape[0])
    lane = lax.broadcasted_iota(jnp.int32, (SPAN, up.shape[0]), 1)
    low_row = lax.broadcasted_iota(jnp.int32, up_grads.shape, 0)
    for i in range(per):
        at = slice(i * SPAN, (i + 1) * SPAN)
        q_here, kp_here, v_here = q[at, :], kp[at, :], v[at, :]
        e = ready(q_here, kp_here, din[at, :], rin[at, :], rows, c)
        start, end, pushed, d_read = starts[at, :], ends[at, :], push_ref[at, :], d_out[at, :]
        grad_end = adds[at, :] + times(grad_in[...], maps[at, :], mask, 0)
        grown = grad_end * e["last"]
        by_state = times(cat(e["K"], e["R"]), grown, mask, 1)
        d_push = -fold(cross(qr_ref[at, :], d_read), mask) - by_state[SPAN:]
        d_rhs = fold(cross(inv_ref[at, :], d_push), mask)
        d_value = (
            by_state[:SPAN]
            + fold(cross(cat(qk_ref[at, :], uk_ref[at, :]), cat(d_read, d_rhs)), mask)
        )
        both = cat(d_rhs, d_read)
        by_value = times(both, v_here, mask, 1)
        by_push = times(both, pushed, mask, 1)
        d_key_pairs = cat(
            jnp.where(c["strict"], by_value[:SPAN], zero), jnp.where(c["incl"], by_value[SPAN:], zero)
        )
        d_removal_pairs = cat(
            jnp.where(c["strict"], -by_push[:SPAN], zero), jnp.where(c["incl"], -by_push[SPAN:], zero)
        )
        d_queries = (
            times(both, start, mask, 0)
            + times(d_key_pairs, e["K"], mask, 0)
            + times(d_removal_pairs, e["R"], mask, 0)
        )
        by_grown = times(cat(v_here, -pushed), grown, mask, 0)
        queries = cat(e["U"], e["Q"])
        d_k_grown = by_grown[:SPAN] + fold(cross(d_key_pairs, queries), mask)
        d_r_grown = by_grown[SPAN:] + fold(cross(d_removal_pairs, queries), mask)
        d_u_grown, d_q_grown = d_queries[:SPAN], d_queries[SPAN:]
        on_unit = d_u_grown * e["U"]
        steps = d_q_grown * e["Q"] - d_k_grown * e["K"] - d_r_grown * e["R"] + on_unit
        d_log = exact_left(c["upper"], steps) - on_unit + column(grad_end * end)
        rate = e["rate"]
        d_k = d_k_grown * e["down"] + dk_post[at, :]
        d_removal = d_r_grown * e["down"]
        d_unit = d_u_grown * e["before"] + d_removal * rate
        d_rate_value = d_removal * e["unit"] + d_k * kp_here * rows[3:4]
        d_scaled = e["inv"] * (d_unit - e["unit"] * head_sum(d_unit * e["unit"], ones))
        d_rate = d_rate_value * rate * (1.0 - rate)
        d_decay = d_log * e["log_decay"] * (1.0 - e["sig"])
        dq_ref[at, :] = (d_q_grown * e["up"] + dq_post[at, :]).astype(bf16)
        dkp_ref[at, :] = (d_k * (1.0 + (rate - 1.0) * rows[3:4]) + d_scaled * rows[2:3]).astype(bf16)
        dv_ref[at, :] = (d_value + dv_post[at, :]).astype(bf16)
        lat = lat_ref[at, :]
        low = lat.astype(bf16)
        d_outs = (d_decay.astype(bf16), d_rate.astype(bf16), d_gate_ref[at, :])
        pick = lambda where, parts: jnp.where(
            where < rank, parts[0], jnp.where(where < gate_at, parts[1], parts[2])
        )
        slope = pick(lane, (1.0 - lat * lat, jnp.ones_like(lat), lat * (1.0 - lat)))
        pre = pick(lane, [dot(x, up, 1, 1) for x in d_outs]) * slope
        pre_ref[at, :] = pre.astype(bf16)
        up_grads[...] += pick(low_row, [dot(low, x, 0, 0) for x in d_outs])
        row_grads[0:1, :] += column(d_decay)
        row_grads[1:2, :] += column(d_rate)
        row_grads[2:3, :] += column(d_scaled * kp_here)
        row_grads[3:4, :] += column(d_k * kp_here * (rate - 1.0))


def run_blocks(kernel, ins, outs, scratch, tokens, reverse=False):
    count = tokens // SPAN
    per = blocks_per_step(count)
    steps = count // per

    def spec(shape, cut):
        if not cut:
            return pl.BlockSpec(shape, lambda i: (0, 0))
        rows = shape[0] // steps
        if reverse:
            return pl.BlockSpec((rows, shape[1]), lambda i: (steps - 1 - i, 0))
        return pl.BlockSpec((rows, shape[1]), lambda i: (i, 0))

    return pl.pallas_call(
        functools.partial(kernel, per),
        grid=(steps,),
        in_specs=[spec(x.shape, cut) for x, cut in ins],
        out_specs=[spec(shape, cut) for shape, _, cut in outs],
        out_shape=[jax.ShapeDtypeStruct(shape, kind) for shape, kind, _ in outs],
        scratch_shapes=[pltpu.VMEM(shape, f32) for shape in scratch],
        compiler_params=pltpu.CompilerParams(dimension_semantics=("arbitrary",)),
        cost_estimate=pl.CostEstimate(flops=10**10, bytes_accessed=2 * 10**7, transcendentals=0),
    )(*[x for x, _ in ins])


def low_parts(width):
    return width // 4, width // 2


def mixed(unit, edge, norms, count):
    first = unit * norms[0:1] + norms[1:2]
    before = (edge[0:1] * norms[0:1] + norms[1:2]) * edge[1:2]
    row = lax.broadcasted_iota(jnp.int32, first.shape, 0)
    diff = jnp.where(row == 0, before, pltpu.roll(first, 1, 0)) - first
    return diff, [(first + diff * norms[4 + i : 5 + i]).astype(bf16) for i in range(count)]


def slab_weights(gathered, width, block):
    parts, rows, _ = gathered.shape
    part = rows // 4
    piece = lambda i, w: jnp.concatenate(
        [gathered[block(j), i * part : (i + 1) * part, :w] for j in range(parts)], axis=0
    )
    return [piece(i, width) for i in range(3)] + [piece(3, gathered.shape[2])]


def project_kernel(quick, ids, unit, edge, norms, gathered, up, q, kp, v, din, rin, gate, lat, low_total):
    width = q.shape[1]
    step = pl.program_id(0)
    norms_here = norms[...]
    _, mixes = mixed(unit[...], edge[...], norms_here, 6)
    block = lambda j: (j + ids[3]) % 2 if quick else j
    w_q, w_k, w_v, w_low = slab_weights(gathered, width, block)
    low_width = w_low.shape[1]
    rank, gate_at = low_parts(low_width)
    lane = lax.broadcasted_iota(jnp.int32, low_total.shape, 1)
    low = jnp.where(
        lane < rank,
        dot(mixes[1], w_low, 1, 0),
        jnp.where(lane < gate_at, dot(mixes[4], w_low, 1, 0), dot(mixes[5], w_low, 1, 0)),
    )

    @pl.when(step == 0)
    def _():
        q[...] = dot(mixes[0], w_q, 1, 0)
        kp[...] = dot(mixes[2], w_k, 1, 0)
        v[...] = dot(mixes[3], w_v, 1, 0)
        low_total[...] = low

    @pl.when(step > 0)
    def _():
        q[...] += dot(mixes[0], w_q, 1, 0)
        kp[...] += dot(mixes[2], w_k, 1, 0)
        v[...] += dot(mixes[3], w_v, 1, 0)
        low_total[...] += low

    @pl.when(step == pl.num_programs(0) - 1)
    def _():
        total = low_total[...]
        lats = jnp.where(
            lane < rank, jnp.tanh(total), jnp.where(lane < gate_at, total, jax.nn.sigmoid(total))
        )
        lat[...] = lats
        zero = jnp.zeros_like(lats)
        chosen = lambda where: jnp.where(where, lats, zero).astype(bf16)
        din[...] = dot(chosen(lane < rank), up[...], 1, 0)
        rin[...] = dot(chosen((lane >= rank) & (lane < gate_at)), up[...], 1, 0)
        gate[...] = dot(chosen(lane >= gate_at), up[...], 1, 0)


def unproject_kernel(quick, ids, unit, edge, scales, norms, gathered, dq, dkp, dv, pre, d_mid,
                     up_grads, second, rows_pre, rows_post, packed, feature, edge_fix, *rest):
    pieces, (all_first, all_unit) = rest[:-2], rest[-2:]
    block = lambda j: (j + ids[3]) % 2 if quick else j
    width = dq.shape[1]
    step = pl.program_id(0)
    n = norms[...]
    edge_here = edge[...]
    unit_here = unit[...]
    diff, mixes = mixed(unit_here, edge_here, n, 6)
    weights = slab_weights(gathered, width, block)
    w_low = weights[3]
    slab, low_width = w_low.shape
    rank, gate_at = low_parts(low_width)
    pre_here = pre[...]
    lane = lax.broadcasted_iota(jnp.int32, pre_here.shape, 1)
    none = jnp.zeros_like(pre_here)
    pres = [
        jnp.where(lane < rank, pre_here, none),
        jnp.where((lane >= rank) & (lane < gate_at), pre_here, none),
        jnp.where(lane >= gate_at, pre_here, none),
    ]
    sources = [(0, dq[...], 0), (2, dkp[...], 1), (3, dv[...], 2), (1, pres[0], 3), (4, pres[1], 3),
               (5, pres[2], 3)]
    low_lane = lax.broadcasted_iota(jnp.int32, (slab, low_width), 1)
    column = lambda x: jnp.sum(x, axis=0, keepdims=True)
    parts = gathered.shape[0]
    part = slab // parts
    direct = shifted = None
    low_grad = None
    for mix, grad, which in sources:
        weight_grad = dot(mixes[mix], grad, 0, 0)
        if which < 3:
            for j in range(parts):
                packed[block(j), which * part : (which + 1) * part, :width] = weight_grad[
                    j * part : (j + 1) * part
                ].astype(bf16)
                if width < low_width:
                    packed[block(j), which * part : (which + 1) * part, width:] = jnp.zeros(
                        (part, low_width - width), bf16
                    )
        else:
            low_grad = weight_grad if low_grad is None else low_grad + weight_grad
        d_mix = dot(grad, weights[which], 1, 1)
        feature[4 + mix : 5 + mix, :] = column(d_mix * diff)
        to_shift = d_mix * n[4 + mix : 5 + mix]
        shifted = to_shift if shifted is None else shifted + to_shift
        direct = d_mix - to_shift if direct is None else direct + (d_mix - to_shift)
    for j in range(parts):
        packed[block(j), 3 * part : 4 * part, :] = low_grad[j * part : (j + 1) * part].astype(bf16)
    tokens = unit_here.shape[0]
    row = lax.broadcasted_iota(jnp.int32, shifted.shape, 0)
    d_first = direct + jnp.where(row == tokens - 1, 0.0, pltpu.roll(shifted, tokens - 1, 0))
    before = shifted[0:1] * edge_here[1:2]
    feature[0:1, :] = column(d_first * unit_here) + before * edge_here[0:1]
    feature[1:2, :] = column(d_first) + before
    feature[2:4, :] = second[0:2, :]
    feature[10:11, :] = second[2:3, :]
    feature[11:, :] = jnp.zeros_like(feature[11:, :])
    if quick:
        up_rows, gate_rows = rank // (8), (low_width - gate_at) // 8
        head_part = width // SPAN * (SPAN // 8)
        row_grads = jnp.concatenate([rows_pre[0:4, :], rows_post[4:8, :]], axis=0)
        source = lax.broadcasted_iota(jnp.int32, (width, width), 0)
        target = lax.broadcasted_iota(jnp.int32, (width, width), 1)
        each = SPAN // 8
        for j in range(parts):
            dest = step * parts + j
            take = lambda at, size: up_grads[pl.ds(pl.multiple_of(at + dest * size, size), size), :]
            ups = jnp.concatenate([take(0, up_rows), take(rank, up_rows)], axis=0)
            chosen = (target // each * SPAN + dest * each + target % each == source) & (
                target < head_part
            )
            heads_here = dot(row_grads.astype(bf16), jnp.where(chosen, 1.0, 0.0).astype(bf16), 1, 0)
            values = feature[:, j * part : (j + 1) * part]
            at = 4 * part
            to = block(j)
            packed[to, at : at + EDGE, :] = ups.astype(bf16)
            packed[to, at + EDGE : at + 2 * EDGE, :] = take(gate_at, gate_rows).astype(bf16)
            packed[to, at + 2 * EDGE : at + 3 * EDGE, :] = jnp.concatenate(
                [values, jnp.zeros_like(values)], axis=1
            ).astype(bf16)
            packed[to, at + 3 * EDGE : at + 4 * EDGE, :] = jnp.concatenate(
                [heads_here, jnp.zeros_like(heads_here)], axis=0
            ).astype(bf16)
    at = pl.ds(pl.multiple_of(step * slab, slab), slab)
    all_first[:tokens, at] = d_first * n[0:1]
    all_first[tokens:, at] = jnp.broadcast_to(before * n[0:1], (8, slab))
    all_unit[:tokens, at] = unit_here
    all_unit[tokens:, at] = jnp.broadcast_to(edge_here[0:1], (8, slab))

    @pl.when(step == pl.num_programs(0) - 1)
    def _():
        d_unit = all_first[...]
        units = all_unit[...]
        features = d_unit.shape[1]
        mean = jnp.sum(d_unit, axis=1, keepdims=True) * (1.0 / features)
        along = jnp.sum(d_unit * units, axis=1, keepdims=True) * (1.0 / features)
        result = scales[...] * (d_unit - mean - units * along)
        edge_fix[...] = result[tokens:] + d_mid[tokens + EDGE - 8 :, :]
        all_first[:tokens, :] = result[:tokens] + d_mid[:tokens, :]
        send_pieces(pieces, all_first, ids[0])


EDGE = 16


def share_of(here, by, devices, size):
    return pl.ds(pl.multiple_of(lax.rem(here + by + devices, devices) * size, size), size)


def send_pieces(pieces, whole, here):
    share = pieces[0].shape[0]
    for by, piece in enumerate(pieces):
        piece[...] = whole[share_of(here, by, len(pieces), share), :].astype(piece.dtype)


def channel_kernel(devices, here, *refs):
    stream, edge_stream, has_edge, cot, norms, out_full, key, value = refs[:8]
    gated, edges = refs[8 : 8 + devices], refs[8 + devices : 8 + 2 * devices]
    refs = refs[8 + 2 * devices :]
    ffn_in, hidden, d_pre, cot_low, d_mid_low, d_mid, feature, middle_share = refs[:8]
    ffn_pieces, refs = refs[8 : 8 + devices], refs[8 + devices :]
    grad_pieces, refs = refs[:devices], refs[devices:]
    fix_pieces, refs = refs[:devices], refs[devices:]
    middle, unit, scale, diff, d_ffn, ffn_out = refs
    step = pl.program_id(0)
    tokens, features = stream.shape
    width = gated[0].shape[1]
    n = norms[...]
    flag = has_edge[0:1, 0:1]
    row = lax.broadcasted_iota(jnp.int32, (tokens + EDGE, features), 0)

    @pl.when(step == 0)
    def _():
        middle[:tokens, :] = stream[...]
        middle[tokens:, :] = edge_stream[...]
        for by in range(devices):
            rows = out_full[share_of(here[0], -by, devices, width), :]
            middle[:tokens, :] += dot(gated[by][...], rows, 1, 0)
            middle[tokens:, :] += dot(edges[by][...], rows, 1, 0)
        middle_share[...] = middle[share_of(here[0], 0, devices, tokens // devices), :]
        values = middle[...]
        center = values - jnp.sum(values, axis=1, keepdims=True) * (1.0 / features)
        spread_here = jnp.sum(center * center, axis=1, keepdims=True) * (1.0 / features)
        scale_here = lax.rsqrt(spread_here + 1e-05)
        unit_here = center * scale_here
        unit[...] = unit_here
        scale[...] = scale_here
        norm = unit_here * n[2:3] + n[3:4]
        before = pltpu.roll(norm, 1, 0)
        diff_here = jnp.where(row == 0, before * flag, before) - norm
        diff[...] = diff_here
        ffn_in[...] = (norm + diff_here * n[10:11])[:tokens].astype(bf16)
        cot_low[...] = cot[...].astype(bf16)
        d_ffn[...] = jnp.zeros_like(d_ffn)
        ffn_out[...] = jnp.zeros_like(ffn_out)

    act = jnp.maximum(dot(ffn_in[...], key[...], 1, 0), 0.0)
    hidden_here = (act * act).astype(bf16)
    hidden[...] = hidden_here
    d_pre_here = (dot(cot_low[...], value[...], 1, 1) * 2.0 * act).astype(bf16)
    d_pre[...] = d_pre_here
    d_ffn[:tokens, :] += dot(d_pre_here, key[...], 1, 1)
    ffn_out[...] += dot(hidden_here, value[...], 1, 0)

    @pl.when(step == pl.num_programs(0) - 1)
    def _():
        send_pieces(ffn_pieces, ffn_out, here[0])
        grad = d_ffn[...]
        to_shift = grad * n[10:11]
        moved = pltpu.roll(to_shift, tokens + EDGE - 1, 0)
        d_second = grad - to_shift + jnp.where(row == tokens + EDGE - 1, moved * flag, moved)
        unit_here = unit[...]
        column = lambda x: jnp.sum(x, axis=0, keepdims=True)
        feature[...] = jnp.zeros_like(feature)
        feature[0:1, :] = column(d_second * unit_here)
        feature[1:2, :] = column(d_second)
        feature[2:3, :] = column(grad * diff[...])
        d_unit = d_second * n[2:3]
        mean = jnp.sum(d_unit, axis=1, keepdims=True) * (1.0 / features)
        along = jnp.sum(d_unit * unit_here, axis=1, keepdims=True) * (1.0 / features)
        d_mid_here = scale[...] * (d_unit - mean - unit_here * along)
        d_mid[...] = d_mid_here
        d_mid_low[tokens:, :] = d_mid_here[tokens:].astype(bf16)
        d_mid_low[:tokens, :] = (d_mid_here[:tokens] + cot[...] * (1.0 / devices)).astype(bf16)
        for by in range(devices):
            rows = out_full[share_of(here[0], by, devices, width), :]
            grad_pieces[by][...] = dot(d_mid_low[:tokens, :], rows, 1, 1).astype(bf16)
            fix_pieces[by][...] = dot(d_mid_low[tokens:, :], rows, 1, 1).astype(bf16)


def large_kernel(devices, here, *refs):
    hidden, cot_low, ffn_in, d_pre, d_mid_low = refs[:5]
    gated, edges, large = refs[5 : 5 + devices], refs[5 + devices : 5 + 2 * devices], refs[-1]
    tokens, hidden_here = hidden.shape
    part = large.shape[2]
    width = gated[0].shape[1]
    large[0, :hidden_here, :] = dot(hidden[...], cot_low[...], 0, 0).astype(bf16)
    key_grad = dot(ffn_in[...], d_pre[...], 0, 0).astype(bf16)
    for j in range(hidden_here // part):
        at = hidden_here + j * part
        large[0, at : at + part, :] = key_grad[:, j * part : (j + 1) * part]
    grad, grad_edge = d_mid_low[:tokens, :], d_mid_low[tokens:, :]
    for by in range(devices):
        rows = dot(gated[by][...], grad, 0, 0) + dot(edges[by][...], grad_edge, 0, 0)
        at = lax.rem(here[0] - by + devices, devices) * width + 2 * hidden_here
        large[0, pl.ds(pl.multiple_of(at, width), width), :] = rows.astype(bf16)


def run_slabs(kernel, ids, ins, outs, scratch, slabs):
    def spec(shape, cut):
        shape = tuple(shape)
        if cut is None:
            return pl.BlockSpec(shape, lambda i, ids: (0,) * len(shape))
        if callable(cut[1]):
            return pl.BlockSpec(*cut)
        dim, size = cut
        block = list(shape)
        block[dim] = shape[dim] // slabs
        if size is not None:
            block[size[0]] = size[1]
        return pl.BlockSpec(
            tuple(block), lambda i, ids: tuple(i if k == dim else 0 for k in range(len(shape)))
        )

    return pl.pallas_call(
        kernel,
        grid_spec=pltpu.PrefetchScalarGridSpec(
            num_scalar_prefetch=1,
            grid=(slabs,),
            in_specs=[spec(x.shape, cut) for x, cut in ins],
            out_specs=[spec(shape, cut) for shape, _, cut in outs],
            scratch_shapes=[pltpu.VMEM(shape, f32) for shape in scratch],
        ),
        out_shape=[jax.ShapeDtypeStruct(shape, kind) for shape, kind, _ in outs],
        compiler_params=pltpu.CompilerParams(dimension_semantics=("arbitrary",)),
        cost_estimate=pl.CostEstimate(flops=10**10, bytes_accessed=2 * 10**7, transcendentals=0),
    )(ids, *[x for x, _ in ins])


def core_sum_kernel(ids, kept, came, send_x, send_y, keep_x, keep_y):
    half = send_x.shape[1]
    total = lambda i, rows: kept[i, rows, :].astype(f32) + came[i, rows, :].astype(f32)
    for y in range(2):
        keep_x[y] = total(y, slice(0, half))
        send_x[y] = total(2 + y, slice(0, half)).astype(bf16)
    for x in range(2):
        keep_y[x] = total(2 * x, slice(half, 2 * half))
        send_y[x] = total(2 * x + 1, slice(half, 2 * half)).astype(bf16)


def side_sum_kernel(ids, keep_x, keep_y, came_x, came_y, left_x, left_y, send_y, send_x):
    left_x[...] = keep_x[0] + came_x[0].astype(f32)
    left_y[...] = keep_y[0] + came_y[0].astype(f32)
    send_y[...] = (keep_x[1] + came_x[1].astype(f32)).astype(bf16)
    send_x[...] = (keep_y[1] + came_y[1].astype(f32)).astype(bf16)


def last_sum_kernel(ids, left_x, left_y, came_y, came_x, fix, rkv, up, gate_up, head, shared, whole):
    half = left_x.shape[0]
    whole[:half, :] = left_x[...] + came_y[...].astype(f32)
    whole[half:, :] = left_y[...] + came_x[...].astype(f32)
    first = rkv.shape[0]
    low = shared.shape[0] - 2 * EDGE
    rkv[...] = whole[:first, :]
    shared[:low, :] = whole[first : first + low, :].astype(bf16)
    at = first + low
    up[...] = whole[at : at + EDGE, :]
    gate_up[...] = whole[at + EDGE : at + 2 * EDGE, :]
    shared[low : low + EDGE, :] = whole[at + 2 * EDGE : at + 3 * EDGE, :].astype(bf16)
    head[...] = whole[at + 3 * EDGE :, :]
    shared[low + EDGE :, :] = fix[...]


def share_sum_kernel(devices, part, ids, *refs):
    pieces, stream, refs = refs[:devices], refs[devices], refs[devices + 1 :]
    down, gate_down, feature, input_grad, ordered = refs
    for by in range(devices):
        ordered[lax.rem(ids[0] - by + devices, devices)] = pieces[by][...].astype(f32)
    total = ordered[0]
    for i in range(1, devices):
        total = total + ordered[i]
    rank, gate_at = low_parts(total.shape[1])
    turned = total[:part, :gate_at].T
    down[0] = turned[:rank]
    down[1] = turned[rank:]
    gate_down[...] = total[:part, gate_at:]
    feature[...] = total[part : part + EDGE, :part]
    share, features = stream.shape
    lanes = total.shape[1]
    input_grad[...] = stream[...]
    ends = (ids[0] == devices - 1).astype(f32)
    for k in range(features // lanes):
        at = part + EDGE + k
        input_grad[share - 1 :, k * lanes : (k + 1) * lanes] += total[at : at + 1] * ends


def to_next(x, axis, by):
    devices = lax.axis_size(axis)
    pairs_here = [(i, i + by) for i in range(devices) if 0 <= i + by < devices]
    return lax.ppermute(x, axis, pairs_here)


def around(x, by):
    devices = lax.axis_size("mp")
    return lax.ppermute(x, "mp", [(i, (i + by) % devices) for i in range(devices)])


def slanted(x, along, by):
    rows, devices = lax.axis_size("seq"), lax.axis_size("mp")
    pairs_here = [
        (s * devices + i, (s + along) * devices + (i + by) % devices)
        for s in range(rows)
        if 0 <= s + along < rows
        for i in range(devices)
    ]
    return lax.ppermute(x, ("seq", "mp"), pairs_here)


def gather_shares(x):
    devices = lax.axis_size("mp")
    came = [x] + [around(x, by) for by in range(1, devices)]
    turned = jnp.stack([came[-k % devices] for k in range(devices)] * 2)
    at = (devices - lax.axis_index("mp")) % devices
    return lax.dynamic_slice_in_dim(turned, at, devices, 0)


def scatter_shares(x):
    devices = lax.axis_size("mp")
    here = lax.axis_index("mp")
    term = lambda at: lax.dynamic_index_in_dim(x, at % devices, 0, keepdims=False)
    total = term(here).astype(f32)
    for by in range(1, devices):
        total = total + around(term(here + by), by).astype(f32)
    return total


def mm_left(a, b):
    return dot(a, b, 0, 0)


def statistics(values):
    center = values - jnp.mean(values, axis=-1, keepdims=True)
    scale = lax.rsqrt(jnp.mean(center * center, axis=-1, keepdims=True) + 1e-05)
    return center * scale, scale


def carry_states(state_map, state_add, by):
    entering = to_next(state_add.astype(bf16), "seq", by).astype(f32)
    heads = state_map.shape[1] // SPAN
    apart = lambda x: x.reshape(SPAN, heads, SPAN).transpose(1, 0, 2)
    for _ in range(lax.axis_size("seq") - 2):
        moved = jnp.einsum("hij,hjl->hil", apart(entering), apart(state_map), precision="highest")
        passed = moved.transpose(1, 0, 2).reshape(state_add.shape) + state_add
        entering = to_next(passed.astype(bf16), "seq", by).astype(f32)
    return entering


def wide(x, width):
    return jnp.pad(x, ((0, 0), (0, width - x.shape[1])))


def body(inputs, rkv_weight, output_weight, first_factors, second_factors, gate_first, gate_second,
         key_weight, value_weight, head_table, feature_table, cotangent):
    group = ("dp", "seq")
    count = lax.axis_size("dp") * lax.axis_size("seq")
    mp = lax.axis_size("mp")
    mp_here = lax.axis_index("mp")
    stream = inputs[0]
    cot = cotangent[0]
    tokens, features = stream.shape
    share = tokens // mp
    share_at = mp_here * share
    part = features // count
    width = rkv_weight.shape[2]
    heads = width // SPAN
    rank, gate_rank = first_factors.shape[2], gate_first.shape[1]
    low_width = 2 * rank + gate_rank
    lanes = max(width, low_width, part)
    up_rows = second_factors.shape[1]
    head_part = head_table.shape[2]
    dp_here, seq_here = lax.axis_index("dp"), lax.axis_index("seq")
    quick = lax.axis_size("dp") == 4 and lax.axis_size("seq") == 2 and part == 128 and width == 256
    ids = jnp.stack([mp_here, dp_here // 2, dp_here % 2, seq_here]).astype(jnp.int32)
    edge_stream = to_next(stream[-EDGE:], "seq", 1)
    edge_row = edge_stream[EDGE - 1 :]
    pieces = [
        wide(rkv_weight.reshape(3 * part, width), lanes),
        wide(jnp.concatenate([first_factors[0], first_factors[1], gate_first], axis=1), lanes),
        wide(second_factors.reshape(2 * up_rows, width), lanes),
        wide(gate_second, lanes),
        jnp.pad(wide(feature_table, lanes), ((0, 5), (0, 0))),
        jnp.pad(wide(head_table.reshape(7, heads * head_part), lanes), ((0, 9), (0, 0))),
    ]
    edges = [0]
    for piece in pieces:
        edges.append(edges[-1] + piece.shape[0])
    packed = jnp.concatenate(pieces, axis=0)
    rows_full = -(-packed.shape[0] // 16) * 16
    packed = jnp.pad(packed, ((0, rows_full - packed.shape[0]), (0, 0)))
    unit_one, scale_one = statistics(stream)
    edge_unit, edge_scale = statistics(edge_row)
    has_edge = (lax.axis_index("seq") > 0).astype(f32)
    edge = jnp.concatenate(
        [edge_unit, jnp.broadcast_to(has_edge, (1, features)), jnp.zeros((6, features), f32)]
    )
    swap = lambda x, bit: lax.ppermute(x, "dp", [(i, i ^ bit) for i in range(4)])
    turn = lambda x: lax.ppermute(x, "seq", [(0, 1), (1, 0)])
    whose = lambda i, ids: (((i + ids[2]) % 2) * 2 + (i // 2 + ids[1]) % 2, 0, 0)
    if quick:
        half = rows_full // 2
        beside, across = swap(packed, 2), turn(packed)
        beside, output_weight = lax.optimization_barrier((beside, output_weight))
    out_column = gather_shares(output_weight).reshape(features, part)
    rest_here = jnp.concatenate([value_weight, out_column], axis=0)
    if quick:
        corner = jnp.concatenate([turn(beside[:half]), swap(across[half:], 2)], axis=0)
        near = jnp.stack([packed, across, beside, corner])
        near, unit_one, scale_one, edge = lax.optimization_barrier(
            (near, unit_one, scale_one, edge)
        )
        gathered = jnp.concatenate([near, swap(near, 1)], axis=0)
        gathered, rest_here, key_weight = lax.optimization_barrier(
            (gathered, rest_here, key_weight)
        )
        small_at = edges[2]
        small = gathered[:, small_at:].reshape(2, 2, 2, rows_full - small_at, lanes)
        for axis, bit in enumerate((ids[2], ids[1], ids[3])):
            small = jnp.where(bit == 1, jnp.flip(small, axis), small)
        small = small.transpose(1, 0, 2, 3, 4).reshape(count, rows_full - small_at, lanes)
    else:
        gathered = lax.all_gather(packed, group, axis=0, tiled=False)
        small_at = edges[2]
        small = gathered[:, small_at:]
    cut = lambda i, w: small[:, edges[i] - small_at : edges[i + 1] - small_at, :w]
    up = cut(2, width).reshape(count, 2, up_rows, width).transpose(1, 0, 2, 3)
    up = jnp.concatenate(
        [up.reshape(2 * rank, width), cut(3, width).reshape(gate_rank, width)], axis=0
    )
    norms = cut(4, part).transpose(1, 0, 2).reshape(16, features).astype(f32)
    head_rows = (
        cut(5, heads * head_part)[:, :7]
        .reshape(count, 7, heads, head_part)
        .transpose(1, 2, 0, 3)
        .reshape(7, width)
        .astype(f32)
    )
    head_rows = jnp.pad(head_rows, ((0, 1), (0, 0)))

    rest = lax.all_gather(rest_here, group, axis=0, tiled=False)
    hidden_here = value_weight.shape[0]
    key_full = lax.all_gather(key_weight, group, axis=0, tiled=True)

    slab = max(256, part)
    slabs = features // slab
    in_slabs = (1, None)
    of_gathered = ((2, 4 * part, lanes), whose) if quick else (0, (1, 4 * part))
    whole = (tokens, width)
    q, kp, v, din, rin, gate, lat = run_slabs(
        functools.partial(project_kernel, quick),
        ids,
        [(unit_one, in_slabs), (edge, in_slabs), (norms, in_slabs), (gathered, of_gathered), (up, None)],
        [(whole, f32, None)] * 6 + [((tokens, low_width), f32, None)],
        [(tokens, low_width)],
        slabs,
    )

    state = (SPAN, width)
    (local_out, read, push_map, push, inv, uk, qk, qr, carry, maps, adds, map_end, add_end) = run_blocks(
        local_kernel,
        [(q, True), (kp, True), (v, True), (din, True), (rin, True), (head_rows, False)],
        [(whole, f32, True)] * 4
        + [(whole, bf16, True)] * 4
        + [((tokens // SPAN * width, width), bf16, True)]
        + [(whole, f32, True)] * 2
        + [(state, f32, False)] * 2,
        [state, state],
        tokens,
    )
    entering = carry_states(map_end, add_end, 1)
    gated, read_out, pushed, starts, ends = run_blocks(
        finish_kernel,
        [(x, True) for x in (q, kp, v, rin, gate)]
        + [(head_rows, False)]
        + [(x, True) for x in (local_out, read, push_map, push, maps, adds)]
        + [(entering, False)],
        [(whole, bf16, True)] + [(whole, f32, True)] * 4,
        [state],
        tokens,
    )

    edge_parts = [slanted(gated[-EDGE:], 1, by) for by in range(mp)]
    gated_parts = [gated] + [around(gated, by) for by in range(1, mp)]
    value_full = rest[:, :hidden_here].transpose(1, 0, 2).reshape(hidden_here, features)
    out_full = rest[:, hidden_here:].transpose(1, 0, 2).reshape(features, features)
    longer = tokens + EDGE
    lots = key_full.shape[1] // part
    channel = run_slabs(
        functools.partial(channel_kernel, mp),
        ids,
        [(stream, None), (edge_stream, None), (edge[1:2, :128], None), (cot, None)]
        + [(norms, None), (out_full, None), (key_full, (1, None)), (value_full, (0, None))]
        + [(x, None) for x in gated_parts + edge_parts],
        [
            ((tokens, features), bf16, None),
            ((tokens, hidden_here), bf16, (1, None)),
            ((tokens, hidden_here), bf16, (1, None)),
            ((tokens, features), bf16, None),
            ((longer, features), bf16, None),
            ((longer, features), f32, None),
            ((8, features), f32, None),
            ((share, features), f32, None),
        ]
        + [((share, features), bf16, None)] * mp
        + [(whole, bf16, None)] * mp
        + [((EDGE, width), bf16, None)] * mp,
        [(longer, features)] * 2
        + [(longer, 1)]
        + [(longer, features)] * 2
        + [(tokens, features)],
        max(1, hidden_here // 256),
    )
    ffn_in, hidden, d_pre, cot_low, d_mid_low, d_mid, second_rows, middle_share = channel[:8]
    ffn_pieces = channel[8 : 8 + mp]
    grad_pieces = channel[8 + mp : 8 + 2 * mp]
    fix_pieces = channel[8 + 2 * mp :]
    fixes = []
    for by in range(mp):
        fixes.append(slanted(fix_pieces[by], -1, by))
    d_gated = [grad_pieces[0]]
    for by in range(1, mp):
        d_gated.append(around(grad_pieces[by], by))

    if part % 128 == 0:
        large = run_slabs(
            functools.partial(large_kernel, mp),
            ids,
            [(hidden, None), (cot_low, (1, None)), (ffn_in, (1, None)), (d_pre, None)]
            + [(d_mid_low, (1, None))]
            + [(x, None) for x in gated_parts + edge_parts],
            [((count, 2 * hidden_here + features, part), bf16, (0, None))],
            [],
            count,
        )[0]
    else:
        by_part = lambda x: x.astype(bf16).reshape(x.shape[0], count, part).transpose(1, 0, 2)
        key_grad = mm_left(ffn_in, d_pre).astype(bf16)
        key_grad = key_grad.reshape(count, part, lots, part).transpose(0, 2, 1, 3)
        order = lambda parts: jnp.concatenate(parts[:1] + parts[:0:-1], axis=0)
        out_rows = order([mm_left(x, d_mid_low[:tokens]) for x in gated_parts]) + order(
            [mm_left(x, d_mid_low[tokens:]) for x in edge_parts]
        )
        large = jnp.concatenate(
            [
                by_part(mm_left(hidden, cot_low)),
                key_grad.reshape(count, lots * part, part),
                by_part(jnp.roll(out_rows, mp_here * width, axis=0)),
            ],
            axis=1,
        )
    large = lax.psum_scatter(large, group, scatter_dimension=0, tiled=False)
    d_gated, ffn_pieces = lax.optimization_barrier((d_gated, ffn_pieces))
    block_out = middle_share + ffn_pieces[0].astype(f32)
    for by in range(1, mp):
        came = around(ffn_pieces[by], by)
        block_out = block_out + came.astype(f32)

    (d_read, dq_post, dk_post, dv_post, d_gate, back_maps, back_adds, back_map_end, back_add_end,
     row_grads_post) = run_blocks(
        functools.partial(reads_kernel, mp),
        [(x, True) for x in (q, kp, v, rin, gate)]
        + [(head_rows, False)]
        + [(x, True) for x in (read_out, read, carry)]
        + [(x, True) for x in d_gated]
        + [(x, False) for x in fixes],
        [(whole, f32, True)] * 4
        + [(whole, bf16, True)]
        + [(whole, f32, True)] * 2
        + [(state, f32, False)] * 2
        + [((8, width), f32, False)],
        [state, state],
        tokens,
        reverse=True,
    )
    grad_in = carry_states(back_map_end, back_add_end, -1)
    dq, dkp, dv, pre, row_grads, up_grads = run_blocks(
        grads_kernel,
        [(x, True) for x in (q, kp, v, din, rin, lat, d_gate)]
        + [(head_rows, False), (up, False)]
        + [
            (x, True)
            for x in (pushed, inv, uk, qk, qr, starts, ends, d_read, dq_post, dk_post, dv_post,
                      back_maps, back_adds)
        ]
        + [(grad_in, False)],
        [(whole, bf16, True)] * 3
        + [((tokens, low_width), bf16, True), ((8, width), f32, False)]
        + [((low_width, width), f32, False)],
        [],
        tokens,
    )

    scales = jnp.concatenate([scale_one, jnp.broadcast_to(edge_scale, (8, 1))], axis=0)
    packed_rows = rows_full if quick else 4 * part
    unprojected = run_slabs(
        functools.partial(unproject_kernel, quick),
        ids,
        [(unit_one, in_slabs), (edge, in_slabs), (scales, None), (norms, in_slabs)]
        + [(gathered, of_gathered), (dq, None), (dkp, None), (dv, None), (pre, None), (d_mid, None)]
        + [(up_grads, None), (second_rows, in_slabs), (row_grads, None), (row_grads_post, None)],
        [
            (
                (count, packed_rows, lanes),
                bf16,
                ((2, packed_rows, lanes), whose) if quick else (0, None),
            ),
            ((16, features), f32, in_slabs),
            ((8, features), f32, None),
        ]
        + [((share, features), bf16, None)] * mp,
        [(tokens + 8, features)] * 2,
        slabs,
    )
    packed, feature_grad, edge_fix = unprojected[:3]
    stream_pieces = unprojected[3:]
    fix = to_next(edge_fix[7:].astype(bf16), "seq", -1)
    stream_came = [stream_pieces[0]]
    for by in range(1, mp):
        stream_came.append(around(stream_pieces[by], by))
    fix_rows = features // lanes
    fix = jnp.pad(fix.reshape(fix_rows, lanes), ((0, EDGE - fix_rows), (0, 0)))

    def settle(large):
        key_grad = large[hidden_here : hidden_here + lots * part].reshape(lots, part, part)
        return (
            large[:hidden_here].astype(f32),
            key_grad.transpose(1, 0, 2).reshape(part, lots * part).astype(f32),
            scatter_shares(large[hidden_here + lots * part :].reshape(mp, width, part)),
        )

    if quick:
        sides = (2, half, lanes)
        came = swap(packed[4:], 1)
        quarter = ((4, rows_full, lanes), lambda i, ids: (0, 0, 0))
        send_x, send_y, keep_x, keep_y = run_slabs(
            core_sum_kernel, ids, [(packed, quarter), (came, None)],
            [(sides, bf16, None)] * 2 + [(sides, f32, None)] * 2, [], 1,
        )
        keep_x, large = lax.optimization_barrier((keep_x, large))
        settled = settle(large)
        left_x, left_y, send_y, send_x = run_slabs(
            side_sum_kernel,
            ids,
            [(x, None) for x in (keep_x, keep_y, swap(send_x, 2), turn(send_y))],
            [(sides[1:], f32, None)] * 2 + [(sides[1:], bf16, None)] * 2,
            [],
            1,
        )
        left_x, settled = lax.optimization_barrier((left_x, settled))
        own_rkv, own_up, own_gate_up, own_head, shared = run_slabs(
            last_sum_kernel,
            ids,
            [(x, None) for x in (left_x, left_y, turn(send_y), swap(send_x, 2), fix)],
            [
                ((3 * part, lanes), f32, None),
                ((EDGE, lanes), f32, None),
                ((EDGE, lanes), f32, None),
                ((EDGE, lanes), f32, None),
                ((part + 2 * EDGE, lanes), bf16, None),
            ],
            [(rows_full, lanes)],
            1,
        )
    else:
        split_rows = lambda x: x.reshape(count, x.shape[0] // count, x.shape[1])
        wider = lambda x: jnp.pad(x.astype(bf16), ((0, 0), (0, 0), (0, lanes - x.shape[2])))
        head_grads = jnp.concatenate([row_grads[:4], row_grads_post[4:]], axis=0)
        grads = [
            split_rows(up_grads[:rank]),
            split_rows(up_grads[rank : 2 * rank]),
            split_rows(up_grads[2 * rank :]),
            feature_grad.reshape(16, count, part).transpose(1, 0, 2),
            head_grads.reshape(8, heads, count, head_part)
            .transpose(2, 0, 1, 3)
            .reshape(count, 8, heads * head_part),
        ]
        grads = jnp.concatenate([wider(x) for x in grads], axis=1)
        grads = jnp.pad(grads, ((0, 0), (0, rows_full - 4 * part - grads.shape[1]), (0, 0)))
        summed = lax.psum_scatter(
            jnp.concatenate([packed, grads], axis=1), group, scatter_dimension=0, tiled=False
        )
        own = lambda i, w: summed[edges[i] : edges[i + 1], :w].astype(f32)
        own_rkv, own_up, own_gate_up, own_head = own(0, width), own(2, width), own(3, width), own(5, lanes)
        shared = jnp.concatenate(
            [summed[edges[1] : edges[2]], summed[edges[4] : edges[5]], fix], axis=0
        )
        settled = settle(large)
    value_grad, key_grad, out_grad = settled
    input_grad = lax.dynamic_slice_in_dim(cot, share_at, share, 0) + sum(
        x.astype(f32) for x in stream_came
    )
    down_grad, gate_down_grad, feature_out, input_grad = run_slabs(
        functools.partial(share_sum_kernel, mp, part),
        ids,
        [(x, None) for x in [shared] + [around(shared, by) for by in range(1, mp)]]
        + [(input_grad, None)],
        [
            ((2, rank, part), f32, None),
            ((part, gate_rank), f32, None),
            ((EDGE, part), f32, None),
            ((share, features), f32, None),
        ],
        [(mp,) + shared.shape],
        1,
    )
    return (
        block_out[None],
        input_grad[None],
        own_rkv.reshape(3, part, width),
        out_grad,
        down_grad.transpose(0, 2, 1),
        own_up.reshape(2, up_rows, width),
        gate_down_grad,
        own_gate_up,
        key_grad,
        value_grad,
        own_head[:7, : heads * head_part].reshape(7, heads, head_part),
        feature_out[:11],
    )


def solution(mesh):
    both = ("dp", "seq")
    return jax.shard_map(
        body,
        mesh=mesh,
        in_specs=(
            P("dp", "seq", None),
            P(None, both, "mp"),
            P("mp", both),
            P(None, both, None),
            P(None, both, "mp"),
            P(both, None),
            P(both, "mp"),
            P(both, "mp"),
            P("mp", both),
            P(None, "mp", both),
            P(None, both),
            P("dp", "seq", None),
        ),
        out_specs=(
            P("dp", ("seq", "mp"), None),
            P("dp", ("seq", "mp"), None),
            P(None, both, "mp"),
            P("mp", both),
            P(None, both, None),
            P(None, both, "mp"),
            P(both, None),
            P(both, "mp"),
            P(both, "mp"),
            P("mp", both),
            P(None, "mp", both),
            P(None, both),
        ),
        check_vma=False,
    )
```
